32 devices in a mesh: ulysses: 4 (over x, core), blk: 8 (over z, y).
Axes of the slice: x: 2, y: 2, z: 4, core: 2. Of those that a mesh axis runs over, the one named last changes fastest.
Arguments:
- inputs: bfloat16 [2, 2048, 768], P(None, ('ulysses', 'blk')), may hold values from -6 to 6
- conditioning: bfloat16 [2, 128], replicated, may hold values from -4 to 4
- w_ada: bfloat16 [128, 4608], P(None, ('ulysses', 'blk')), may hold values from -0.5 to 0.5
- w_qkv: bfloat16 [768, 2304], P(('ulysses', 'blk')), may hold values from -0.21875 to 0.21875
- w_out: bfloat16 [768, 768], P(('ulysses', 'blk')), may hold values from -6 to 6
- w_up: bfloat16 [768, 3072], P(('ulysses', 'blk')), may hold values from -0.21875 to 0.21875
- w_down: bfloat16 [3072, 768], P(('ulysses', 'blk')), may hold values from -0.109375 to 0.109375
- gain_one: bfloat16 [768], P(('ulysses', 'blk')), may hold values from 0.099609375 to 1.8984375
- gain_two: bfloat16 [768], P(('ulysses', 'blk')), may hold values from 0.099609375 to 1.8984375
- cotangent: bfloat16 [2, 2048, 768], P(None, ('ulysses', 'blk')), may hold values from -6 to 6
Outputs:
- output: float32 [2, 2048, 768], P(None, ('ulysses', 'blk'))
- inputs_grad: float32 [2, 2048, 768], P(None, ('ulysses', 'blk'))
- conditioning_grad: float32 [2, 128], replicated
- w_ada_grad: float32 [128, 4608], P(None, ('ulysses', 'blk'))
- w_qkv_grad: float32 [768, 2304], P(('ulysses', 'blk'))
- w_out_grad: float32 [768, 768], P(('ulysses', 'blk'))
- w_up_grad: float32 [768, 3072], P(('ulysses', 'blk'))
- w_down_grad: float32 [3072, 768], P(('ulysses', 'blk'))
- gain_one_grad: float32 [768], P(('ulysses', 'blk'))
- gain_two_grad: float32 [768], P(('ulysses', 'blk'))
The draws below stay inside these ranges and needn't reach their ends.
All inputs are finite; a program needn't handle non-finite values.
Results may differ from the reference program's by a relative error of at most 0.0158.
The reference program's roundings to bfloat16 on the way count: a program that leaves them out, or rounds other values in their place, can miss the bound.
Values may be sent and summed in bfloat16 or wider, within the bound.
No kernel may reach another device: no remote copies, remote signals or barrier semaphores. Data moves between devices by JAX's collectives and lax.ppermute only.
A program may use at most 256 MiB of HBM per device.

```python
import jax
import jax.numpy as jnp
from jax import lax

D = 768
HEADS = 12
HEAD_DIM = 64
FF = 3072
COND = 128
SEQ_LEN = 2048
SEQS = 2


def block_levels(own_key, extent, pieces, smallest, high):
    def one(axis_at, parts):
        steps = jax.random.uniform(jax.random.fold_in(jax.random.fold_in(own_key, 6), axis_at), (parts,), jnp.float32, smallest / len(pieces), high / len(pieces))
        return jnp.repeat(jnp.exp(steps), extent[axis_at] // parts).reshape((-1,) + (1,) * (len(extent) - axis_at - 1))

    level = one(*pieces[0])
    for cut in pieces[1:]:
        level = level * one(*cut)
    return level


def bell_draw(stream_key, extent, deviation, most, pieces=(), held_as=jnp.bfloat16):
    level = block_levels(stream_key, extent, pieces, -0.22, 0.18) if pieces else 1.0
    array = jax.random.normal(stream_key, extent, jnp.float32) * deviation * level
    return jnp.minimum(jnp.maximum(array, -most), most).astype(held_as)


def setup_inputs(seed: int = 0) -> dict:
    seeds = jax.random.split(jax.random.key(seed), 11)
    inputs = bell_draw(seeds[0], (SEQS, SEQ_LEN, D), 1.0, 6.0, ((1, 32),))
    conditioning = bell_draw(seeds[1], (SEQS, COND), 0.5, 4.0)
    w_ada = bell_draw(seeds[2], (COND, 6 * D), COND ** -0.5, 0.5, ((1, 32),))
    w_qkv = bell_draw(seeds[3], (D, 3 * D), D ** -0.5, 0.21875, ((0, 32),))
    w_out = bell_draw(seeds[4], (D, D), (max(1, SEQ_LEN // 8192)), 6.0, ((0, 32),))
    w_up = bell_draw(seeds[5], (D, FF), D ** -0.5, 0.21875, ((0, 32),))
    w_down = bell_draw(seeds[6], (FF, D), FF ** -0.5, 0.109375, ((0, 32),))
    gain_one = jnp.clip(1.0 + 0.18 * jax.random.normal(seeds[7], (D,), jnp.float32), 0.099609375, 1.8984375).astype(jnp.bfloat16)
    gain_two = jnp.clip(1.0 + 0.18 * jax.random.normal(seeds[8], (D,), jnp.float32), 0.099609375, 1.8984375).astype(jnp.bfloat16)
    cotangent = bell_draw(seeds[9], (SEQS, SEQ_LEN, D), 1.0, 6.0, ((1, 32),))
    return dict(inputs=inputs, conditioning=conditioning, w_ada=w_ada, w_qkv=w_qkv, w_out=w_out, w_up=w_up, w_down=w_down, gain_one=gain_one, gain_two=gain_two, cotangent=cotangent)


@jax.custom_vjp
def low(v):
    return lax.optimization_barrier(v.astype(jnp.bfloat16)).astype(jnp.float32)

@jax.custom_vjp
def low_back(v):
    return v

def low_keep(v):
    return (low(v), None)

def low_pass(kept, grad):
    return (grad,)

def back_keep(v):
    return (v, None)

def back_low(kept, grad):
    return (low(grad),)
low.defvjp(low_keep, low_pass)
low_back.defvjp(back_keep, back_low)
highest = lax.Precision.HIGHEST
eps_norm = 1e-06

def matmul(left, right):
    return jnp.dot(left, right, precision=highest, preferred_element_type=jnp.float32)

def normalize(values):
    average = lax.optimization_barrier(jnp.mean(values, axis=-1, keepdims=True))
    centered = values - average
    variance = lax.optimization_barrier(jnp.mean(centered * centered, axis=-1, keepdims=True))
    return centered * lax.rsqrt(variance + eps_norm)

def rotary_tables(length):
    half_dim = HEAD_DIM // 2
    frequency = jnp.exp(-jnp.log(10000.0) * jnp.arange(half_dim, dtype=jnp.float32) * 2.0 / HEAD_DIM)
    angles = jnp.arange(length, dtype=jnp.float32)[:, None] * frequency[None, :]
    return (jnp.cos(angles)[:, None, :], jnp.sin(angles)[:, None, :])

def rotate(values, cos_table, sin_table):
    half_dim = values.shape[-1] // 2
    first_half = values[..., :half_dim]
    second_half = values[..., half_dim:]
    return jnp.concatenate([first_half * cos_table - second_half * sin_table, second_half * cos_table + first_half * sin_table], axis=-1)

def attention(queries, keys, values):
    length = queries.shape[0]
    rows_block = min(512, length)
    score_scale = HEAD_DIM ** (-0.5)
    blocks = queries.reshape(length // rows_block, rows_block, HEADS, HEAD_DIM)

    def one_block(query_block):
        scores = low_back(jnp.einsum('qhd,khd->hqk', query_block, keys, precision=highest) * score_scale)
        weights = low(jax.nn.softmax(scores, axis=-1))
        return jnp.einsum('hqk,khd->qhd', weights, values, precision=highest)
    result = lax.map(jax.checkpoint(one_block), blocks)
    return result.reshape(length, HEADS * HEAD_DIM)

def seq_forward(inputs, cond_row, w_ada, w_qkv, w_out, w_up, w_down, gain_one, gain_two):
    length = inputs.shape[0]
    modulation = low_back(matmul(cond_row[None, :], w_ada)[0])
    shift_one, scale_one, gate_one, shift_two, scale_two, gate_two = jnp.split(modulation, 6)
    first_in = low(normalize(inputs) * gain_one * (1.0 + scale_one) + shift_one)
    projected = low_back(matmul(first_in, w_qkv)).reshape(length, 3, HEADS, HEAD_DIM)
    cos_table, sin_table = rotary_tables(length)
    queries = low(low_back(rotate(projected[:, 0], cos_table, sin_table)))
    keys = low(low_back(rotate(projected[:, 1], cos_table, sin_table)))
    values = low(low_back(projected[:, 2]))
    attended = low(low_back(attention(queries, keys, values)))
    branch = low_back(matmul(attended, w_out))
    middle = inputs + gate_one * branch
    second_in = low(normalize(middle) * gain_two * (1.0 + scale_two) + shift_two)
    raised = low_back(matmul(second_in, w_up))
    hidden = low(jax.nn.gelu(raised, approximate=True))
    lowered = low_back(matmul(hidden, w_down))
    return middle + gate_two * lowered

def reference(inputs, conditioning, w_ada, w_qkv, w_out, w_up, w_down, gain_one, gain_two, cotangent):
    params = tuple((p.astype(jnp.float32) for p in (w_ada, w_qkv, w_out, w_up, w_down, gain_one, gain_two)))

    def per_sequence(summed, sequence):
        seq_inputs, seq_cond, seq_cot = sequence
        result, pullback = jax.vjp(seq_forward, seq_inputs.astype(jnp.float32), seq_cond.astype(jnp.float32), *params)
        gradients = pullback(seq_cot.astype(jnp.float32))
        summed = tuple((a + b for a, b in zip(summed, gradients[2:])))
        return (summed, (result, gradients[0], gradients[1]))
    zeros = tuple((jnp.zeros(p.shape, jnp.float32) for p in params))
    summed, (output, inputs_grad, cond_grad) = lax.scan(per_sequence, zeros, (inputs, conditioning, cotangent))
    return (output, inputs_grad, cond_grad, summed[0], summed[1], summed[2], summed[3], summed[4], summed[5], summed[6])
```

```python
import functools
import math

import jax
import jax.numpy as jnp
from jax import lax
from jax.experimental import pallas as pl
from jax.experimental.pallas import tpu as pltpu
from jax.sharding import PartitionSpec as P

f32, bf16 = jnp.float32, jnp.bfloat16
DOT = functools.partial(jnp.dot, preferred_element_type=f32)

def attn_fwd_kernel(x_ref, o_ref, of_ref, lse_ref, kt_ref, v_ref):
    nb, rows3, _ = x_ref.shape
    half = rows3 // 3
    rows = 2 * half
    for j in range(nb):
        kt_ref[:, j * rows : (j + 1) * rows] = x_ref[j, :rows, 64:].T
        v_ref[j * rows : j * rows + half, :] = x_ref[j, rows:, :64]
        v_ref[j * rows + half : (j + 1) * rows, :] = x_ref[j, rows:, 64:]

    def step(j, _):
        q = x_ref[j, :rows, :64] * jnp.asarray(0.125, bf16)
        s = DOT(q, kt_ref[...])
        top = jnp.max(s, axis=1, keepdims=True)
        p = jnp.exp(s - top)
        total = jnp.sum(p, axis=1, keepdims=True)
        o = DOT(p.astype(bf16), v_ref[...]) / total
        packed = jnp.concatenate([o[:half], o[half:]], axis=1)
        of_ref[j] = packed
        o_ref[j] = packed.astype(bf16)
        lse = jnp.broadcast_to(top + jnp.log(total), (rows, 128)).T
        lse_ref[j] = lse[:8]
        return 0
    lax.fori_loop(0, nb, step, 0, unroll=2)

def attn_fwd(x):
    nb, rows3, _ = x.shape
    half = rows3 // 3
    n = nb * half * 2
    return pl.pallas_call(
        attn_fwd_kernel,
        out_shape=(jax.ShapeDtypeStruct((nb, half, 128), bf16), jax.ShapeDtypeStruct((nb, half, 128), f32),
                   jax.ShapeDtypeStruct((nb, 8, 2 * half), f32)),
        scratch_shapes=[pltpu.VMEM((64, n), bf16), pltpu.VMEM((n, 64), bf16)],
        cost_estimate=pl.CostEstimate(flops=4 * n * n * 64, bytes_accessed=n * 64 * 2 * 8, transcendentals=n * n),
        compiler_params=pltpu.CompilerParams(vmem_limit_bytes=48 << 20),
        name="attn_fwd",
    )(x)

def attn_bwd_kernel(x_ref, d_ref, of_ref, lse_ref, g_ref, qt_ref, dt_ref, q_ref, dd_ref, lse_s, del_s, dqt_ref):
    nb, rows3, _ = x_ref.shape
    half = rows3 // 3
    rows = 2 * half
    for j in range(nb):
        sl = slice(j * rows, (j + 1) * rows)
        q = x_ref[j, :rows, :64] * jnp.asarray(0.125, bf16)
        q_ref[sl, :] = q
        qt_ref[:, sl] = q.T
        d = jnp.concatenate([d_ref[j, :, :64], d_ref[j, :, 64:]], axis=0)
        dd_ref[sl, :] = d
        dt_ref[:, sl] = d.T
        o = jnp.concatenate([of_ref[j, :, :64], of_ref[j, :, 64:]], axis=0)
        delta = jnp.sum(d.astype(f32) * o, axis=1, keepdims=True)
        del_s[:, sl] = jnp.broadcast_to(delta, (rows, 128)).T[:8]
        lse_s[:, sl] = lse_ref[j]
    dqt_ref[...] = jnp.zeros_like(dqt_ref)

    def step(j, _):
        k = x_ref[j, :rows, 64:]
        v = jnp.concatenate([x_ref[j, rows:, :64], x_ref[j, rows:, 64:]], axis=0)
        s = DOT(k, qt_ref[...])
        p = jnp.exp(s - lse_s[0:1, :])
        dp = DOT(v, dt_ref[...])
        ds = (p * (dp - del_s[0:1, :])).astype(bf16)
        dv = DOT(p.astype(bf16), dd_ref[...])
        dk = DOT(ds, q_ref[...])
        dqt_ref[...] += DOT(k.T, ds)
        g_ref[j, :rows, 64:] = dk.astype(bf16)
        g_ref[j, rows:, :] = jnp.concatenate([dv[:half], dv[half:]], axis=1).astype(bf16)
        return 0
    lax.fori_loop(0, nb, step, 0, unroll=2)
    for j in range(nb):
        g_ref[j, :rows, :64] = (dqt_ref[:, j * rows : (j + 1) * rows].T * 0.125).astype(bf16)

def attn_bwd(x, d, of, lse):
    nb, rows3, _ = x.shape
    half = rows3 // 3
    n = nb * half * 2
    return pl.pallas_call(
        attn_bwd_kernel,
        out_shape=jax.ShapeDtypeStruct((nb, rows3, 128), bf16),
        scratch_shapes=[pltpu.VMEM((64, n), bf16), pltpu.VMEM((64, n), bf16), pltpu.VMEM((n, 64), bf16), pltpu.VMEM((n, 64), bf16),
                        pltpu.VMEM((8, n), f32), pltpu.VMEM((8, n), f32), pltpu.VMEM((64, n), f32)],
        cost_estimate=pl.CostEstimate(flops=10 * n * n * 64, bytes_accessed=n * 64 * 2 * 12, transcendentals=n * n),
        compiler_params=pltpu.CompilerParams(vmem_limit_bytes=48 << 20),
        name="attn_bwd",
    )(x, d, of, lse)

HEADS = 12
HEAD_DIM = 64
SEQ_MB = 1
MICRO = 2


eps_norm = 1e-06
shard_group = 4


def normalize(values):
    average = jnp.mean(values, axis=-1, keepdims=True)
    centered = values - average
    variance = jnp.mean(centered * centered, axis=-1, keepdims=True)
    inv_std = lax.rsqrt(variance + eps_norm)
    return (centered * inv_std, inv_std)


def norm_back(grad_out, normed, inv_std, gain, scale_mod):
    factor = 1.0 + scale_mod
    d_normed = grad_out * gain * factor
    gain_term = jnp.sum(grad_out * normed * factor, axis=(0, 1))
    scale_term = jnp.sum(grad_out * normed * gain, axis=1)
    shift_term = jnp.sum(grad_out, axis=1)
    centred = d_normed - jnp.mean(d_normed, axis=-1, keepdims=True)
    d_inputs = inv_std * (centred - normed * jnp.mean(d_normed * normed, axis=-1, keepdims=True))
    return (d_inputs, gain_term, scale_term, shift_term)


def rotary_tables(positions):
    half_dim = HEAD_DIM // 2
    frequency = jnp.exp(
        -jnp.log(10000.0) * jnp.arange(half_dim, dtype=jnp.float32) * 2.0 / HEAD_DIM
    )
    angles = positions[:, None] * frequency[None, :]
    return (jnp.cos(angles)[:, None, :], jnp.sin(angles)[:, None, :])


def rotate(values, cos_table, sin_table):
    half_dim = values.shape[-1] // 2
    first_half = values[..., :half_dim]
    second_half = values[..., half_dim:]
    return jnp.concatenate(
        [
            first_half * cos_table - second_half * sin_table,
            second_half * cos_table + first_half * sin_table,
        ],
        axis=-1,
    )


def unrotate(grads, cos_table, sin_table):
    half_dim = grads.shape[-1] // 2
    first_half = grads[..., :half_dim]
    second_half = grads[..., half_dim:]
    return jnp.concatenate(
        [
            first_half * cos_table + second_half * sin_table,
            second_half * cos_table - first_half * sin_table,
        ],
        axis=-1,
    )


def gelu_tanh(values):
    return jax.nn.gelu(values, approximate=True)


def split_pairs(block):
    batch_seqs = block.shape[0]
    key_rows = block.shape[1]
    heads_here = block.shape[3] // HEAD_DIM
    keys = block[:, :, 0].reshape(batch_seqs, key_rows, heads_here, HEAD_DIM)
    values = block[:, :, 1].reshape(batch_seqs, key_rows, heads_here, HEAD_DIM)
    return (keys, values)


def split_blocks(piece, shard_rows):
    count = piece.shape[1] // shard_rows
    group = math.gcd(count, shard_group)
    steps = count // group
    shaped = piece.reshape((piece.shape[0], steps, group * shard_rows) + piece.shape[2:])
    return jnp.moveaxis(shaped, 1, 0)


def forward_block(query_heads, carry, block):
    top, totals, accum = carry
    keys, values = split_pairs(block)
    scores = jnp.einsum(
        "shqd,skhd->shqk", query_heads, keys, preferred_element_type=jnp.float32
    ) * HEAD_DIM ** (-0.5)
    new_top = jnp.maximum(top, jnp.max(scores, axis=-1))
    probs = jnp.exp(scores - new_top[..., None])
    fade = jnp.exp(top - new_top)
    totals = totals * fade + jnp.sum(probs, axis=-1)
    accum = accum * fade[..., None] + jnp.einsum(
        "shqk,skhd->shqd", probs.astype(jnp.bfloat16), values, preferred_element_type=jnp.float32
    )
    return (new_top, totals, accum)


def shards(inputs, conditioning, w_ada, w_qkv, w_out, w_up, w_down, gain_one, gain_two, cotangent):
    gathered = (
        lax.all_gather(w_ada, ("ulysses", "blk"), axis=1, tiled=True),
        lax.all_gather(w_qkv, ("ulysses", "blk"), axis=0, tiled=True),
        lax.all_gather(w_out, ("ulysses", "blk"), axis=0, tiled=True),
        lax.all_gather(w_up, ("ulysses", "blk"), axis=0, tiled=True),
        lax.all_gather(w_down, ("ulysses", "blk"), axis=0, tiled=True),
        lax.all_gather(gain_one, ("ulysses", "blk"), axis=0, tiled=True),
        lax.all_gather(gain_two, ("ulysses", "blk"), axis=0, tiled=True),
    )
    ada_full, qkv_full, out_full, up_full, down_full = (
        gathered[0],
        gathered[1],
        gathered[2],
        gathered[3],
        gathered[4],
    )
    gain_first = gathered[5].astype(jnp.float32)
    gain_second = gathered[6].astype(jnp.float32)
    rows = inputs.shape[1]
    width = inputs.shape[2]
    device_index = lax.axis_index(("ulysses", "blk"))
    positions = (device_index * rows + jnp.arange(rows, dtype=jnp.int32)).astype(jnp.float32)
    cos_table, sin_table = rotary_tables(positions)
    score_scale = HEAD_DIM ** (-0.5)
    ada_cols = w_ada.shape[1]
    grad_shapes = (
        w_qkv.shape,
        w_out.shape,
        w_up.shape,
        w_down.shape,
        gain_one.shape,
        gain_two.shape,
    )
    grad_totals = tuple((jnp.zeros(shape, jnp.float32) for shape in grad_shapes))
    ada_grad = jnp.zeros(w_ada.shape, jnp.float32)
    outputs_list = []
    input_grads = []
    cond_grads = []
    for micro_step in range(MICRO):
        offset = micro_step * SEQ_MB
        seq_inputs = inputs[offset : offset + SEQ_MB].astype(jnp.float32)
        cond_rows = conditioning[offset : offset + SEQ_MB]
        modulation = jnp.dot(cond_rows, ada_full, preferred_element_type=jnp.float32)
        pieces = [p[:, None, :] for p in jnp.split(modulation, 6, axis=1)]
        shift_one, scale_one, gate_one, shift_two, scale_two, gate_two = pieces
        normed_one, inv_one = normalize(seq_inputs)
        first_in = (normed_one * gain_first * (1.0 + scale_one) + shift_one).astype(jnp.bfloat16)
        projected = jnp.dot(first_in, qkv_full, preferred_element_type=jnp.float32)
        projected = projected.reshape(SEQ_MB, rows, 3, HEADS, HEAD_DIM)
        rot_query = rotate(projected[:, :, 0], cos_table, sin_table)
        rot_key = rotate(projected[:, :, 1], cos_table, sin_table)
        packed = jnp.stack([rot_query, rot_key, projected[:, :, 2]], axis=2).reshape(
            SEQ_MB, rows, 3, width
        )
        regrouped = lax.all_to_all(
            packed.astype(jnp.bfloat16), "ulysses", split_axis=3, concat_axis=1, tiled=True
        )
        query_rows = regrouped.shape[1]
        head_width = regrouped.shape[3]
        local_heads = head_width // HEAD_DIM
        query_heads = (
            regrouped[:, :, 0]
            .reshape(SEQ_MB, query_rows, local_heads, HEAD_DIM)
            .transpose(0, 2, 1, 3)
        )
        kv_local = regrouped[:, :, 1:]
        start_carry = (
            jnp.full((SEQ_MB, local_heads, query_rows), -1e30, jnp.float32),
            jnp.zeros((SEQ_MB, local_heads, query_rows), jnp.float32),
            jnp.zeros((SEQ_MB, local_heads, query_rows, HEAD_DIM), jnp.float32),
        )

        def scan_forward(carry, block):
            return (forward_block(query_heads, carry, block), None)

        result, _ = lax.scan(
            scan_forward,
            start_carry,
            split_blocks(lax.all_gather(kv_local, "blk", axis=1, tiled=True), query_rows),
        )
        carry = result
        top, totals, accum = carry
        attn_heads = accum / totals[..., None]
        log_total = top + jnp.log(totals)
        attn_tokens = (
            attn_heads.astype(jnp.bfloat16)
            .transpose(0, 2, 1, 3)
            .reshape(SEQ_MB, query_rows, head_width)
        )
        attended = lax.all_to_all(attn_tokens, "ulysses", split_axis=1, concat_axis=2, tiled=True)
        branch = jnp.dot(attended, out_full, preferred_element_type=jnp.float32)
        middle = seq_inputs + gate_one * branch
        normed_two, inv_two = normalize(middle)
        second_in = (normed_two * gain_second * (1.0 + scale_two) + shift_two).astype(jnp.bfloat16)
        raised = jnp.dot(second_in, up_full, preferred_element_type=jnp.float32)
        hidden, gelu_pull = jax.vjp(gelu_tanh, raised)
        hidden_low = hidden.astype(jnp.bfloat16)
        lowered = jnp.dot(hidden_low, down_full, preferred_element_type=jnp.float32)
        outputs_list.append(middle + gate_two * lowered)
        grad_out = cotangent[offset : offset + SEQ_MB].astype(jnp.float32)
        d_lowered = (gate_two * grad_out).astype(jnp.bfloat16)
        d_gate_two = jnp.sum(grad_out * lowered, axis=1)
        down_term = jnp.einsum(
            "srf,srd->fd", hidden_low, d_lowered, preferred_element_type=jnp.float32
        )
        d_hidden = jnp.einsum(
            "srd,fd->srf", d_lowered, down_full, preferred_element_type=jnp.float32
        )
        (d_raised,) = gelu_pull(d_hidden)
        d_raised_low = d_raised.astype(jnp.bfloat16)
        up_term = jnp.einsum(
            "srd,srf->df", second_in, d_raised_low, preferred_element_type=jnp.float32
        )
        d_second = jnp.einsum(
            "srf,df->srd", d_raised_low, up_full, preferred_element_type=jnp.float32
        )
        d_norm_two, gain_two_term, d_scale_two, d_shift_two = norm_back(
            d_second, normed_two, inv_two, gain_second, scale_two
        )
        d_middle = grad_out + d_norm_two
        d_gate_one = jnp.sum(d_middle * branch, axis=1)
        d_branch = (gate_one * d_middle).astype(jnp.bfloat16)
        out_term = jnp.einsum("srd,sre->de", attended, d_branch, preferred_element_type=jnp.float32)
        d_attended = jnp.einsum(
            "sre,de->srd", d_branch, out_full, preferred_element_type=jnp.float32
        ).astype(jnp.bfloat16)
        d_attn_rows = lax.all_to_all(d_attended, "ulysses", split_axis=2, concat_axis=1, tiled=True)
        d_attn_heads = d_attn_rows.reshape(SEQ_MB, query_rows, local_heads, HEAD_DIM).transpose(
            0, 2, 1, 3
        )
        delta = jnp.sum(d_attn_heads.astype(jnp.float32) * attn_heads, axis=-1)
        all_pairs = lax.all_gather(kv_local, "blk", axis=1, tiled=True)

        def back_step(d_query, block):
            keys, values = split_pairs(block)
            scores = (
                jnp.einsum("shqd,skhd->shqk", query_heads, keys, preferred_element_type=jnp.float32)
                * score_scale
            )
            probs = jnp.exp(scores - log_total[..., None])
            d_probs = jnp.einsum(
                "shqd,skhd->shqk", d_attn_heads, values, preferred_element_type=jnp.float32
            )
            d_scores = (probs * (d_probs - delta[..., None])).astype(jnp.bfloat16)
            d_query = (
                d_query
                + jnp.einsum("shqk,skhd->shqd", d_scores, keys, preferred_element_type=jnp.float32)
                * score_scale
            )
            d_keys = (
                jnp.einsum(
                    "shqk,shqd->skhd", d_scores, query_heads, preferred_element_type=jnp.float32
                )
                * score_scale
            )
            d_values = jnp.einsum(
                "shqk,shqd->skhd",
                probs.astype(jnp.bfloat16),
                d_attn_heads,
                preferred_element_type=jnp.float32,
            )
            key_rows = block.shape[1]
            pair = jnp.stack(
                [
                    d_keys.reshape(SEQ_MB, key_rows, head_width),
                    d_values.reshape(SEQ_MB, key_rows, head_width),
                ],
                axis=2,
            )
            return (d_query, pair)

        query_zero = jnp.zeros((SEQ_MB, local_heads, query_rows, HEAD_DIM), jnp.float32)
        d_query, pair_terms = lax.scan(back_step, query_zero, split_blocks(all_pairs, query_rows))
        pair_terms = jnp.moveaxis(pair_terms, 0, 1)
        pair_terms = pair_terms.reshape(
            SEQ_MB, pair_terms.shape[1] * pair_terms.shape[2], 2, head_width
        )
        pair_sums = lax.psum_scatter(pair_terms, "blk", scatter_dimension=1, tiled=True)
        query_grad = d_query.transpose(0, 2, 1, 3).reshape(SEQ_MB, query_rows, 1, head_width)
        d_packed = jnp.concatenate([query_grad, pair_sums], axis=2).astype(jnp.bfloat16)
        d_local = lax.all_to_all(d_packed, "ulysses", split_axis=1, concat_axis=3, tiled=True)
        d_local = d_local.astype(jnp.float32).reshape(SEQ_MB, rows, 3, HEADS, HEAD_DIM)
        d_projected = (
            jnp.stack(
                [
                    unrotate(d_local[:, :, 0], cos_table, sin_table),
                    unrotate(d_local[:, :, 1], cos_table, sin_table),
                    d_local[:, :, 2],
                ],
                axis=2,
            )
            .reshape(SEQ_MB, rows, 3 * width)
            .astype(jnp.bfloat16)
        )
        qkv_term = jnp.einsum(
            "srd,sre->de", first_in, d_projected, preferred_element_type=jnp.float32
        )
        d_first = jnp.einsum(
            "sre,de->srd", d_projected, qkv_full, preferred_element_type=jnp.float32
        )
        d_norm_one, gain_one_term, d_scale_one, d_shift_one = norm_back(
            d_first, normed_one, inv_one, gain_first, scale_one
        )
        input_grads.append(d_middle + d_norm_one)
        mod_local = jnp.concatenate(
            [d_shift_one, d_scale_one, d_gate_one, d_shift_two, d_scale_two, d_gate_two], axis=1
        )
        mod_total = lax.psum(mod_local, ("ulysses", "blk"))
        mod_low = mod_total.astype(jnp.bfloat16)
        cond_grads.append(
            jnp.einsum("sm,cm->sc", mod_low, ada_full, preferred_element_type=jnp.float32)
        )
        mod_part = lax.dynamic_slice_in_dim(mod_low, device_index * ada_cols, ada_cols, 1)
        ada_grad = ada_grad + jnp.einsum(
            "sc,sm->cm", cond_rows, mod_part, preferred_element_type=jnp.float32
        )
        terms = (qkv_term, out_term, up_term, down_term, gain_one_term, gain_two_term)
        reduced = (
            lax.psum_scatter(terms[0], ("ulysses", "blk"), scatter_dimension=0, tiled=True),
            lax.psum_scatter(terms[1], ("ulysses", "blk"), scatter_dimension=0, tiled=True),
            lax.psum_scatter(terms[2], ("ulysses", "blk"), scatter_dimension=0, tiled=True),
            lax.psum_scatter(terms[3], ("ulysses", "blk"), scatter_dimension=0, tiled=True),
            lax.psum_scatter(terms[4], ("ulysses", "blk"), scatter_dimension=0, tiled=True),
            lax.psum_scatter(terms[5], ("ulysses", "blk"), scatter_dimension=0, tiled=True),
        )
        grad_totals = tuple((a + b for a, b in zip(grad_totals, reduced)))
    output = jnp.concatenate(outputs_list, axis=0)
    inputs_grad = jnp.concatenate(input_grads, axis=0)
    conditioning_grad = jnp.concatenate(cond_grads, axis=0)
    return (
        output,
        inputs_grad,
        conditioning_grad,
        ada_grad,
        grad_totals[0],
        grad_totals[1],
        grad_totals[2],
        grad_totals[3],
        grad_totals[4],
        grad_totals[5],
    )


def fits_tp(mesh):
    ulysses, blk = mesh.shape["ulysses"], mesh.shape["blk"]
    return ulysses == 4 and blk == 8 and HEADS % ulysses == 0


def swap_u(values, mask):
    return lax.ppermute(values, "ulysses", [(i, i ^ mask) for i in range(4)])


def swap_b(values, mask):
    return lax.ppermute(values, "blk", [(i, i ^ mask) for i in range(8)])


def gather_u(values):
    across = swap_u(values, 2)
    return jnp.stack([values, swap_u(values, 1), across, swap_u(across, 1)])


def half_sum_u(parts):
    got = swap_u(jnp.stack([parts[1], parts[3]]).astype(bf16), 1).astype(f32)
    return parts[0] + got[0], parts[2] + got[1]


def scatter_sum_u(parts):
    near, far = half_sum_u(parts)
    return near + swap_u(far.astype(bf16), 2).astype(f32)


def sum_u(parts):
    near, far = half_sum_u(parts)
    got = swap_u(jnp.stack([near, far]).astype(bf16), 2).astype(f32)
    near, far = near + got[1], far + got[0]
    got = swap_u(jnp.stack([near, far]).astype(bf16), 1).astype(f32)
    return jnp.stack([near, got[0], far, got[1]])


def sum_all(values):
    values = values + swap_u(values, 1)
    values = values + swap_u(values, 2)
    for mask in (1, 2, 4):
        values = values + swap_b(values, mask)
    return values


def pick(values, index, axis=0):
    return lax.dynamic_index_in_dim(values, index, axis, keepdims=False)


def pack_halves(values):
    lead, rows = values.shape[:-2], values.shape[-2]
    return jnp.concatenate(
        [values[..., : rows // 2, :], values[..., rows // 2 :, :]], axis=-1
    ).reshape(lead + (rows // 2, 2 * HEAD_DIM))


def unpack_halves(values):
    return jnp.concatenate([values[..., :HEAD_DIM], values[..., HEAD_DIM:]], axis=-2)


def to_owners(chunks):
    blank = jnp.zeros((1,) + chunks.shape[1:], chunks.dtype)
    return lax.all_to_all(
        jnp.concatenate([blank, chunks, blank]), "blk", split_axis=0, concat_axis=0, tiled=True
    )


def from_owners(blocks):
    return lax.all_to_all(blocks, "blk", split_axis=0, concat_axis=0, tiled=True)[1:-1]


def tp_shards(inputs, conditioning, w_ada, w_qkv, w_out, w_up, w_down, gain_one, gain_two, cotangent):
    n_u, n_b = 4, 8
    seqs, rows, width = inputs.shape
    u = lax.axis_index("ulysses")
    b = lax.axis_index("blk")
    device_index = u * n_b + b
    local_heads = HEADS // n_u
    head_width = local_heads * HEAD_DIM
    w_rows = w_qkv.shape[0]
    ff_local = w_up.shape[1] // n_u
    tokens = n_u * seqs * rows
    ada_cols = w_ada.shape[1]

    x_all = gather_u(inputs)

    qkv_pieces = w_qkv.reshape(w_rows, 3, n_u, head_width)
    qkv_near = jnp.stack(
        [pick(qkv_pieces, u, 2)] + [swap_u(pick(qkv_pieces, u ^ m, 2), m) for m in (1, 2, 3)]
    ).reshape(n_u * w_rows, 3 * head_width)
    qkv_z = [qkv_near] + [swap_b(qkv_near, 2 * m) for m in (1, 2, 3)]
    qkv_rel = jnp.concatenate(qkv_z + [swap_b(part, 1) for part in qkv_z], axis=0)
    column = jnp.arange(width, dtype=jnp.int32)
    part_y = column // (n_u * n_u * w_rows)
    part_z = (column // (n_u * w_rows)) % 4
    part_u = (column // w_rows) % n_u
    home = ((u ^ part_u) * n_b + (b ^ (2 * part_z + part_y))) * w_rows + column % w_rows
    order = (jnp.arange(width, dtype=jnp.int32)[:, None] == home[None, :]).astype(bf16)
    w_qkv_u = DOT(order, qkv_rel).astype(bf16)

    mod_own = jnp.dot(conditioning, w_ada, preferred_element_type=f32)
    mod_all = lax.dynamic_update_slice_in_dim(
        jnp.zeros((seqs, 6 * width), f32), mod_own, device_index * ada_cols, 1
    )
    gains_own = jnp.stack([gain_one, gain_two]).astype(f32)
    gains_all = lax.dynamic_update_slice_in_dim(
        jnp.zeros((2, width), f32), gains_own, device_index * gain_one.shape[0], 1
    )
    table = sum_all(jnp.concatenate([mod_all, gains_all], axis=1))
    shift_one, scale_one, gate_one, shift_two, scale_two, gate_two = [
        table[None, :, None, i * width : (i + 1) * width] for i in range(6)
    ]
    gain_first = table[0, 6 * width :]
    gain_second = table[1, 6 * width :]

    up_pieces = w_up.reshape(w_rows, n_u, ff_local)
    up_near = [pick(up_pieces, u, 1)] + [swap_u(pick(up_pieces, u ^ m, 1), m) for m in (1, 2, 3)]
    slices = lax.all_gather(
        jnp.concatenate(up_near + [w_down, w_out], axis=0), "blk", axis=0, tiled=False
    )
    up_rows = n_u * w_rows
    home_up = ((u ^ part_u) * n_b + column // up_rows) * w_rows + column % w_rows
    order_up = (jnp.arange(width, dtype=jnp.int32)[:, None] == home_up[None, :]).astype(bf16)
    w_up_u = DOT(order_up, slices[:, :up_rows].reshape(width, ff_local)).astype(bf16)
    w_down_u = slices[:, up_rows : up_rows + w_down.shape[0]].reshape(ff_local, width)
    w_out_u = slices[:, up_rows + w_down.shape[0] :].reshape(head_width, width)
    g_all = gather_u(cotangent)
    ada_rows = lax.all_gather(w_ada.T, ("ulysses", "blk"), axis=0, tiled=True)

    x_f = x_all.astype(f32)
    normed_one, inv_one = normalize(x_f)
    first_in = (normed_one * gain_first * (1.0 + scale_one) + shift_one).astype(bf16)
    first_in = first_in.reshape(tokens, width)
    blocks = u ^ jnp.arange(n_u, dtype=jnp.int32)
    positions = ((blocks * n_b + b) * rows)[:, None] + jnp.arange(rows, dtype=jnp.int32)[None, :]
    cos_table, sin_table = rotary_tables(positions.reshape(-1).astype(f32))
    cos_table = cos_table.reshape(n_u, 1, rows, 1, HEAD_DIM // 2)
    sin_table = sin_table.reshape(n_u, 1, rows, 1, HEAD_DIM // 2)
    projected = DOT(first_in, w_qkv_u).reshape(n_u, seqs, rows, 3, local_heads, HEAD_DIM)

    def by_pair(values):
        return values.transpose(1, 3, 0, 2, 4).reshape(seqs * local_heads, n_u * rows, HEAD_DIM)

    def by_token(values):
        shaped = values.reshape(seqs, local_heads, n_u, rows, HEAD_DIM)
        return shaped.transpose(2, 0, 3, 1, 4)

    queries = by_pair(rotate(projected[:, :, :, 0], cos_table, sin_table).astype(bf16))
    keys = by_pair(rotate(projected[:, :, :, 1], cos_table, sin_table).astype(bf16))
    values = by_pair(projected[:, :, :, 2].astype(bf16))
    owned = to_owners(
        jnp.concatenate(
            [jnp.concatenate([queries, keys], axis=2), pack_halves(values)], axis=1
        )
    )
    attn_low, attn_full, log_total = attn_fwd(owned)
    attended = by_token(unpack_halves(from_owners(attn_low))).reshape(tokens, head_width)

    full = (n_u, seqs, rows, width)
    branch = sum_u(DOT(attended, w_out_u).reshape(full))
    middle = x_f + gate_one * branch
    normed_two, inv_two = normalize(middle)
    second_in = (normed_two * gain_second * (1.0 + scale_two) + shift_two).astype(bf16)
    second_in = second_in.reshape(tokens, width)
    raised = DOT(second_in, w_up_u)
    hidden, gelu_pull = jax.vjp(gelu_tanh, raised)
    hidden = hidden.astype(bf16)
    lowered_part = DOT(hidden, w_down_u).reshape(full)

    grad_out = g_all.astype(f32)
    d_lowered = (gate_two * grad_out).astype(bf16).reshape(tokens, width)
    d_hidden = jnp.einsum("td,fd->tf", d_lowered, w_down_u, preferred_element_type=f32)
    d_raised = gelu_pull(d_hidden)[0].astype(bf16)
    d_second_part = jnp.einsum("tf,df->td", d_raised, w_up_u, preferred_element_type=f32)
    d_second_part = d_second_part.reshape(full)
    d_second = sum_u(d_second_part)
    factor_two = gain_second * (1.0 + scale_two)
    e_two = d_second * factor_two
    d_middle = grad_out + inv_two * (
        e_two
        - jnp.mean(e_two, axis=-1, keepdims=True)
        - normed_two * jnp.mean(e_two * normed_two, axis=-1, keepdims=True)
    )
    d_branch = (gate_one * d_middle).astype(bf16).reshape(tokens, width)
    d_attended = jnp.einsum("td,ed->te", d_branch, w_out_u, preferred_element_type=f32)
    d_attended = d_attended.astype(bf16).reshape(n_u, seqs, rows, local_heads, HEAD_DIM)
    d_owned = to_owners(pack_halves(by_pair(d_attended)))

    output = middle[0] + gate_two[0] * scatter_sum_u(lowered_part)
    down_term = jnp.einsum("tf,td->fd", hidden, d_lowered, preferred_element_type=f32)
    up_term = jnp.einsum("td,tf->df", second_in, d_raised, preferred_element_type=f32)
    out_term = jnp.einsum("te,td->ed", attended, d_branch, preferred_element_type=f32)
    sums_two = sum_all(
        jnp.concatenate(
            [
                jnp.sum(d_middle[0] * branch[0], axis=1),
                jnp.sum(d_second_part, axis=(0, 2)),
                jnp.sum(d_second_part * normed_two, axis=(0, 2)),
                jnp.sum(grad_out * lowered_part, axis=(0, 2)),
            ],
            axis=1,
        )
    )
    up_blocks = up_term.reshape(n_u, n_b, w_rows, ff_local)
    down_blocks = down_term.reshape(n_b, w_down.shape[0], width)
    out_blocks = out_term.reshape(n_b, w_rows, width)

    def ff_block(m):
        return jnp.concatenate(
            [
                pick(up_blocks, b ^ m, 1).reshape(up_rows, width),
                pick(down_blocks, b ^ m),
                pick(out_blocks, b ^ m),
            ],
            axis=0,
        )

    ff_sum = ff_block(0)
    for m in range(1, n_b):
        ff_sum = ff_sum + swap_b(ff_block(m).astype(bf16), m).astype(f32)
    up_grad = lax.all_to_all(
        ff_sum[:up_rows].reshape(n_u, w_rows, ff_local),
        "ulysses",
        split_axis=0,
        concat_axis=0,
        tiled=True,
    )
    up_grad = up_grad.transpose(1, 0, 2).reshape(w_up.shape)
    down_grad = ff_sum[up_rows : up_rows + w_down.shape[0]]
    out_grad = ff_sum[up_rows + w_down.shape[0] :]

    grads = from_owners(attn_bwd(owned, d_owned, attn_full, log_total)).astype(f32)
    span = n_u * rows
    d_query = by_token(grads[:, :span, :HEAD_DIM])
    d_key = by_token(grads[:, :span, HEAD_DIM:])
    d_value = by_token(unpack_halves(grads[:, span:]))
    d_projected = (
        jnp.stack(
            [
                unrotate(d_query, cos_table, sin_table),
                unrotate(d_key, cos_table, sin_table),
                d_value,
            ],
            axis=3,
        )
        .reshape(tokens, 3 * head_width)
        .astype(bf16)
    )
    d_first_part = jnp.einsum("te,de->td", d_projected, w_qkv_u, preferred_element_type=f32)
    d_first_part = d_first_part.reshape(full)
    d_first = scatter_sum_u(d_first_part)
    e_one = d_first * (gain_first * (1.0 + scale_one[0]))
    inputs_grad = d_middle[0] + inv_one[0] * (
        e_one
        - jnp.mean(e_one, axis=-1, keepdims=True)
        - normed_one[0] * jnp.mean(e_one * normed_one[0], axis=-1, keepdims=True)
    )
    qkv_term = jnp.einsum("td,te->de", first_in, d_projected, preferred_element_type=f32)
    qkv_blocks = qkv_term.reshape(n_u, n_b, w_rows, 3 * head_width)
    qkv_sum = pick(qkv_blocks, b, 1)
    for m in range(1, n_b):
        qkv_sum = qkv_sum + swap_b(pick(qkv_blocks, b ^ m, 1).astype(bf16), m).astype(f32)
    qkv_grad = lax.all_to_all(qkv_sum, "ulysses", split_axis=0, concat_axis=0, tiled=True)
    qkv_grad = qkv_grad.reshape(n_u, w_rows, 3, head_width).transpose(1, 2, 0, 3)
    qkv_grad = qkv_grad.reshape(w_qkv.shape)

    sums_one = sum_all(
        jnp.concatenate(
            [
                jnp.sum(d_first_part, axis=(0, 2)),
                jnp.sum(d_first_part * normed_one, axis=(0, 2)),
            ],
            axis=1,
        )
    )
    d_gate_one, d_shift_two, dot_two, d_gate_two = [
        sums_two[:, i * width : (i + 1) * width] for i in range(4)
    ]
    d_shift_one, dot_one = sums_one[:, :width], sums_one[:, width:]
    gain_one_full = jnp.sum((1.0 + scale_one[0, :, 0]) * dot_one, axis=0)
    gain_two_full = jnp.sum((1.0 + scale_two[0, :, 0]) * dot_two, axis=0)
    gain_cols = gain_one.shape[0]
    gain_one_grad = lax.dynamic_slice_in_dim(gain_one_full, device_index * gain_cols, gain_cols, 0)
    gain_two_grad = lax.dynamic_slice_in_dim(gain_two_full, device_index * gain_cols, gain_cols, 0)
    mod_low = jnp.concatenate(
        [d_shift_one, dot_one * gain_first, d_gate_one, d_shift_two, dot_two * gain_second, d_gate_two],
        axis=1,
    ).astype(bf16)
    conditioning_grad = DOT(mod_low, ada_rows)
    mod_part = lax.dynamic_slice_in_dim(mod_low, device_index * ada_cols, ada_cols, 1)
    ada_grad = jnp.einsum("sc,sm->cm", conditioning, mod_part, preferred_element_type=f32)
    return (
        output,
        inputs_grad,
        conditioning_grad,
        ada_grad,
        qkv_grad,
        out_grad,
        up_grad,
        down_grad,
        gain_one_grad,
        gain_two_grad,
    )


def solution(mesh):
    body = tp_shards if fits_tp(mesh) else shards
    in_specs = (
        P(None, ("ulysses", "blk"), None),
        P(),
        P(None, ("ulysses", "blk")),
        P(("ulysses", "blk"), None),
        P(("ulysses", "blk"), None),
        P(("ulysses", "blk"), None),
        P(("ulysses", "blk"), None),
        P(("ulysses", "blk")),
        P(("ulysses", "blk")),
        P(None, ("ulysses", "blk"), None),
    )
    out_specs = (
        P(None, ("ulysses", "blk"), None),
        P(None, ("ulysses", "blk"), None),
        P(),
        P(None, ("ulysses", "blk")),
        P(("ulysses", "blk"), None),
        P(("ulysses", "blk"), None),
        P(("ulysses", "blk"), None),
        P(("ulysses", "blk"), None),
        P(("ulysses", "blk")),
        P(("ulysses", "blk")),
    )
    return jax.shard_map(body, mesh=mesh, in_specs=in_specs, out_specs=out_specs, check_vma=False)
```

```python
import functools
import math

import jax
import jax.numpy as jnp
from jax import lax
from jax.experimental import pallas as pl
from jax.experimental.pallas import tpu as pltpu
from jax.sharding import PartitionSpec as P

f32, bf16 = jnp.float32, jnp.bfloat16
DOT = functools.partial(jnp.dot, preferred_element_type=f32)

def attn_fwd_kernel(x_ref, o_ref, of_ref, lse_ref, kt_ref, v_ref):
    nb, rows3, _ = x_ref.shape
    half = rows3 // 3
    rows = 2 * half
    for j in range(nb):
        kt_ref[:, j * rows : (j + 1) * rows] = x_ref[j, :rows, 64:].T
        v_ref[j * rows : j * rows + half, :] = x_ref[j, rows:, :64]
        v_ref[j * rows + half : (j + 1) * rows, :] = x_ref[j, rows:, 64:]

    def step(j, _):
        q = x_ref[j, :rows, :64] * jnp.asarray(0.125, bf16)
        s = DOT(q, kt_ref[...])
        top = jnp.max(s, axis=1, keepdims=True)
        p = jnp.exp(s - top)
        total = jnp.sum(p, axis=1, keepdims=True)
        o = DOT(p.astype(bf16), v_ref[...]) / total
        packed = jnp.concatenate([o[:half], o[half:]], axis=1)
        of_ref[j] = packed
        o_ref[j] = packed.astype(bf16)
        lse = jnp.broadcast_to(top + jnp.log(total), (rows, 128)).T
        lse_ref[j] = lse[:8]
        return 0
    lax.fori_loop(0, nb, step, 0, unroll=2)

def attn_fwd(x):
    nb, rows3, _ = x.shape
    half = rows3 // 3
    n = nb * half * 2
    return pl.pallas_call(
        attn_fwd_kernel,
        out_shape=(jax.ShapeDtypeStruct((nb, half, 128), bf16), jax.ShapeDtypeStruct((nb, half, 128), f32),
                   jax.ShapeDtypeStruct((nb, 8, 2 * half), f32)),
        scratch_shapes=[pltpu.VMEM((64, n), bf16), pltpu.VMEM((n, 64), bf16)],
        cost_estimate=pl.CostEstimate(flops=4 * n * n * 64, bytes_accessed=n * 64 * 2 * 8, transcendentals=n * n),
        compiler_params=pltpu.CompilerParams(vmem_limit_bytes=32 << 20),
        name="attn_fwd",
    )(x)

def attn_bwd_kernel(x_ref, d_ref, of_ref, lse_ref, g_ref, qt_ref, dt_ref, q_ref, dd_ref, lse_s, del_s, dqt_ref):
    nb, rows3, _ = x_ref.shape
    half = rows3 // 3
    rows = 2 * half
    for j in range(nb):
        sl = slice(j * rows, (j + 1) * rows)
        q = x_ref[j, :rows, :64] * jnp.asarray(0.125, bf16)
        q_ref[sl, :] = q
        qt_ref[:, sl] = q.T
        d = jnp.concatenate([d_ref[j, :, :64], d_ref[j, :, 64:]], axis=0)
        dd_ref[sl, :] = d
        dt_ref[:, sl] = d.T
        o = jnp.concatenate([of_ref[j, :, :64], of_ref[j, :, 64:]], axis=0)
        delta = jnp.sum(d.astype(f32) * o, axis=1, keepdims=True)
        del_s[:, sl] = jnp.broadcast_to(delta, (rows, 128)).T[:8]
        lse_s[:, sl] = lse_ref[j]
    dqt_ref[...] = jnp.zeros_like(dqt_ref)

    def step(j, _):
        k = x_ref[j, :rows, 64:]
        v = jnp.concatenate([x_ref[j, rows:, :64], x_ref[j, rows:, 64:]], axis=0)
        s = DOT(k, qt_ref[...])
        p = jnp.exp(s - lse_s[0:1, :])
        dp = DOT(v, dt_ref[...])
        ds = (p * (dp - del_s[0:1, :])).astype(bf16)
        dv = DOT(p.astype(bf16), dd_ref[...])
        dk = DOT(ds, q_ref[...])
        dqt_ref[...] += DOT(k.T, ds)
        g_ref[j, :rows, 64:] = dk.astype(bf16)
        g_ref[j, rows:, :] = jnp.concatenate([dv[:half], dv[half:]], axis=1).astype(bf16)
        return 0
    lax.fori_loop(0, nb, step, 0, unroll=2)
    for j in range(nb):
        g_ref[j, :rows, :64] = (dqt_ref[:, j * rows : (j + 1) * rows].T * 0.125).astype(bf16)

def attn_bwd(x, d, of, lse):
    nb, rows3, _ = x.shape
    half = rows3 // 3
    n = nb * half * 2
    return pl.pallas_call(
        attn_bwd_kernel,
        out_shape=jax.ShapeDtypeStruct((nb, rows3, 128), bf16),
        scratch_shapes=[pltpu.VMEM((64, n), bf16), pltpu.VMEM((64, n), bf16), pltpu.VMEM((n, 64), bf16), pltpu.VMEM((n, 64), bf16),
                        pltpu.VMEM((8, n), f32), pltpu.VMEM((8, n), f32), pltpu.VMEM((64, n), f32)],
        cost_estimate=pl.CostEstimate(flops=n * n * 64, bytes_accessed=n * 64 * 2, transcendentals=0),
        compiler_params=pltpu.CompilerParams(vmem_limit_bytes=32 << 20),
        name="attn_bwd",
    )(x, d, of, lse)

HEADS = 12
HEAD_DIM = 64
SEQ_MB = 1
MICRO = 2


eps_norm = 1e-06
shard_group = 4


def normalize(values):
    average = jnp.mean(values, axis=-1, keepdims=True)
    centered = values - average
    variance = jnp.mean(centered * centered, axis=-1, keepdims=True)
    inv_std = lax.rsqrt(variance + eps_norm)
    return (centered * inv_std, inv_std)


def norm_back(grad_out, normed, inv_std, gain, scale_mod):
    factor = 1.0 + scale_mod
    d_normed = grad_out * gain * factor
    gain_term = jnp.sum(grad_out * normed * factor, axis=(0, 1))
    scale_term = jnp.sum(grad_out * normed * gain, axis=1)
    shift_term = jnp.sum(grad_out, axis=1)
    centred = d_normed - jnp.mean(d_normed, axis=-1, keepdims=True)
    d_inputs = inv_std * (centred - normed * jnp.mean(d_normed * normed, axis=-1, keepdims=True))
    return (d_inputs, gain_term, scale_term, shift_term)


def rotary_tables(positions):
    half_dim = HEAD_DIM // 2
    frequency = jnp.exp(
        -jnp.log(10000.0) * jnp.arange(half_dim, dtype=jnp.float32) * 2.0 / HEAD_DIM
    )
    angles = positions[:, None] * frequency[None, :]
    return (jnp.cos(angles)[:, None, :], jnp.sin(angles)[:, None, :])


def rotate(values, cos_table, sin_table):
    half_dim = values.shape[-1] // 2
    first_half = values[..., :half_dim]
    second_half = values[..., half_dim:]
    return jnp.concatenate(
        [
            first_half * cos_table - second_half * sin_table,
            second_half * cos_table + first_half * sin_table,
        ],
        axis=-1,
    )


def unrotate(grads, cos_table, sin_table):
    half_dim = grads.shape[-1] // 2
    first_half = grads[..., :half_dim]
    second_half = grads[..., half_dim:]
    return jnp.concatenate(
        [
            first_half * cos_table + second_half * sin_table,
            second_half * cos_table - first_half * sin_table,
        ],
        axis=-1,
    )


def gelu_tanh(values):
    return jax.nn.gelu(values, approximate=True)


def split_pairs(block):
    batch_seqs = block.shape[0]
    key_rows = block.shape[1]
    heads_here = block.shape[3] // HEAD_DIM
    keys = block[:, :, 0].reshape(batch_seqs, key_rows, heads_here, HEAD_DIM)
    values = block[:, :, 1].reshape(batch_seqs, key_rows, heads_here, HEAD_DIM)
    return (keys, values)


def split_blocks(piece, shard_rows):
    count = piece.shape[1] // shard_rows
    group = math.gcd(count, shard_group)
    steps = count // group
    shaped = piece.reshape((piece.shape[0], steps, group * shard_rows) + piece.shape[2:])
    return jnp.moveaxis(shaped, 1, 0)


def forward_block(query_heads, carry, block):
    top, totals, accum = carry
    keys, values = split_pairs(block)
    scores = jnp.einsum(
        "shqd,skhd->shqk", query_heads, keys, preferred_element_type=jnp.float32
    ) * HEAD_DIM ** (-0.5)
    new_top = jnp.maximum(top, jnp.max(scores, axis=-1))
    probs = jnp.exp(scores - new_top[..., None])
    fade = jnp.exp(top - new_top)
    totals = totals * fade + jnp.sum(probs, axis=-1)
    accum = accum * fade[..., None] + jnp.einsum(
        "shqk,skhd->shqd", probs.astype(jnp.bfloat16), values, preferred_element_type=jnp.float32
    )
    return (new_top, totals, accum)


def shards(inputs, conditioning, w_ada, w_qkv, w_out, w_up, w_down, gain_one, gain_two, cotangent):
    gathered = (
        lax.all_gather(w_ada, ("ulysses", "blk"), axis=1, tiled=True),
        lax.all_gather(w_qkv, ("ulysses", "blk"), axis=0, tiled=True),
        lax.all_gather(w_out, ("ulysses", "blk"), axis=0, tiled=True),
        lax.all_gather(w_up, ("ulysses", "blk"), axis=0, tiled=True),
        lax.all_gather(w_down, ("ulysses", "blk"), axis=0, tiled=True),
        lax.all_gather(gain_one, ("ulysses", "blk"), axis=0, tiled=True),
        lax.all_gather(gain_two, ("ulysses", "blk"), axis=0, tiled=True),
    )
    ada_full, qkv_full, out_full, up_full, down_full = (
        gathered[0],
        gathered[1],
        gathered[2],
        gathered[3],
        gathered[4],
    )
    gain_first = gathered[5].astype(jnp.float32)
    gain_second = gathered[6].astype(jnp.float32)
    rows = inputs.shape[1]
    width = inputs.shape[2]
    device_index = lax.axis_index(("ulysses", "blk"))
    positions = (device_index * rows + jnp.arange(rows, dtype=jnp.int32)).astype(jnp.float32)
    cos_table, sin_table = rotary_tables(positions)
    score_scale = HEAD_DIM ** (-0.5)
    ada_cols = w_ada.shape[1]
    grad_shapes = (
        w_qkv.shape,
        w_out.shape,
        w_up.shape,
        w_down.shape,
        gain_one.shape,
        gain_two.shape,
    )
    grad_totals = tuple((jnp.zeros(shape, jnp.float32) for shape in grad_shapes))
    ada_grad = jnp.zeros(w_ada.shape, jnp.float32)
    outputs_list = []
    input_grads = []
    cond_grads = []
    for micro_step in range(MICRO):
        offset = micro_step * SEQ_MB
        seq_inputs = inputs[offset : offset + SEQ_MB].astype(jnp.float32)
        cond_rows = conditioning[offset : offset + SEQ_MB]
        modulation = jnp.dot(cond_rows, ada_full, preferred_element_type=jnp.float32)
        pieces = [p[:, None, :] for p in jnp.split(modulation, 6, axis=1)]
        shift_one, scale_one, gate_one, shift_two, scale_two, gate_two = pieces
        normed_one, inv_one = normalize(seq_inputs)
        first_in = (normed_one * gain_first * (1.0 + scale_one) + shift_one).astype(jnp.bfloat16)
        projected = jnp.dot(first_in, qkv_full, preferred_element_type=jnp.float32)
        projected = projected.reshape(SEQ_MB, rows, 3, HEADS, HEAD_DIM)
        rot_query = rotate(projected[:, :, 0], cos_table, sin_table)
        rot_key = rotate(projected[:, :, 1], cos_table, sin_table)
        packed = jnp.stack([rot_query, rot_key, projected[:, :, 2]], axis=2).reshape(
            SEQ_MB, rows, 3, width
        )
        regrouped = lax.all_to_all(
            packed.astype(jnp.bfloat16), "ulysses", split_axis=3, concat_axis=1, tiled=True
        )
        query_rows = regrouped.shape[1]
        head_width = regrouped.shape[3]
        local_heads = head_width // HEAD_DIM
        query_heads = (
            regrouped[:, :, 0]
            .reshape(SEQ_MB, query_rows, local_heads, HEAD_DIM)
            .transpose(0, 2, 1, 3)
        )
        kv_local = regrouped[:, :, 1:]
        start_carry = (
            jnp.full((SEQ_MB, local_heads, query_rows), -1e30, jnp.float32),
            jnp.zeros((SEQ_MB, local_heads, query_rows), jnp.float32),
            jnp.zeros((SEQ_MB, local_heads, query_rows, HEAD_DIM), jnp.float32),
        )

        def scan_forward(carry, block):
            return (forward_block(query_heads, carry, block), None)

        result, _ = lax.scan(
            scan_forward,
            start_carry,
            split_blocks(lax.all_gather(kv_local, "blk", axis=1, tiled=True), query_rows),
        )
        carry = result
        top, totals, accum = carry
        attn_heads = accum / totals[..., None]
        log_total = top + jnp.log(totals)
        attn_tokens = (
            attn_heads.astype(jnp.bfloat16)
            .transpose(0, 2, 1, 3)
            .reshape(SEQ_MB, query_rows, head_width)
        )
        attended = lax.all_to_all(attn_tokens, "ulysses", split_axis=1, concat_axis=2, tiled=True)
        branch = jnp.dot(attended, out_full, preferred_element_type=jnp.float32)
        middle = seq_inputs + gate_one * branch
        normed_two, inv_two = normalize(middle)
        second_in = (normed_two * gain_second * (1.0 + scale_two) + shift_two).astype(jnp.bfloat16)
        raised = jnp.dot(second_in, up_full, preferred_element_type=jnp.float32)
        hidden, gelu_pull = jax.vjp(gelu_tanh, raised)
        hidden_low = hidden.astype(jnp.bfloat16)
        lowered = jnp.dot(hidden_low, down_full, preferred_element_type=jnp.float32)
        outputs_list.append(middle + gate_two * lowered)
        grad_out = cotangent[offset : offset + SEQ_MB].astype(jnp.float32)
        d_lowered = (gate_two * grad_out).astype(jnp.bfloat16)
        d_gate_two = jnp.sum(grad_out * lowered, axis=1)
        down_term = jnp.einsum(
            "srf,srd->fd", hidden_low, d_lowered, preferred_element_type=jnp.float32
        )
        d_hidden = jnp.einsum(
            "srd,fd->srf", d_lowered, down_full, preferred_element_type=jnp.float32
        )
        (d_raised,) = gelu_pull(d_hidden)
        d_raised_low = d_raised.astype(jnp.bfloat16)
        up_term = jnp.einsum(
            "srd,srf->df", second_in, d_raised_low, preferred_element_type=jnp.float32
        )
        d_second = jnp.einsum(
            "srf,df->srd", d_raised_low, up_full, preferred_element_type=jnp.float32
        )
        d_norm_two, gain_two_term, d_scale_two, d_shift_two = norm_back(
            d_second, normed_two, inv_two, gain_second, scale_two
        )
        d_middle = grad_out + d_norm_two
        d_gate_one = jnp.sum(d_middle * branch, axis=1)
        d_branch = (gate_one * d_middle).astype(jnp.bfloat16)
        out_term = jnp.einsum("srd,sre->de", attended, d_branch, preferred_element_type=jnp.float32)
        d_attended = jnp.einsum(
            "sre,de->srd", d_branch, out_full, preferred_element_type=jnp.float32
        ).astype(jnp.bfloat16)
        d_attn_rows = lax.all_to_all(d_attended, "ulysses", split_axis=2, concat_axis=1, tiled=True)
        d_attn_heads = d_attn_rows.reshape(SEQ_MB, query_rows, local_heads, HEAD_DIM).transpose(
            0, 2, 1, 3
        )
        delta = jnp.sum(d_attn_heads.astype(jnp.float32) * attn_heads, axis=-1)
        all_pairs = lax.all_gather(kv_local, "blk", axis=1, tiled=True)

        def back_step(d_query, block):
            keys, values = split_pairs(block)
            scores = (
                jnp.einsum("shqd,skhd->shqk", query_heads, keys, preferred_element_type=jnp.float32)
                * score_scale
            )
            probs = jnp.exp(scores - log_total[..., None])
            d_probs = jnp.einsum(
                "shqd,skhd->shqk", d_attn_heads, values, preferred_element_type=jnp.float32
            )
            d_scores = (probs * (d_probs - delta[..., None])).astype(jnp.bfloat16)
            d_query = (
                d_query
                + jnp.einsum("shqk,skhd->shqd", d_scores, keys, preferred_element_type=jnp.float32)
                * score_scale
            )
            d_keys = (
                jnp.einsum(
                    "shqk,shqd->skhd", d_scores, query_heads, preferred_element_type=jnp.float32
                )
                * score_scale
            )
            d_values = jnp.einsum(
                "shqk,shqd->skhd",
                probs.astype(jnp.bfloat16),
                d_attn_heads,
                preferred_element_type=jnp.float32,
            )
            key_rows = block.shape[1]
            pair = jnp.stack(
                [
                    d_keys.reshape(SEQ_MB, key_rows, head_width),
                    d_values.reshape(SEQ_MB, key_rows, head_width),
                ],
                axis=2,
            )
            return (d_query, pair)

        query_zero = jnp.zeros((SEQ_MB, local_heads, query_rows, HEAD_DIM), jnp.float32)
        d_query, pair_terms = lax.scan(back_step, query_zero, split_blocks(all_pairs, query_rows))
        pair_terms = jnp.moveaxis(pair_terms, 0, 1)
        pair_terms = pair_terms.reshape(
            SEQ_MB, pair_terms.shape[1] * pair_terms.shape[2], 2, head_width
        )
        pair_sums = lax.psum_scatter(pair_terms, "blk", scatter_dimension=1, tiled=True)
        query_grad = d_query.transpose(0, 2, 1, 3).reshape(SEQ_MB, query_rows, 1, head_width)
        d_packed = jnp.concatenate([query_grad, pair_sums], axis=2).astype(jnp.bfloat16)
        d_local = lax.all_to_all(d_packed, "ulysses", split_axis=1, concat_axis=3, tiled=True)
        d_local = d_local.astype(jnp.float32).reshape(SEQ_MB, rows, 3, HEADS, HEAD_DIM)
        d_projected = (
            jnp.stack(
                [
                    unrotate(d_local[:, :, 0], cos_table, sin_table),
                    unrotate(d_local[:, :, 1], cos_table, sin_table),
                    d_local[:, :, 2],
                ],
                axis=2,
            )
            .reshape(SEQ_MB, rows, 3 * width)
            .astype(jnp.bfloat16)
        )
        qkv_term = jnp.einsum(
            "srd,sre->de", first_in, d_projected, preferred_element_type=jnp.float32
        )
        d_first = jnp.einsum(
            "sre,de->srd", d_projected, qkv_full, preferred_element_type=jnp.float32
        )
        d_norm_one, gain_one_term, d_scale_one, d_shift_one = norm_back(
            d_first, normed_one, inv_one, gain_first, scale_one
        )
        input_grads.append(d_middle + d_norm_one)
        mod_local = jnp.concatenate(
            [d_shift_one, d_scale_one, d_gate_one, d_shift_two, d_scale_two, d_gate_two], axis=1
        )
        mod_total = lax.psum(mod_local, ("ulysses", "blk"))
        mod_low = mod_total.astype(jnp.bfloat16)
        cond_grads.append(
            jnp.einsum("sm,cm->sc", mod_low, ada_full, preferred_element_type=jnp.float32)
        )
        mod_part = lax.dynamic_slice_in_dim(mod_low, device_index * ada_cols, ada_cols, 1)
        ada_grad = ada_grad + jnp.einsum(
            "sc,sm->cm", cond_rows, mod_part, preferred_element_type=jnp.float32
        )
        terms = (qkv_term, out_term, up_term, down_term, gain_one_term, gain_two_term)
        reduced = (
            lax.psum_scatter(terms[0], ("ulysses", "blk"), scatter_dimension=0, tiled=True),
            lax.psum_scatter(terms[1], ("ulysses", "blk"), scatter_dimension=0, tiled=True),
            lax.psum_scatter(terms[2], ("ulysses", "blk"), scatter_dimension=0, tiled=True),
            lax.psum_scatter(terms[3], ("ulysses", "blk"), scatter_dimension=0, tiled=True),
            lax.psum_scatter(terms[4], ("ulysses", "blk"), scatter_dimension=0, tiled=True),
            lax.psum_scatter(terms[5], ("ulysses", "blk"), scatter_dimension=0, tiled=True),
        )
        grad_totals = tuple((a + b for a, b in zip(grad_totals, reduced)))
    output = jnp.concatenate(outputs_list, axis=0)
    inputs_grad = jnp.concatenate(input_grads, axis=0)
    conditioning_grad = jnp.concatenate(cond_grads, axis=0)
    return (
        output,
        inputs_grad,
        conditioning_grad,
        ada_grad,
        grad_totals[0],
        grad_totals[1],
        grad_totals[2],
        grad_totals[3],
        grad_totals[4],
        grad_totals[5],
    )


def dot_nt(left, right):
    return lax.dot_general(left, right, (((1,), (1,)), ((), ())), preferred_element_type=f32)


def dot_tn(left, right):
    return lax.dot_general(left, right, (((0,), (0,)), ((), ())), preferred_element_type=f32)


def row_norm(values):
    centered = values - jnp.mean(values, axis=1, keepdims=True)
    inv_std = lax.rsqrt(jnp.mean(centered * centered, axis=1, keepdims=True) + eps_norm)
    return centered * inv_std, inv_std


def row_back(grads, normed, inv_std):
    return inv_std * (
        grads
        - jnp.mean(grads, axis=1, keepdims=True)
        - normed * jnp.mean(grads * normed, axis=1, keepdims=True)
    )


def turn(values, cos_ref, sin_ref, sign):
    lane = lax.broadcasted_iota(jnp.int32, values.shape, 1) % HEAD_DIM
    swapped = jnp.where(
        lane < HEAD_DIM // 2, pltpu.roll(values, 128 - HEAD_DIM // 2, 1), pltpu.roll(values, HEAD_DIM // 2, 1)
    )
    return values * cos_ref[...] + sign * (swapped * sin_ref[...])


def mod_row(table_ref, s, i):
    width = table_ref.shape[1] // 7
    return table_ref[s : s + 1, i * width : (i + 1) * width]


EXTRA = 48


def split_low(values):
    high = values.astype(bf16).astype(f32)
    return high, values - high


def extra_rows(mods, gains, s_rows, store):
    for s in range(s_rows):
        for part, (mod, gain) in enumerate(zip(split_low(mods[s : s + 1]), split_low(gains[s : s + 1]))):
            at = (part * s_rows + s) * 4
            for i in range(3):
                store(at + i, mod[:, EXTRA * i : EXTRA * (i + 1)])
            store(at + 3, gain)


def pack_kernel(
    at_ref, x_ref, g_ref, qkv_ref, ada_ref, cond_ref, one_ref, two_ref, up_ref,
    xc_ref, chunk_ref, p0, p1, p2, p3, ext_ref,
):
    u = at_ref[0]
    n_all, block, cols = chunk_ref.shape
    xc_ref[0] = x_ref[...]
    xc_ref[1] = g_ref[...]
    width = qkv_ref.shape[1] // 3
    n_u = 4
    heads = width // n_u // HEAD_DIM
    ext_ref[...] = jnp.zeros_like(ext_ref)
    mods = DOT(cond_ref[...], ada_ref[...])
    gains = jnp.concatenate([one_ref[...], two_ref[...]], axis=0).astype(f32)

    def store(row, value):
        ext_ref[row : row + 1, : value.shape[1]] = value

    extra_rows(mods, gains, mods.shape[0], store)
    extra = ext_ref[...].astype(bf16)
    for i in range(n_u):
        pieces = []
        for h in range(heads):
            at = (i * heads + h) * HEAD_DIM
            pieces += [qkv_ref[:, at : at + HEAD_DIM], qkv_ref[:, width + at : width + at + HEAD_DIM]]
        at = 2 * width + i * heads * HEAD_DIM
        pieces += [qkv_ref[:, at : at + heads * HEAD_DIM], extra]
        whole = jnp.concatenate(pieces, axis=1)
        for j in range(n_all // n_u):
            chunk_ref[i * (n_all // n_u) + j] = whole
    cols = up_ref.shape[1] // n_u
    for i, out_ref in enumerate((p0, p1, p2, p3)):
        out_ref[...] = up_ref[:, pl.ds(pl.multiple_of((u ^ i) * cols, 128), cols)]


def first_kernel(at_ref, xg_ref, w_ref, cos_ref, sin_ref, chunk_ref, first_ref, table_ref):
    u = at_ref[0]
    n_u, _, seqs, rows, width = xg_ref.shape
    span = n_u * rows
    cols = w_ref.shape[1] - HEAD_DIM
    heads = cols // 192
    block = width // 32
    for s in range(seqs):
        mods, gains = [], []
        for d in range(32):
            at = d * block + s * 4
            pair = w_ref[d * block : (d + 1) * block, cols:].astype(f32)
            both = pair[s * 4 : s * 4 + 4] + pair[(seqs + s) * 4 : (seqs + s) * 4 + 4]
            mods += [both[i : i + 1, :EXTRA] for i in range(3)]
            gains.append(both[3:4, :block])
        table_ref[s : s + 1, :] = jnp.concatenate(mods + gains, axis=1)
    gain = mod_row(table_ref, 0, 6)
    zero = jnp.zeros(chunk_ref.shape[1:], bf16)
    chunk_ref[0] = zero
    chunk_ref[chunk_ref.shape[0] - 1] = zero
    for s in range(seqs):
        factor = gain * (1.0 + mod_row(table_ref, s, 1))
        for m in range(n_u):
            normed, _ = row_norm(xg_ref[u ^ m, 0, s].astype(f32))
            first = normed * factor + mod_row(table_ref, s, 0)
            first_ref[s * span + m * rows : s * span + (m + 1) * rows, :] = first.astype(bf16)
        projected = DOT(first_ref[s * span : (s + 1) * span, :], w_ref[:, :cols])
        for h in range(heads):
            pair = 1 + s * heads + h
            both = turn(projected[:, 128 * h : 128 * (h + 1)], cos_ref, sin_ref, 1.0)
            chunk_ref[pair, :span, :] = both.astype(bf16)
            v = projected[:, 128 * heads + 64 * h : 128 * heads + 64 * (h + 1)].astype(bf16)
            chunk_ref[pair, span:, :] = jnp.concatenate([v[: span // 2], v[span // 2 :]], axis=1)


def unpack_tokens(t_ref, s, h, heads):
    half = t_ref[1 + s * heads + h]
    return jnp.concatenate([half[:, :HEAD_DIM], half[:, HEAD_DIM:]], axis=0)


def store_parts(send_ref, keep_ref, part, s, rows):
    for m in range(4):
        block = part[m * rows : (m + 1) * rows]
        if m % 2:
            send_ref[m // 2, s] = block.astype(bf16)
        else:
            keep_ref[m // 2, s] = block


def out_kernel(
    at_ref, t_ref, a0, a1, a2, a3, a4, a5, a6, a7, att_ref, send_ref, keep_ref, w_ref, wide_ref,
):
    _, seqs, rows, _ = send_ref.shape
    block = a0.shape[0]
    for i, part_ref in enumerate((a0, a1, a2, a3, a4, a5, a6, a7)):
        start = pl.multiple_of((at_ref[1] ^ i) * block, 8)
        wide_ref[pl.ds(start, block), :] = part_ref[...].astype(f32)
    w_ref[...] = wide_ref[...].astype(bf16)
    heads = w_ref.shape[0] // HEAD_DIM
    span = 4 * rows
    for s in range(seqs):
        att = jnp.concatenate([unpack_tokens(t_ref, s, h, heads) for h in range(heads)], axis=1)
        att_ref[s * span : (s + 1) * span, :] = att
        store_parts(send_ref, keep_ref, DOT(att, w_ref[...]), s, rows)


def block_of(own_ref, got_ref, m, s):
    return (got_ref if m % 2 else own_ref)[m // 2, s].astype(f32)


def middle_of(xg_ref, own_ref, got_ref, table_ref, u, m, s):
    return xg_ref[u ^ m, 0, s].astype(f32) + mod_row(table_ref, s, 2) * block_of(own_ref, got_ref, m, s)


def ff_kernel(
    at_ref, xg_ref, own_ref, got_ref, table_ref, a0, a1, a2, a3, a4, a5, a6, a7,
    lsend_ref, lkeep_ref, dsend_ref, dkeep_ref, sums_ref, ukeep_ref, usend_ref, wkeep_ref, wsend_ref,
    second_ref, hidden_ref, low_ref, raised_ref, normed_ref, wide_ref, up_ref, down_ref,
):
    u = at_ref[0]
    n_u, _, seqs, rows, width = xg_ref.shape
    span = n_u * rows
    gain = mod_row(table_ref, 1, 6)
    scale = math.sqrt(2.0 / math.pi)
    block = width // 32
    low = n_u * block
    u, b = at_ref[0], at_ref[1]
    for i, part_ref in enumerate((a0, a1, a2, a3, a4, a5, a6, a7)):
        there = b ^ i
        down_ref[pl.ds(pl.multiple_of(there * low, 32), low), :] = part_ref[low:, :]
        for j in range(n_u):
            start = pl.multiple_of(((u ^ j) * 8 + there) * block, 8)
            wide_ref[pl.ds(start, block), :] = part_ref[j * block : (j + 1) * block, :].astype(f32)
    up_ref[...] = wide_ref[...].astype(bf16)
    for s in range(seqs):
        at = slice(s * span, (s + 1) * span)
        factor = gain * (1.0 + mod_row(table_ref, s, 4))
        gate = mod_row(table_ref, s, 5)
        for m in range(n_u):
            here = slice(s * span + m * rows, s * span + (m + 1) * rows)
            normed, _ = row_norm(middle_of(xg_ref, own_ref, got_ref, table_ref, u, m, s))
            normed_ref[m * rows : (m + 1) * rows, :] = normed
            second_ref[here, :] = (normed * factor + mod_row(table_ref, s, 3)).astype(bf16)
            low_ref[here, :] = (gate * xg_ref[u ^ m, 1, s].astype(f32)).astype(bf16)
        raised = DOT(second_ref[at, :], up_ref[...])
        d_hidden = dot_nt(low_ref[at, :], down_ref[...])
        square = raised * raised
        t = jnp.tanh(scale * raised * (1.0 + 0.044715 * square))
        hidden_ref[at, :] = (0.5 * raised * (1.0 + t)).astype(bf16)
        slope = 0.5 * (1.0 + t) + 0.5 * raised * (1.0 - t * t) * (scale * (1.0 + 3.0 * 0.044715 * square))
        raised_ref[at, :] = (d_hidden * slope).astype(bf16)
        d_second = dot_nt(raised_ref[at, :], up_ref[...])
        store_parts(dsend_ref, dkeep_ref, d_second, s, rows)
        lowered = DOT(hidden_ref[at, :], down_ref[...])
        store_parts(lsend_ref, lkeep_ref, lowered, s, rows)
        sums_ref[s, 0:1, :] = jnp.sum(d_second, axis=0, keepdims=True)
        sums_ref[s, 1:2, :] = jnp.sum(d_second * normed_ref[...], axis=0, keepdims=True)
        gated = jnp.zeros((1, width), f32)
        for m in range(n_u):
            grad = xg_ref[u ^ m, 1, s].astype(f32)
            gated = gated + jnp.sum(grad * lowered[m * rows : (m + 1) * rows], axis=0, keepdims=True)
        sums_ref[s, 2:3, :] = gated
    n_z = ukeep_ref.shape[0]
    wide_ref[...] = dot_tn(second_ref[...], raised_ref[...])
    for y, out_ref in enumerate((ukeep_ref, usend_ref)):
        for z in range(n_z):
            for i in range(n_u):
                start = pl.multiple_of(((u ^ i) * 2 * n_z + (b ^ (2 * z + y))) * block, 8)
                out_ref[z, i] = wide_ref[pl.ds(start, block), :].astype(bf16)
    wide_ref[...] = dot_tn(hidden_ref[...], low_ref[...])
    for y, out_ref in enumerate((wkeep_ref, wsend_ref)):
        for z in range(n_z):
            for i in range(n_u):
                start = pl.multiple_of(((b ^ (2 * z + y)) * n_u + i) * block, 8)
                out_ref[z, i] = wide_ref[pl.ds(start, block), :].astype(bf16)


def middle_back_kernel(
    at_ref, xg_ref, own_ref, got_ref, down_ref, dgot_ref, table_ref, w_ref, att_ref,
    chunk_ref, dmid_ref, gate_ref, okeep_ref, osend_ref, branch_ref, outs_ref,
):
    u = at_ref[0]
    n_u, _, seqs, rows, width = xg_ref.shape
    span = n_u * rows
    heads = w_ref.shape[0] // HEAD_DIM
    gain = mod_row(table_ref, 1, 6)
    zero = jnp.zeros(chunk_ref.shape[1:], bf16)
    chunk_ref[0] = zero
    chunk_ref[chunk_ref.shape[0] - 1] = zero
    for s in range(seqs):
        at = slice(s * span, (s + 1) * span)
        factor = gain * (1.0 + mod_row(table_ref, s, 4))
        gate = mod_row(table_ref, s, 2)
        for m in range(n_u):
            normed, inv_std = row_norm(middle_of(xg_ref, own_ref, got_ref, table_ref, u, m, s))
            grads = block_of(down_ref, dgot_ref, m, s) * factor
            d_middle = xg_ref[u ^ m, 1, s].astype(f32) + row_back(grads, normed, inv_std)
            branch_ref[s * span + m * rows : s * span + (m + 1) * rows, :] = (gate * d_middle).astype(bf16)
            if m == 0:
                dmid_ref[s] = d_middle
                gate_ref[s] = jnp.sum(d_middle * own_ref[0, s].astype(f32), axis=0, keepdims=True)
        d_att = dot_nt(branch_ref[at, :], w_ref[...]).astype(bf16)
        for h in range(heads):
            d = d_att[:, HEAD_DIM * h : HEAD_DIM * (h + 1)]
            chunk_ref[1 + s * heads + h] = jnp.concatenate([d[: span // 2], d[span // 2 :]], axis=1)
    n_z, block, _ = okeep_ref.shape
    outs_ref[...] = dot_tn(att_ref[...], branch_ref[...])
    for y, out_ref in enumerate((okeep_ref, osend_ref)):
        for z in range(n_z):
            start = pl.multiple_of((at_ref[1] ^ (2 * z + y)) * block, 8)
            out_ref[z] = outs_ref[pl.ds(start, block), :].astype(bf16)


def first_back_kernel(
    at_ref, t_ref, xg_ref, table_ref, cos_ref, sin_ref, w_ref, first_ref, gate_ref, two_ref,
    send_ref, keep_ref, blocks_ref, proj_ref, normed_ref, sums_ref, ext_ref,
):
    u = at_ref[0]
    n_u, _, seqs, rows, width = xg_ref.shape
    span = n_u * rows
    cols = w_ref.shape[1] - HEAD_DIM
    heads = cols // 192
    gain_grads = [jnp.zeros((1, width), f32)] * 2
    total, block, _ = blocks_ref.shape
    for s in range(seqs):
        at = slice(s * span, (s + 1) * span)
        for h in range(heads):
            pair = t_ref[1 + s * heads + h]
            both = turn(pair[:span].astype(f32), cos_ref, sin_ref, -1.0)
            proj_ref[at, 128 * h : 128 * (h + 1)] = both.astype(bf16)
            v = pair[span:]
            proj_ref[at, 128 * heads + 64 * h : 128 * heads + 64 * (h + 1)] = jnp.concatenate(
                [v[:, :HEAD_DIM], v[:, HEAD_DIM:]], axis=0
            )
        d_first = dot_nt(proj_ref[at, :], w_ref[:, :cols])
        store_parts(send_ref, keep_ref, d_first, s, rows)
        for m in range(n_u):
            normed, _ = row_norm(xg_ref[u ^ m, 0, s].astype(f32))
            normed_ref[m * rows : (m + 1) * rows, :] = normed
        dots = [jnp.sum(d_first * normed_ref[...], axis=0, keepdims=True), two_ref[s, 1:2, :]]
        for i in range(2):
            gain_grads[i] = gain_grads[i] + dots[i] * (1.0 + mod_row(table_ref, s, 1 + 3 * i))
        rows_out = [
            jnp.sum(d_first, axis=0, keepdims=True),
            dots[0] * mod_row(table_ref, 0, 6),
            gate_ref[s],
            two_ref[s, 0:1, :],
            dots[1] * mod_row(table_ref, 1, 6),
            two_ref[s, 2:3, :],
        ]
        for i, row in enumerate(rows_out):
            sums_ref[s : s + 1, i * width : (i + 1) * width] = row
    for i in range(2):
        sums_ref[i : i + 1, 6 * width :] = gain_grads[i]
    ext_ref[...] = jnp.zeros_like(ext_ref)
    for d in range(total):

        def store(row, value):
            ext_ref[d * block + row : d * block + row + 1, : value.shape[1]] = value

        mods = sums_ref[:, 3 * EXTRA * d : 3 * EXTRA * (d + 1)]
        extra_rows(mods, sums_ref[:, 6 * width + block * d : 6 * width + block * (d + 1)], seqs, store)
    grads = dot_tn(first_ref[...], proj_ref[...])
    for i in range(total):
        at = slice(i * block, (i + 1) * block)
        blocks_ref[i, :, :cols] = grads[at].astype(bf16)
        blocks_ref[i, :, cols:] = ext_ref[at].astype(bf16)


def row_grad_kernel(at_ref, raw_ref, p0, p1, p2, p3, ada_ref, cond_ref, qkv_ref, up_ref, part_ref, adag_ref, gain_ref, mod_ref):
    u = at_ref[0]
    total, block, cols = raw_ref.shape
    cols = cols - HEAD_DIM
    n_u = 4
    n_b = total // n_u
    heads = cols // 192
    width = qkv_ref.shape[1] // 3
    seqs = mod_ref.shape[0]
    extra = jnp.zeros((block, HEAD_DIM), f32)
    for i in range(n_u):
        part = raw_ref[i * n_b].astype(f32)
        for j in range(1, n_b):
            part = part + raw_ref[i * n_b + j].astype(f32)
        extra = extra + part[:, cols:]
        for h in range(heads):
            to = (i * heads + h) * HEAD_DIM
            qkv_ref[:, to : to + HEAD_DIM] = part[:, 128 * h : 128 * h + HEAD_DIM]
            qkv_ref[:, width + to : width + to + HEAD_DIM] = part[:, 128 * h + HEAD_DIM : 128 * (h + 1)]
        at = i * heads * HEAD_DIM
        qkv_ref[:, 2 * width + at : 2 * width + at + heads * HEAD_DIM] = part[:, 128 * heads : cols]
    for s in range(seqs):
        both = extra[s * 4 : s * 4 + 4] + extra[(seqs + s) * 4 : (seqs + s) * 4 + 4]
        mod_ref[s : s + 1, :] = jnp.concatenate([both[i : i + 1, :EXTRA] for i in range(3)], axis=1)
        gain_ref[s : s + 1, :] = both[3:4, :block]
    mods = mod_ref[...].astype(bf16)
    grads = dot_nt(mods, ada_ref[...])
    for i in range(total):
        part_ref[i] = grads
    adag_ref[...] = dot_tn(cond_ref[...], mods)
    cols = up_ref.shape[1] // n_u
    for i, piece_ref in enumerate((p0, p1, p2, p3)):
        up_ref[:, pl.ds(pl.multiple_of((u ^ i) * cols, 128), cols)] = piece_ref[...]


def input_grad_kernel(x_ref, near_ref, got_ref, dmid_ref, table_ref, out_ref):
    seqs = x_ref.shape[0]
    for s in range(seqs):
        factor = mod_row(table_ref, 0, 6) * (1.0 + mod_row(table_ref, s, 1))
        normed, inv_std = row_norm(x_ref[s].astype(f32))
        grads = (near_ref[s] + got_ref[s].astype(f32)) * factor
        out_ref[s] = dmid_ref[s] + row_back(grads, normed, inv_std)


def call(kernel, name, outs, scratch, flops, *args, limit=16, staged=()):
    count = len(args)
    specs = [
        pl.BlockSpec(
            memory_space=pltpu.SMEM if a.dtype == jnp.int32 else pltpu.HBM if i in staged else pltpu.VMEM
        )
        for i, a in enumerate(args)
    ]
    size = sum(math.prod(a.shape) * a.dtype.itemsize for a in args)
    size += sum(math.prod(shape) * jnp.dtype(dtype).itemsize for shape, dtype in outs)
    shapes = [pltpu.VMEM(*s) for s in scratch]
    body = kernel
    if staged:
        shapes = [pltpu.VMEM(args[i].shape, args[i].dtype) for i in staged] + [
            pltpu.SemaphoreType.DMA((len(staged),))
        ] + shapes

        def body(*refs):
            ins, rest = list(refs[:count]), refs[count:]
            out_refs, held = rest[: len(outs)], rest[len(outs) :]
            sems = held[len(staged)]
            copies = []
            for j, i in enumerate(staged):
                copies.append(pltpu.make_async_copy(ins[i], held[j], sems.at[j]))
                ins[i] = held[j]
            for copy in copies:
                copy.start()
            for copy in copies:
                copy.wait()
            kernel(*ins, *out_refs, *held[len(staged) + 1 :])

    return pl.pallas_call(
        body,
        out_shape=tuple(jax.ShapeDtypeStruct(shape, dtype) for shape, dtype in outs),
        in_specs=specs,
        out_specs=tuple(pl.BlockSpec(memory_space=pltpu.VMEM) for _ in outs),
        scratch_shapes=shapes,
        cost_estimate=pl.CostEstimate(flops=int(flops), bytes_accessed=int(size), transcendentals=0),
        compiler_params=pltpu.CompilerParams(vmem_limit_bytes=limit << 20),
        name=name,
    )(*args)


def fits_tp(mesh):
    ulysses, blk = mesh.shape["ulysses"], mesh.shape["blk"]
    return ulysses == 4 and blk == 8 and HEADS % ulysses == 0


def swap_u(values, mask):
    return lax.ppermute(values, "ulysses", [(i, i ^ mask) for i in range(4)])


def swap_b(values, mask):
    return lax.ppermute(values, "blk", [(i, i ^ mask) for i in range(8)])


def exchange(blocks, axis):
    return lax.all_to_all(blocks, axis, split_axis=0, concat_axis=0, tiled=True)


def half_sum(send, keep):
    return keep + swap_u(send, 1).astype(f32)


def along_z(values):
    return [values] + [swap_b(values, 2 * m) for m in (1, 2, 3)]


def along_y(parts):
    out = []
    for part in parts:
        out += [part, swap_b(part, 1)]
    return out


def sum_z(half):
    total = half[0]
    for m in (1, 2, 3):
        total = total + swap_b(half[m].astype(bf16), 2 * m).astype(f32)
    return total


def tp_shards(inputs, conditioning, w_ada, w_qkv, w_out, w_up, w_down, gain_one, gain_two, cotangent):
    n_u, n_b = 4, 8
    n_all = n_u * n_b
    everywhere = ("ulysses", "blk")
    seqs, rows, width = inputs.shape
    u = lax.axis_index("ulysses")
    b = lax.axis_index("blk")
    at = jnp.stack([u, b]).astype(jnp.int32)
    heads = HEADS // n_u
    head_width = heads * HEAD_DIM
    cols = 3 * head_width
    w_rows, down_rows = w_qkv.shape[0], w_down.shape[0]
    ff_local = w_up.shape[1] // n_u
    span = n_u * rows
    tokens = seqs * span

    packed = call(
        pack_kernel, "pack",
        [((2,) + inputs.shape, bf16), ((n_all, w_rows, cols + HEAD_DIM), bf16)] + [((w_rows, ff_local), bf16)] * n_u,
        [((w_rows, HEAD_DIM), f32)], 0,
        at, inputs, cotangent, w_qkv, w_ada, conditioning, gain_one[None], gain_two[None], w_up,
        limit=60,
    )
    ff_near = jnp.concatenate([packed[2]] + [swap_u(packed[2 + m], m) for m in (1, 2, 3)] + [w_down], axis=0)
    raw = exchange(packed[1], everywhere)
    xg = lax.all_gather(packed[0], "ulysses", axis=0, tiled=False)
    out_zy = along_y(along_z(w_out))
    raw, xg, ff_near, out_zy = lax.optimization_barrier((raw, xg, ff_near, out_zy))
    w_qkv_u = raw.reshape(width, cols + HEAD_DIM)

    blocks = u ^ jnp.arange(n_u, dtype=jnp.int32)
    positions = ((blocks * n_b + b) * rows)[:, None] + jnp.arange(rows, dtype=jnp.int32)[None, :]
    cos_table, sin_table = rotary_tables(positions.reshape(-1).astype(f32))
    cos_table, sin_table = cos_table[:, 0], sin_table[:, 0]
    cos_table = jnp.concatenate([cos_table] * 4, axis=1)
    sin_table = jnp.concatenate([-sin_table, sin_table] * 2, axis=1)

    chunks, first_in, table = call(
        first_kernel, "first",
        [((n_b, 3 * span // 2, 128), bf16), ((tokens, width), bf16), ((seqs, 7 * width), f32)], [],
        2 * tokens * width * cols,
        at, xg, w_qkv_u, cos_table, sin_table,
    )
    owned = exchange(chunks, "blk")
    owned, ff_near = lax.optimization_barrier((owned, ff_near))
    ff_0y, ff_2 = swap_b(ff_near, 1), swap_b(ff_near, 4)
    attn_low, attn_full, log_total = attn_fwd(owned)
    part_shape = (2, seqs, rows, width)
    attn_low, ff_0y, ff_2, ff_near = lax.optimization_barrier((attn_low, ff_0y, ff_2, ff_near))
    attn_tokens = exchange(attn_low, "blk")
    ff_1, ff_3, ff_2y = swap_b(ff_near, 2), swap_b(ff_near, 6), swap_b(ff_2, 1)
    attn_tokens, ff_1, ff_3, ff_2y = lax.optimization_barrier((attn_tokens, ff_1, ff_3, ff_2y))
    attended, send, keep, w_out_u = call(
        out_kernel, "out",
        [((tokens, head_width), bf16), (part_shape, bf16), (part_shape, f32), ((head_width, width), bf16)],
        [((head_width, width), f32)],
        2 * tokens * width * head_width,
        at, attn_tokens, *out_zy,
    )

    half = half_sum(send, keep)
    across = swap_u(half.astype(bf16), 2)
    ff_zy = [ff_near, ff_0y, ff_1, swap_b(ff_1, 1), ff_2, ff_2y, ff_3, swap_b(ff_3, 1)]
    across, ff_zy = lax.optimization_barrier((across, ff_zy))
    own = (half + across[::-1].astype(f32)).astype(bf16)
    got = swap_u(own, 1)
    lsend, lkeep, dsend, dkeep, sums_two, up_keep, up_send, down_keep, down_send = call(
        ff_kernel, "ff",
        [(part_shape, bf16), (part_shape, f32), (part_shape, bf16), (part_shape, f32), ((seqs, 3, width), f32)]
        + [((n_b // 2, n_u, w_rows, width), bf16)] * 4,
        [((tokens, width), bf16), ((tokens, ff_local), bf16), ((tokens, width), bf16), ((tokens, ff_local), bf16),
         ((span, width), f32), ((width, ff_local), f32), ((width, ff_local), bf16), ((ff_local, width), bf16)],
        12 * tokens * width * ff_local,
        at, xg, own, got, table, *ff_zy,
        limit=28,
    )
    up_other, down_other = swap_b(up_send, 1), swap_b(down_send, 1)
    half = half_sum(dsend, dkeep)
    across = swap_u(half.astype(bf16), 2)
    d_own = (half + across[::-1].astype(f32)).astype(bf16)
    d_got = swap_u(d_own, 1)
    d_chunks, d_middle, sum_gate, out_keep, out_send = call(
        middle_back_kernel, "middle_back",
        [((n_b, span // 2, 128), bf16), ((seqs, rows, width), f32), ((seqs, 1, width), f32)]
        + [((n_b // 2, w_rows, width), bf16)] * 2,
        [((tokens, width), bf16), ((head_width, width), f32)],
        4 * tokens * width * head_width,
        at, xg, own, got, d_own, d_got, table, w_out_u, attended,
        limit=60,
    )
    d_chunks, up_other = lax.optimization_barrier((d_chunks, up_other))
    d_attn = exchange(d_chunks, "blk")
    up_sum = sum_z(up_keep.astype(f32) + up_other.astype(f32))
    out_other = swap_b(out_send, 1)
    d_attn, up_sum, down_other, out_other = lax.optimization_barrier((d_attn, up_sum, down_other, out_other))
    down_sum = sum_z(
        jnp.concatenate(
            [down_keep.astype(f32) + down_other.astype(f32), (out_keep.astype(f32) + out_other.astype(f32))[:, None]],
            axis=1,
        )
    )
    d_owned = attn_bwd(owned, d_attn, attn_full, log_total)
    lhalf = half_sum(lsend, lkeep)
    lowered = lhalf[0] + swap_u(lhalf[1].astype(bf16), 2).astype(f32)
    gates = table.reshape(2, 7, 1, width)
    output = inputs.astype(f32) + gates[:, 2] * own[0].astype(f32) + gates[:, 5] * lowered
    d_owned, output, down_sum = lax.optimization_barrier((d_owned, output, down_sum))
    up_parts = [up_sum[0]] + [swap_u(up_sum[m], m) for m in (1, 2, 3)]
    d_tokens = exchange(d_owned, "blk")
    d_tokens, up_parts = lax.optimization_barrier((d_tokens, up_parts))

    send, keep, qkv_blocks = call(
        first_back_kernel, "first_back",
        [(part_shape, bf16), (part_shape, f32), ((n_all, w_rows, cols + HEAD_DIM), bf16)],
        [((tokens, cols), bf16), ((span, width), f32), ((seqs, 7 * width), f32), ((width, HEAD_DIM), f32)],
        4 * tokens * width * cols,
        at, d_tokens, xg, table, cos_table, sin_table, w_qkv_u, first_in, sum_gate, sums_two,
        limit=60,
    )
    half = half_sum(send, keep)
    far = swap_u(half[1].astype(bf16), 2)
    inputs_grad, = call(
        input_grad_kernel, "input_grad",
        [((seqs, rows, width), f32)], [], 0,
        inputs, half[0], far, d_middle, table,
    )
    qkv_grad, up_grad, cond_part, ada_grad, gain_grads, _ = call(
        row_grad_kernel, "row_grad",
        [(w_qkv.shape, f32), (w_up.shape, f32), ((n_all,) + conditioning.shape, f32), (w_ada.shape, f32),
         ((2, w_rows), f32), ((seqs, w_ada.shape[1]), f32)],
        [], 0,
        at, exchange(qkv_blocks, everywhere), *up_parts, w_ada, conditioning,
        limit=60,
    )
    conditioning_grad = jnp.sum(exchange(cond_part, everywhere), axis=0)
    return (
        output,
        inputs_grad,
        conditioning_grad,
        ada_grad,
        qkv_grad,
        down_sum[n_u],
        up_grad,
        down_sum[:n_u].reshape(w_down.shape),
        gain_grads[0],
        gain_grads[1],
    )


def solution(mesh):
    body = tp_shards if fits_tp(mesh) else shards
    in_specs = (
        P(None, ("ulysses", "blk"), None),
        P(),
        P(None, ("ulysses", "blk")),
        P(("ulysses", "blk"), None),
        P(("ulysses", "blk"), None),
        P(("ulysses", "blk"), None),
        P(("ulysses", "blk"), None),
        P(("ulysses", "blk")),
        P(("ulysses", "blk")),
        P(None, ("ulysses", "blk"), None),
    )
    out_specs = (
        P(None, ("ulysses", "blk"), None),
        P(None, ("ulysses", "blk"), None),
        P(),
        P(None, ("ulysses", "blk")),
        P(("ulysses", "blk"), None),
        P(("ulysses", "blk"), None),
        P(("ulysses", "blk"), None),
        P(("ulysses", "blk"), None),
        P(("ulysses", "blk")),
        P(("ulysses", "blk")),
    )
    return jax.shard_map(body, mesh=mesh, in_specs=in_specs, out_specs=out_specs, check_vma=False)
```

```python
import functools
import math

import jax
import jax.numpy as jnp
from jax import lax
from jax.experimental import pallas as pl
from jax.experimental.pallas import tpu as pltpu
from jax.sharding import PartitionSpec as P

f32, bf16 = jnp.float32, jnp.bfloat16
DOT = functools.partial(jnp.dot, preferred_element_type=f32)

def attn_fwd_kernel(x_ref, o_ref, of_ref, lse_ref, kt_ref, v_ref):
    nb, rows3, _ = x_ref.shape
    half = rows3 // 3
    rows = 2 * half
    for j in range(nb):
        kt_ref[:, j * rows : (j + 1) * rows] = x_ref[j, :rows, 64:].T
        v_ref[j * rows : j * rows + half, :] = x_ref[j, rows:, :64]
        v_ref[j * rows + half : (j + 1) * rows, :] = x_ref[j, rows:, 64:]

    def step(j, _):
        q = x_ref[j, :rows, :64] * jnp.asarray(0.125, bf16)
        s = DOT(q, kt_ref[...])
        top = jnp.max(s, axis=1, keepdims=True)
        p = jnp.exp(s - top)
        total = jnp.sum(p, axis=1, keepdims=True)
        o = DOT(p.astype(bf16), v_ref[...]) / total
        packed = jnp.concatenate([o[:half], o[half:]], axis=1)
        of_ref[j] = packed
        o_ref[j] = packed.astype(bf16)
        lse = jnp.broadcast_to(top + jnp.log(total), (rows, 128)).T
        lse_ref[j] = lse[:8]
        return 0
    lax.fori_loop(0, nb, step, 0, unroll=2)

def attn_fwd(x):
    nb, rows3, _ = x.shape
    half = rows3 // 3
    n = nb * half * 2
    return pl.pallas_call(
        attn_fwd_kernel,
        out_shape=(jax.ShapeDtypeStruct((nb, half, 128), bf16), jax.ShapeDtypeStruct((nb, half, 128), f32),
                   jax.ShapeDtypeStruct((nb, 8, 2 * half), f32)),
        scratch_shapes=[pltpu.VMEM((64, n), bf16), pltpu.VMEM((n, 64), bf16)],
        cost_estimate=pl.CostEstimate(flops=4 * n * n * 64, bytes_accessed=n * 64 * 2 * 8, transcendentals=n * n),
        compiler_params=pltpu.CompilerParams(vmem_limit_bytes=32 << 20),
        name="attn_fwd",
    )(x)

def attn_bwd_kernel(x_ref, d_ref, of_ref, lse_ref, g_ref, qt_ref, dt_ref, q_ref, dd_ref, lse_s, del_s, dqt_ref):
    nb, rows3, _ = x_ref.shape
    half = rows3 // 3
    rows = 2 * half
    for j in range(nb):
        sl = slice(j * rows, (j + 1) * rows)
        q = x_ref[j, :rows, :64] * jnp.asarray(0.125, bf16)
        q_ref[sl, :] = q
        qt_ref[:, sl] = q.T
        d = jnp.concatenate([d_ref[j, :, :64], d_ref[j, :, 64:]], axis=0)
        dd_ref[sl, :] = d
        dt_ref[:, sl] = d.T
        o = jnp.concatenate([of_ref[j, :, :64], of_ref[j, :, 64:]], axis=0)
        delta = jnp.sum(d.astype(f32) * o, axis=1, keepdims=True)
        del_s[:, sl] = jnp.broadcast_to(delta, (rows, 128)).T[:8]
        lse_s[:, sl] = lse_ref[j]
    dqt_ref[...] = jnp.zeros_like(dqt_ref)

    def step(j, _):
        k = x_ref[j, :rows, 64:]
        v = jnp.concatenate([x_ref[j, rows:, :64], x_ref[j, rows:, 64:]], axis=0)
        s = DOT(k, qt_ref[...])
        p = jnp.exp(s - lse_s[0:1, :])
        dp = DOT(v, dt_ref[...])
        ds = (p * (dp - del_s[0:1, :])).astype(bf16)
        dv = DOT(p.astype(bf16), dd_ref[...])
        dk = DOT(ds, q_ref[...])
        dqt_ref[...] += DOT(k.T, ds)
        g_ref[j, :rows, 64:] = dk.astype(bf16)
        g_ref[j, rows:, :] = jnp.concatenate([dv[:half], dv[half:]], axis=1).astype(bf16)
        return 0
    lax.fori_loop(0, nb, step, 0, unroll=2)
    for j in range(nb):
        g_ref[j, :rows, :64] = (dqt_ref[:, j * rows : (j + 1) * rows].T * 0.125).astype(bf16)

def attn_bwd(x, d, of, lse):
    nb, rows3, _ = x.shape
    half = rows3 // 3
    n = nb * half * 2
    return pl.pallas_call(
        attn_bwd_kernel,
        out_shape=jax.ShapeDtypeStruct((nb, rows3, 128), bf16),
        scratch_shapes=[pltpu.VMEM((64, n), bf16), pltpu.VMEM((64, n), bf16), pltpu.VMEM((n, 64), bf16), pltpu.VMEM((n, 64), bf16),
                        pltpu.VMEM((8, n), f32), pltpu.VMEM((8, n), f32), pltpu.VMEM((64, n), f32)],
        cost_estimate=pl.CostEstimate(flops=n * n * 64, bytes_accessed=n * 64 * 2, transcendentals=0),
        compiler_params=pltpu.CompilerParams(vmem_limit_bytes=32 << 20),
        name="attn_bwd",
    )(x, d, of, lse)

HEADS = 12
HEAD_DIM = 64
SEQ_MB = 1
MICRO = 2


eps_norm = 1e-06
shard_group = 4


def normalize(values):
    average = jnp.mean(values, axis=-1, keepdims=True)
    centered = values - average
    variance = jnp.mean(centered * centered, axis=-1, keepdims=True)
    inv_std = lax.rsqrt(variance + eps_norm)
    return (centered * inv_std, inv_std)


def norm_back(grad_out, normed, inv_std, gain, scale_mod):
    factor = 1.0 + scale_mod
    d_normed = grad_out * gain * factor
    gain_term = jnp.sum(grad_out * normed * factor, axis=(0, 1))
    scale_term = jnp.sum(grad_out * normed * gain, axis=1)
    shift_term = jnp.sum(grad_out, axis=1)
    centred = d_normed - jnp.mean(d_normed, axis=-1, keepdims=True)
    d_inputs = inv_std * (centred - normed * jnp.mean(d_normed * normed, axis=-1, keepdims=True))
    return (d_inputs, gain_term, scale_term, shift_term)


def rotary_tables(positions):
    half_dim = HEAD_DIM // 2
    frequency = jnp.exp(
        -jnp.log(10000.0) * jnp.arange(half_dim, dtype=jnp.float32) * 2.0 / HEAD_DIM
    )
    angles = positions[:, None] * frequency[None, :]
    return (jnp.cos(angles)[:, None, :], jnp.sin(angles)[:, None, :])


def rotate(values, cos_table, sin_table):
    half_dim = values.shape[-1] // 2
    first_half = values[..., :half_dim]
    second_half = values[..., half_dim:]
    return jnp.concatenate(
        [
            first_half * cos_table - second_half * sin_table,
            second_half * cos_table + first_half * sin_table,
        ],
        axis=-1,
    )


def unrotate(grads, cos_table, sin_table):
    half_dim = grads.shape[-1] // 2
    first_half = grads[..., :half_dim]
    second_half = grads[..., half_dim:]
    return jnp.concatenate(
        [
            first_half * cos_table + second_half * sin_table,
            second_half * cos_table - first_half * sin_table,
        ],
        axis=-1,
    )


def gelu_tanh(values):
    return jax.nn.gelu(values, approximate=True)


def split_pairs(block):
    batch_seqs = block.shape[0]
    key_rows = block.shape[1]
    heads_here = block.shape[3] // HEAD_DIM
    keys = block[:, :, 0].reshape(batch_seqs, key_rows, heads_here, HEAD_DIM)
    values = block[:, :, 1].reshape(batch_seqs, key_rows, heads_here, HEAD_DIM)
    return (keys, values)


def split_blocks(piece, shard_rows):
    count = piece.shape[1] // shard_rows
    group = math.gcd(count, shard_group)
    steps = count // group
    shaped = piece.reshape((piece.shape[0], steps, group * shard_rows) + piece.shape[2:])
    return jnp.moveaxis(shaped, 1, 0)


def forward_block(query_heads, carry, block):
    top, totals, accum = carry
    keys, values = split_pairs(block)
    scores = jnp.einsum(
        "shqd,skhd->shqk", query_heads, keys, preferred_element_type=jnp.float32
    ) * HEAD_DIM ** (-0.5)
    new_top = jnp.maximum(top, jnp.max(scores, axis=-1))
    probs = jnp.exp(scores - new_top[..., None])
    fade = jnp.exp(top - new_top)
    totals = totals * fade + jnp.sum(probs, axis=-1)
    accum = accum * fade[..., None] + jnp.einsum(
        "shqk,skhd->shqd", probs.astype(jnp.bfloat16), values, preferred_element_type=jnp.float32
    )
    return (new_top, totals, accum)


def shards(inputs, conditioning, w_ada, w_qkv, w_out, w_up, w_down, gain_one, gain_two, cotangent):
    gathered = (
        lax.all_gather(w_ada, ("ulysses", "blk"), axis=1, tiled=True),
        lax.all_gather(w_qkv, ("ulysses", "blk"), axis=0, tiled=True),
        lax.all_gather(w_out, ("ulysses", "blk"), axis=0, tiled=True),
        lax.all_gather(w_up, ("ulysses", "blk"), axis=0, tiled=True),
        lax.all_gather(w_down, ("ulysses", "blk"), axis=0, tiled=True),
        lax.all_gather(gain_one, ("ulysses", "blk"), axis=0, tiled=True),
        lax.all_gather(gain_two, ("ulysses", "blk"), axis=0, tiled=True),
    )
    ada_full, qkv_full, out_full, up_full, down_full = (
        gathered[0],
        gathered[1],
        gathered[2],
        gathered[3],
        gathered[4],
    )
    gain_first = gathered[5].astype(jnp.float32)
    gain_second = gathered[6].astype(jnp.float32)
    rows = inputs.shape[1]
    width = inputs.shape[2]
    device_index = lax.axis_index(("ulysses", "blk"))
    positions = (device_index * rows + jnp.arange(rows, dtype=jnp.int32)).astype(jnp.float32)
    cos_table, sin_table = rotary_tables(positions)
    score_scale = HEAD_DIM ** (-0.5)
    ada_cols = w_ada.shape[1]
    grad_shapes = (
        w_qkv.shape,
        w_out.shape,
        w_up.shape,
        w_down.shape,
        gain_one.shape,
        gain_two.shape,
    )
    grad_totals = tuple((jnp.zeros(shape, jnp.float32) for shape in grad_shapes))
    ada_grad = jnp.zeros(w_ada.shape, jnp.float32)
    outputs_list = []
    input_grads = []
    cond_grads = []
    for micro_step in range(MICRO):
        offset = micro_step * SEQ_MB
        seq_inputs = inputs[offset : offset + SEQ_MB].astype(jnp.float32)
        cond_rows = conditioning[offset : offset + SEQ_MB]
        modulation = jnp.dot(cond_rows, ada_full, preferred_element_type=jnp.float32)
        pieces = [p[:, None, :] for p in jnp.split(modulation, 6, axis=1)]
        shift_one, scale_one, gate_one, shift_two, scale_two, gate_two = pieces
        normed_one, inv_one = normalize(seq_inputs)
        first_in = (normed_one * gain_first * (1.0 + scale_one) + shift_one).astype(jnp.bfloat16)
        projected = jnp.dot(first_in, qkv_full, preferred_element_type=jnp.float32)
        projected = projected.reshape(SEQ_MB, rows, 3, HEADS, HEAD_DIM)
        rot_query = rotate(projected[:, :, 0], cos_table, sin_table)
        rot_key = rotate(projected[:, :, 1], cos_table, sin_table)
        packed = jnp.stack([rot_query, rot_key, projected[:, :, 2]], axis=2).reshape(
            SEQ_MB, rows, 3, width
        )
        regrouped = lax.all_to_all(
            packed.astype(jnp.bfloat16), "ulysses", split_axis=3, concat_axis=1, tiled=True
        )
        query_rows = regrouped.shape[1]
        head_width = regrouped.shape[3]
        local_heads = head_width // HEAD_DIM
        query_heads = (
            regrouped[:, :, 0]
            .reshape(SEQ_MB, query_rows, local_heads, HEAD_DIM)
            .transpose(0, 2, 1, 3)
        )
        kv_local = regrouped[:, :, 1:]
        start_carry = (
            jnp.full((SEQ_MB, local_heads, query_rows), -1e30, jnp.float32),
            jnp.zeros((SEQ_MB, local_heads, query_rows), jnp.float32),
            jnp.zeros((SEQ_MB, local_heads, query_rows, HEAD_DIM), jnp.float32),
        )

        def scan_forward(carry, block):
            return (forward_block(query_heads, carry, block), None)

        result, _ = lax.scan(
            scan_forward,
            start_carry,
            split_blocks(lax.all_gather(kv_local, "blk", axis=1, tiled=True), query_rows),
        )
        carry = result
        top, totals, accum = carry
        attn_heads = accum / totals[..., None]
        log_total = top + jnp.log(totals)
        attn_tokens = (
            attn_heads.astype(jnp.bfloat16)
            .transpose(0, 2, 1, 3)
            .reshape(SEQ_MB, query_rows, head_width)
        )
        attended = lax.all_to_all(attn_tokens, "ulysses", split_axis=1, concat_axis=2, tiled=True)
        branch = jnp.dot(attended, out_full, preferred_element_type=jnp.float32)
        middle = seq_inputs + gate_one * branch
        normed_two, inv_two = normalize(middle)
        second_in = (normed_two * gain_second * (1.0 + scale_two) + shift_two).astype(jnp.bfloat16)
        raised = jnp.dot(second_in, up_full, preferred_element_type=jnp.float32)
        hidden, gelu_pull = jax.vjp(gelu_tanh, raised)
        hidden_low = hidden.astype(jnp.bfloat16)
        lowered = jnp.dot(hidden_low, down_full, preferred_element_type=jnp.float32)
        outputs_list.append(middle + gate_two * lowered)
        grad_out = cotangent[offset : offset + SEQ_MB].astype(jnp.float32)
        d_lowered = (gate_two * grad_out).astype(jnp.bfloat16)
        d_gate_two = jnp.sum(grad_out * lowered, axis=1)
        down_term = jnp.einsum(
            "srf,srd->fd", hidden_low, d_lowered, preferred_element_type=jnp.float32
        )
        d_hidden = jnp.einsum(
            "srd,fd->srf", d_lowered, down_full, preferred_element_type=jnp.float32
        )
        (d_raised,) = gelu_pull(d_hidden)
        d_raised_low = d_raised.astype(jnp.bfloat16)
        up_term = jnp.einsum(
            "srd,srf->df", second_in, d_raised_low, preferred_element_type=jnp.float32
        )
        d_second = jnp.einsum(
            "srf,df->srd", d_raised_low, up_full, preferred_element_type=jnp.float32
        )
        d_norm_two, gain_two_term, d_scale_two, d_shift_two = norm_back(
            d_second, normed_two, inv_two, gain_second, scale_two
        )
        d_middle = grad_out + d_norm_two
        d_gate_one = jnp.sum(d_middle * branch, axis=1)
        d_branch = (gate_one * d_middle).astype(jnp.bfloat16)
        out_term = jnp.einsum("srd,sre->de", attended, d_branch, preferred_element_type=jnp.float32)
        d_attended = jnp.einsum(
            "sre,de->srd", d_branch, out_full, preferred_element_type=jnp.float32
        ).astype(jnp.bfloat16)
        d_attn_rows = lax.all_to_all(d_attended, "ulysses", split_axis=2, concat_axis=1, tiled=True)
        d_attn_heads = d_attn_rows.reshape(SEQ_MB, query_rows, local_heads, HEAD_DIM).transpose(
            0, 2, 1, 3
        )
        delta = jnp.sum(d_attn_heads.astype(jnp.float32) * attn_heads, axis=-1)
        all_pairs = lax.all_gather(kv_local, "blk", axis=1, tiled=True)

        def back_step(d_query, block):
            keys, values = split_pairs(block)
            scores = (
                jnp.einsum("shqd,skhd->shqk", query_heads, keys, preferred_element_type=jnp.float32)
                * score_scale
            )
            probs = jnp.exp(scores - log_total[..., None])
            d_probs = jnp.einsum(
                "shqd,skhd->shqk", d_attn_heads, values, preferred_element_type=jnp.float32
            )
            d_scores = (probs * (d_probs - delta[..., None])).astype(jnp.bfloat16)
            d_query = (
                d_query
                + jnp.einsum("shqk,skhd->shqd", d_scores, keys, preferred_element_type=jnp.float32)
                * score_scale
            )
            d_keys = (
                jnp.einsum(
                    "shqk,shqd->skhd", d_scores, query_heads, preferred_element_type=jnp.float32
                )
                * score_scale
            )
            d_values = jnp.einsum(
                "shqk,shqd->skhd",
                probs.astype(jnp.bfloat16),
                d_attn_heads,
                preferred_element_type=jnp.float32,
            )
            key_rows = block.shape[1]
            pair = jnp.stack(
                [
                    d_keys.reshape(SEQ_MB, key_rows, head_width),
                    d_values.reshape(SEQ_MB, key_rows, head_width),
                ],
                axis=2,
            )
            return (d_query, pair)

        query_zero = jnp.zeros((SEQ_MB, local_heads, query_rows, HEAD_DIM), jnp.float32)
        d_query, pair_terms = lax.scan(back_step, query_zero, split_blocks(all_pairs, query_rows))
        pair_terms = jnp.moveaxis(pair_terms, 0, 1)
        pair_terms = pair_terms.reshape(
            SEQ_MB, pair_terms.shape[1] * pair_terms.shape[2], 2, head_width
        )
        pair_sums = lax.psum_scatter(pair_terms, "blk", scatter_dimension=1, tiled=True)
        query_grad = d_query.transpose(0, 2, 1, 3).reshape(SEQ_MB, query_rows, 1, head_width)
        d_packed = jnp.concatenate([query_grad, pair_sums], axis=2).astype(jnp.bfloat16)
        d_local = lax.all_to_all(d_packed, "ulysses", split_axis=1, concat_axis=3, tiled=True)
        d_local = d_local.astype(jnp.float32).reshape(SEQ_MB, rows, 3, HEADS, HEAD_DIM)
        d_projected = (
            jnp.stack(
                [
                    unrotate(d_local[:, :, 0], cos_table, sin_table),
                    unrotate(d_local[:, :, 1], cos_table, sin_table),
                    d_local[:, :, 2],
                ],
                axis=2,
            )
            .reshape(SEQ_MB, rows, 3 * width)
            .astype(jnp.bfloat16)
        )
        qkv_term = jnp.einsum(
            "srd,sre->de", first_in, d_projected, preferred_element_type=jnp.float32
        )
        d_first = jnp.einsum(
            "sre,de->srd", d_projected, qkv_full, preferred_element_type=jnp.float32
        )
        d_norm_one, gain_one_term, d_scale_one, d_shift_one = norm_back(
            d_first, normed_one, inv_one, gain_first, scale_one
        )
        input_grads.append(d_middle + d_norm_one)
        mod_local = jnp.concatenate(
            [d_shift_one, d_scale_one, d_gate_one, d_shift_two, d_scale_two, d_gate_two], axis=1
        )
        mod_total = lax.psum(mod_local, ("ulysses", "blk"))
        mod_low = mod_total.astype(jnp.bfloat16)
        cond_grads.append(
            jnp.einsum("sm,cm->sc", mod_low, ada_full, preferred_element_type=jnp.float32)
        )
        mod_part = lax.dynamic_slice_in_dim(mod_low, device_index * ada_cols, ada_cols, 1)
        ada_grad = ada_grad + jnp.einsum(
            "sc,sm->cm", cond_rows, mod_part, preferred_element_type=jnp.float32
        )
        terms = (qkv_term, out_term, up_term, down_term, gain_one_term, gain_two_term)
        reduced = (
            lax.psum_scatter(terms[0], ("ulysses", "blk"), scatter_dimension=0, tiled=True),
            lax.psum_scatter(terms[1], ("ulysses", "blk"), scatter_dimension=0, tiled=True),
            lax.psum_scatter(terms[2], ("ulysses", "blk"), scatter_dimension=0, tiled=True),
            lax.psum_scatter(terms[3], ("ulysses", "blk"), scatter_dimension=0, tiled=True),
            lax.psum_scatter(terms[4], ("ulysses", "blk"), scatter_dimension=0, tiled=True),
            lax.psum_scatter(terms[5], ("ulysses", "blk"), scatter_dimension=0, tiled=True),
        )
        grad_totals = tuple((a + b for a, b in zip(grad_totals, reduced)))
    output = jnp.concatenate(outputs_list, axis=0)
    inputs_grad = jnp.concatenate(input_grads, axis=0)
    conditioning_grad = jnp.concatenate(cond_grads, axis=0)
    return (
        output,
        inputs_grad,
        conditioning_grad,
        ada_grad,
        grad_totals[0],
        grad_totals[1],
        grad_totals[2],
        grad_totals[3],
        grad_totals[4],
        grad_totals[5],
    )


def dot_nt(left, right):
    return lax.dot_general(left, right, (((1,), (1,)), ((), ())), preferred_element_type=f32)


def dot_tn(left, right):
    return lax.dot_general(left, right, (((0,), (0,)), ((), ())), preferred_element_type=f32)


def row_norm(values):
    centered = values - jnp.mean(values, axis=1, keepdims=True)
    inv_std = lax.rsqrt(jnp.mean(centered * centered, axis=1, keepdims=True) + eps_norm)
    return centered * inv_std, inv_std


def row_back(grads, normed, inv_std):
    return inv_std * (
        grads
        - jnp.mean(grads, axis=1, keepdims=True)
        - normed * jnp.mean(grads * normed, axis=1, keepdims=True)
    )


def turn(values, cos_ref, sin_ref, sign):
    lane = lax.broadcasted_iota(jnp.int32, values.shape, 1) % HEAD_DIM
    swapped = jnp.where(
        lane < HEAD_DIM // 2, pltpu.roll(values, 128 - HEAD_DIM // 2, 1), pltpu.roll(values, HEAD_DIM // 2, 1)
    )
    return values * cos_ref[...] + sign * (swapped * sin_ref[...])


def mod_row(table_ref, s, i):
    width = table_ref.shape[1] // 7
    return table_ref[s : s + 1, i * width : (i + 1) * width]


EXTRA = 48


def split_low(values):
    high = values.astype(bf16).astype(f32)
    return high, values - high


def extra_rows(mods, gains, s_rows, store):
    for s in range(s_rows):
        for part, (mod, gain) in enumerate(zip(split_low(mods[s : s + 1]), split_low(gains[s : s + 1]))):
            at = (part * s_rows + s) * 4
            for i in range(3):
                store(at + i, mod[:, EXTRA * i : EXTRA * (i + 1)])
            store(at + 3, gain)


def pack_kernel(
    x_ref, g_ref, qkv_ref, ada_ref, cond_ref, one_ref, two_ref, up_ref, xc_ref, piece_ref, ext_ref,
):
    n_u, block, cols = piece_ref.shape
    xc_ref[0] = x_ref[...]
    xc_ref[1] = g_ref[...]
    width = qkv_ref.shape[1] // 3
    ff = up_ref.shape[1] // n_u
    heads = width // n_u // HEAD_DIM
    ext_ref[...] = jnp.zeros_like(ext_ref)
    mods = dot_nt(cond_ref[...], ada_ref[...])
    gains = jnp.concatenate([one_ref[...], two_ref[...]], axis=0).astype(f32)

    def store(row, value):
        ext_ref[row : row + 1, : value.shape[1]] = value

    extra_rows(mods, gains, mods.shape[0], store)
    extra = ext_ref[...].astype(bf16)
    for i in range(n_u):
        pieces = []
        for h in range(heads):
            at = (i * heads + h) * HEAD_DIM
            pieces += [qkv_ref[:, at : at + HEAD_DIM], qkv_ref[:, width + at : width + at + HEAD_DIM]]
        at = 2 * width + i * heads * HEAD_DIM
        pieces += [qkv_ref[:, at : at + heads * HEAD_DIM], extra]
        piece_ref[i, :, : cols - ff] = jnp.concatenate(pieces, axis=1)
        piece_ref[i, :, cols - ff :] = up_ref[:, i * ff : (i + 1) * ff]


def first_kernel(
    at_ref, xg_ref, cos_ref, sin_ref, a0, a1, a2, a3, a4, a5, a6, a7,
    chunk_ref, first_ref, table_ref, w_ref, out_ref, wide_ref, wout_ref,
):
    u, b = at_ref[0], at_ref[1]
    n_u, _, seqs, rows, width = xg_ref.shape
    span = n_u * rows
    cols = w_ref.shape[1]
    heads = cols // 192
    block = width // 32
    for i, part_ref in enumerate((a0, a1, a2, a3, a4, a5, a6, a7)):
        there = b ^ i
        part = part_ref[...].astype(f32)
        quarter = part.shape[1] - cols - HEAD_DIM
        for j in range(n_u):
            start = pl.multiple_of((j * 8 + there) * block, 8)
            wide_ref[pl.ds(start, block), :] = part[j * block : (j + 1) * block, : cols + HEAD_DIM]
            start = pl.multiple_of(there * block, 8)
            wout_ref[pl.ds(start, block), j * quarter : (j + 1) * quarter] = part[
                j * block : (j + 1) * block, cols + HEAD_DIM :
            ]
    w_ref[...] = wide_ref[:, :cols].astype(bf16)
    out_ref[...] = wout_ref[...].astype(bf16)
    for s in range(seqs):
        mods, gains = [], []
        for d in range(32):
            pair = wide_ref[d * block : (d + 1) * block, cols:]
            both = pair[s * 4 : s * 4 + 4] + pair[(seqs + s) * 4 : (seqs + s) * 4 + 4]
            mods += [both[i : i + 1, :EXTRA] for i in range(3)]
            gains.append(both[3:4, :block])
        table_ref[s : s + 1, :] = jnp.concatenate(mods + gains, axis=1)
    gain = mod_row(table_ref, 0, 6)
    zero = jnp.zeros(chunk_ref.shape[1:], bf16)
    chunk_ref[0] = zero
    chunk_ref[chunk_ref.shape[0] - 1] = zero
    for s in range(seqs):
        factor = gain * (1.0 + mod_row(table_ref, s, 1))
        for m in range(n_u):
            normed, _ = row_norm(xg_ref[u ^ m, 0, s].astype(f32))
            first = normed * factor + mod_row(table_ref, s, 0)
            first_ref[s * span + m * rows : s * span + (m + 1) * rows, :] = first.astype(bf16)
        projected = DOT(first_ref[s * span : (s + 1) * span, :], w_ref[...])
        for h in range(heads):
            pair = 1 + s * heads + h
            both = turn(projected[:, 128 * h : 128 * (h + 1)], cos_ref, sin_ref, 1.0)
            chunk_ref[pair, :span, :] = both.astype(bf16)
            v = projected[:, 128 * heads + 64 * h : 128 * heads + 64 * (h + 1)].astype(bf16)
            chunk_ref[pair, span:, :] = jnp.concatenate([v[: span // 2], v[span // 2 :]], axis=1)


def unpack_tokens(t_ref, s, h, heads):
    half = t_ref[1 + s * heads + h]
    return jnp.concatenate([half[:, :HEAD_DIM], half[:, HEAD_DIM:]], axis=0)


def store_parts(send_ref, keep_ref, part, s, rows):
    for m in range(4):
        block = part[m * rows : (m + 1) * rows]
        if m % 2:
            send_ref[m // 2, s] = block.astype(bf16)
        else:
            keep_ref[m // 2, s] = block


def out_kernel(t_ref, w_ref, att_ref, send_ref, keep_ref):
    _, seqs, rows, _ = send_ref.shape
    heads = w_ref.shape[0] // HEAD_DIM
    span = 4 * rows
    for s in range(seqs):
        att = jnp.concatenate([unpack_tokens(t_ref, s, h, heads) for h in range(heads)], axis=1)
        att_ref[s * span : (s + 1) * span, :] = att
        store_parts(send_ref, keep_ref, DOT(att, w_ref[...]), s, rows)


def block_of(own_ref, got_ref, m, s):
    return (got_ref if m % 2 else own_ref)[m // 2, s].astype(f32)


def middle_of(xg_ref, own_ref, got_ref, table_ref, u, m, s):
    return xg_ref[u ^ m, 0, s].astype(f32) + mod_row(table_ref, s, 2) * block_of(own_ref, got_ref, m, s)


def ff_kernel(
    at_ref, xg_ref, own_ref, got_ref, table_ref, a0, a1, a2, a3, a4, a5, a6, a7, b0, b1, b2, b3, b4, b5, b6, b7,
    lsend_ref, lkeep_ref, dsend_ref, dkeep_ref, sums_ref, ukeep_ref, usend_ref, dgrad_ref,
    second_ref, hidden_ref, low_ref, raised_ref, normed_ref, wide_ref, up_ref, down_ref,
):
    u = at_ref[0]
    n_u, _, seqs, rows, width = xg_ref.shape
    span = n_u * rows
    gain = mod_row(table_ref, 1, 6)
    scale = math.sqrt(2.0 / math.pi)
    block = width // 32
    low = n_u * block
    u, b = at_ref[0], at_ref[1]
    ups, downs = (a0, a1, a2, a3, a4, a5, a6, a7), (b0, b1, b2, b3, b4, b5, b6, b7)
    for i, (part_ref, low_part_ref) in enumerate(zip(ups, downs)):
        there = b ^ i
        down_ref[pl.ds(pl.multiple_of(there * low, 32), low), :] = low_part_ref[...]
        for j in range(n_u):
            start = pl.multiple_of((j * 8 + there) * block, 8)
            wide_ref[pl.ds(start, block), :] = part_ref[j * block : (j + 1) * block, :].astype(f32)
    up_ref[...] = wide_ref[...].astype(bf16)
    for s in range(seqs):
        at = slice(s * span, (s + 1) * span)
        factor = gain * (1.0 + mod_row(table_ref, s, 4))
        gate = mod_row(table_ref, s, 5)
        for m in range(n_u):
            here = slice(s * span + m * rows, s * span + (m + 1) * rows)
            normed, _ = row_norm(middle_of(xg_ref, own_ref, got_ref, table_ref, u, m, s))
            normed_ref[m * rows : (m + 1) * rows, :] = normed
            second_ref[here, :] = (normed * factor + mod_row(table_ref, s, 3)).astype(bf16)
            low_ref[here, :] = (gate * xg_ref[u ^ m, 1, s].astype(f32)).astype(bf16)
        raised = DOT(second_ref[at, :], up_ref[...])
        d_hidden = dot_nt(low_ref[at, :], down_ref[...])
        square = raised * raised
        t = jnp.tanh(scale * raised * (1.0 + 0.044715 * square))
        hidden_ref[at, :] = (0.5 * raised * (1.0 + t)).astype(bf16)
        slope = 0.5 * (1.0 + t) + 0.5 * raised * (1.0 - t * t) * (scale * (1.0 + 3.0 * 0.044715 * square))
        raised_ref[at, :] = (d_hidden * slope).astype(bf16)
        d_second = dot_nt(raised_ref[at, :], up_ref[...])
        store_parts(dsend_ref, dkeep_ref, d_second, s, rows)
        lowered = DOT(hidden_ref[at, :], down_ref[...])
        store_parts(lsend_ref, lkeep_ref, lowered, s, rows)
        sums_ref[s, 0:1, :] = jnp.sum(d_second, axis=0, keepdims=True)
        sums_ref[s, 1:2, :] = jnp.sum(d_second * normed_ref[...], axis=0, keepdims=True)
        gated = jnp.zeros((1, width), f32)
        for m in range(n_u):
            grad = xg_ref[u ^ m, 1, s].astype(f32)
            gated = gated + jnp.sum(grad * lowered[m * rows : (m + 1) * rows], axis=0, keepdims=True)
        sums_ref[s, 2:3, :] = gated
    n_z = ukeep_ref.shape[0]
    wide_ref[...] = dot_tn(second_ref[...], raised_ref[...])
    for y, out_ref in enumerate((ukeep_ref, usend_ref)):
        for z in range(n_z):
            for i in range(n_u):
                start = pl.multiple_of(((u ^ i) * 2 * n_z + (b ^ (2 * z + y))) * block, 8)
                out_ref[z, i] = wide_ref[pl.ds(start, block), :].astype(bf16)
    dgrad_ref[...] = dot_tn(hidden_ref[...], low_ref[...]).astype(bf16)


def middle_back_kernel(
    at_ref, xg_ref, own_ref, got_ref, down_ref, dgot_ref, table_ref, w_ref, att_ref,
    chunk_ref, dmid_ref, gate_ref, okeep_ref, osend_ref, branch_ref, outs_ref,
):
    u = at_ref[0]
    n_u, _, seqs, rows, width = xg_ref.shape
    span = n_u * rows
    heads = w_ref.shape[0] // HEAD_DIM
    gain = mod_row(table_ref, 1, 6)
    zero = jnp.zeros(chunk_ref.shape[1:], bf16)
    chunk_ref[0] = zero
    chunk_ref[chunk_ref.shape[0] - 1] = zero
    for s in range(seqs):
        at = slice(s * span, (s + 1) * span)
        factor = gain * (1.0 + mod_row(table_ref, s, 4))
        gate = mod_row(table_ref, s, 2)
        for m in range(n_u):
            normed, inv_std = row_norm(middle_of(xg_ref, own_ref, got_ref, table_ref, u, m, s))
            grads = block_of(down_ref, dgot_ref, m, s) * factor
            d_middle = xg_ref[u ^ m, 1, s].astype(f32) + row_back(grads, normed, inv_std)
            branch_ref[s * span + m * rows : s * span + (m + 1) * rows, :] = (gate * d_middle).astype(bf16)
            if m == 0:
                dmid_ref[s] = d_middle
                gate_ref[s] = jnp.sum(d_middle * own_ref[0, s].astype(f32), axis=0, keepdims=True)
        d_att = dot_nt(branch_ref[at, :], w_ref[...]).astype(bf16)
        for h in range(heads):
            d = d_att[:, HEAD_DIM * h : HEAD_DIM * (h + 1)]
            chunk_ref[1 + s * heads + h] = jnp.concatenate([d[: span // 2], d[span // 2 :]], axis=1)
    n_z, block, _ = okeep_ref.shape
    outs_ref[...] = dot_tn(att_ref[...], branch_ref[...])
    for y, out_ref in enumerate((okeep_ref, osend_ref)):
        for z in range(n_z):
            start = pl.multiple_of((at_ref[1] ^ (2 * z + y)) * block, 8)
            out_ref[z] = outs_ref[pl.ds(start, block), :].astype(bf16)


def first_back_kernel(
    at_ref, t_ref, xg_ref, table_ref, cos_ref, sin_ref, w_ref, first_ref, gate_ref, two_ref,
    send_ref, keep_ref, blocks_ref, proj_ref, normed_ref, sums_ref, ext_ref,
):
    u = at_ref[0]
    n_u, _, seqs, rows, width = xg_ref.shape
    span = n_u * rows
    cols = w_ref.shape[1]
    heads = cols // 192
    gain_grads = [jnp.zeros((1, width), f32)] * 2
    total, block, _ = blocks_ref.shape
    for s in range(seqs):
        at = slice(s * span, (s + 1) * span)
        for h in range(heads):
            pair = t_ref[1 + s * heads + h]
            both = turn(pair[:span].astype(f32), cos_ref, sin_ref, -1.0)
            proj_ref[at, 128 * h : 128 * (h + 1)] = both.astype(bf16)
            v = pair[span:]
            proj_ref[at, 128 * heads + 64 * h : 128 * heads + 64 * (h + 1)] = jnp.concatenate(
                [v[:, :HEAD_DIM], v[:, HEAD_DIM:]], axis=0
            )
        d_first = dot_nt(proj_ref[at, :], w_ref[...])
        store_parts(send_ref, keep_ref, d_first, s, rows)
        for m in range(n_u):
            normed, _ = row_norm(xg_ref[u ^ m, 0, s].astype(f32))
            normed_ref[m * rows : (m + 1) * rows, :] = normed
        dots = [jnp.sum(d_first * normed_ref[...], axis=0, keepdims=True), two_ref[s, 1:2, :]]
        for i in range(2):
            gain_grads[i] = gain_grads[i] + dots[i] * (1.0 + mod_row(table_ref, s, 1 + 3 * i))
        rows_out = [
            jnp.sum(d_first, axis=0, keepdims=True),
            dots[0] * mod_row(table_ref, 0, 6),
            gate_ref[s],
            two_ref[s, 0:1, :],
            dots[1] * mod_row(table_ref, 1, 6),
            two_ref[s, 2:3, :],
        ]
        for i, row in enumerate(rows_out):
            sums_ref[s : s + 1, i * width : (i + 1) * width] = row
    for i in range(2):
        sums_ref[i : i + 1, 6 * width :] = gain_grads[i]
    ext_ref[...] = jnp.zeros_like(ext_ref)
    for d in range(total):

        def store(row, value):
            ext_ref[d * block + row : d * block + row + 1, : value.shape[1]] = value

        mods = sums_ref[:, 3 * EXTRA * d : 3 * EXTRA * (d + 1)]
        extra_rows(mods, sums_ref[:, 6 * width + block * d : 6 * width + block * (d + 1)], seqs, store)
    grads = dot_tn(first_ref[...], proj_ref[...])
    for i in range(total):
        at = slice(i * block, (i + 1) * block)
        blocks_ref[i, :, :cols] = grads[at].astype(bf16)
        blocks_ref[i, :, cols:] = ext_ref[at].astype(bf16)


def row_grad_kernel(at_ref, raw_ref, p0, p1, p2, p3, ada_ref, cond_ref, qkv_ref, up_ref, part_ref, adag_ref, gain_ref, mod_ref):
    u = at_ref[0]
    total, block, cols = raw_ref.shape
    cols = cols - HEAD_DIM
    n_u = 4
    n_b = total // n_u
    heads = cols // 192
    width = qkv_ref.shape[1] // 3
    seqs = mod_ref.shape[0]
    extra = jnp.zeros((block, HEAD_DIM), f32)
    for i in range(n_u):
        part = raw_ref[i * n_b].astype(f32)
        for j in range(1, n_b):
            part = part + raw_ref[i * n_b + j].astype(f32)
        extra = extra + part[:, cols:]
        for h in range(heads):
            to = (i * heads + h) * HEAD_DIM
            qkv_ref[:, to : to + HEAD_DIM] = part[:, 128 * h : 128 * h + HEAD_DIM]
            qkv_ref[:, width + to : width + to + HEAD_DIM] = part[:, 128 * h + HEAD_DIM : 128 * (h + 1)]
        at = i * heads * HEAD_DIM
        qkv_ref[:, 2 * width + at : 2 * width + at + heads * HEAD_DIM] = part[:, 128 * heads : cols]
    for s in range(seqs):
        both = extra[s * 4 : s * 4 + 4] + extra[(seqs + s) * 4 : (seqs + s) * 4 + 4]
        mod_ref[s : s + 1, :] = jnp.concatenate([both[i : i + 1, :EXTRA] for i in range(3)], axis=1)
        gain_ref[s : s + 1, :] = both[3:4, :block]
    mods = mod_ref[...].astype(bf16)
    grads = DOT(mods, ada_ref[...])
    for i in range(total):
        part_ref[i] = grads
    adag_ref[...] = dot_tn(mods, cond_ref[...])
    cols = up_ref.shape[1] // n_u
    for i, piece_ref in enumerate((p0, p1, p2, p3)):
        up_ref[:, pl.ds(pl.multiple_of((u ^ i) * cols, 128), cols)] = piece_ref[...]


def input_grad_kernel(x_ref, near_ref, got_ref, dmid_ref, table_ref, out_ref):
    seqs = x_ref.shape[0]
    for s in range(seqs):
        factor = mod_row(table_ref, 0, 6) * (1.0 + mod_row(table_ref, s, 1))
        normed, inv_std = row_norm(x_ref[s].astype(f32))
        grads = (near_ref[s] + got_ref[s].astype(f32)) * factor
        out_ref[s] = dmid_ref[s] + row_back(grads, normed, inv_std)


def call(kernel, name, outs, scratch, flops, *args, limit=16, staged=()):
    count = len(args)
    specs = [
        pl.BlockSpec(
            memory_space=pltpu.SMEM if a.dtype == jnp.int32 else pltpu.HBM if i in staged else pltpu.VMEM
        )
        for i, a in enumerate(args)
    ]
    size = sum(math.prod(a.shape) * a.dtype.itemsize for a in args)
    size += sum(math.prod(shape) * jnp.dtype(dtype).itemsize for shape, dtype in outs)
    shapes = [pltpu.VMEM(*s) for s in scratch]
    body = kernel
    if staged:
        shapes = [pltpu.VMEM(args[i].shape, args[i].dtype) for i in staged] + [
            pltpu.SemaphoreType.DMA((len(staged),))
        ] + shapes

        def body(*refs):
            ins, rest = list(refs[:count]), refs[count:]
            out_refs, held = rest[: len(outs)], rest[len(outs) :]
            sems = held[len(staged)]
            copies = []
            for j, i in enumerate(staged):
                copies.append(pltpu.make_async_copy(ins[i], held[j], sems.at[j]))
                ins[i] = held[j]
            for copy in copies:
                copy.start()
            for copy in copies:
                copy.wait()
            kernel(*ins, *out_refs, *held[len(staged) + 1 :])

    return pl.pallas_call(
        body,
        out_shape=tuple(jax.ShapeDtypeStruct(shape, dtype) for shape, dtype in outs),
        in_specs=specs,
        out_specs=tuple(pl.BlockSpec(memory_space=pltpu.VMEM) for _ in outs),
        scratch_shapes=shapes,
        cost_estimate=pl.CostEstimate(flops=int(flops) // 1000, bytes_accessed=int(size) // 1000, transcendentals=0),
        compiler_params=pltpu.CompilerParams(vmem_limit_bytes=limit << 20),
        name=name,
    )(*args)


def fits_tp(mesh):
    ulysses, blk = mesh.shape["ulysses"], mesh.shape["blk"]
    return ulysses == 4 and blk == 8 and HEADS % ulysses == 0


def swap_u(values, mask):
    return lax.ppermute(values, "ulysses", [(i, i ^ mask) for i in range(4)])


def swap_b(values, mask):
    return lax.ppermute(values, "blk", [(i, i ^ mask) for i in range(8)])


def exchange(blocks, axis):
    return lax.all_to_all(blocks, axis, split_axis=0, concat_axis=0, tiled=True)


def half_sum(send, keep):
    return keep + swap_u(send, 1).astype(f32)


def along_z(values):
    return [values] + [swap_b(values, 2 * m) for m in (1, 2, 3)]


def along_y(parts):
    out = []
    for part in parts:
        out += [part, swap_b(part, 1)]
    return out


def sum_z(half):
    total = half[0]
    for m in (1, 2, 3):
        total = total + swap_b(half[m].astype(bf16), 2 * m).astype(f32)
    return total


def tp_shards(inputs, conditioning, w_ada, w_qkv, w_out, w_up, w_down, gain_one, gain_two, cotangent):
    n_u, n_b = 4, 8
    n_all = n_u * n_b
    everywhere = ("ulysses", "blk")
    seqs, rows, width = inputs.shape
    u = lax.axis_index("ulysses")
    b = lax.axis_index("blk")
    at = jnp.stack([u, b]).astype(jnp.int32)
    heads = HEADS // n_u
    head_width = heads * HEAD_DIM
    cols = 3 * head_width
    w_rows, down_rows = w_qkv.shape[0], w_down.shape[0]
    ff_local = w_up.shape[1] // n_u
    span = n_u * rows
    tokens = seqs * span

    both, pieces = call(
        pack_kernel, "pack",
        [((2,) + inputs.shape, bf16), ((n_u, w_rows, cols + HEAD_DIM + ff_local), bf16)],
        [((w_rows, HEAD_DIM), f32)], 0,
        inputs, cotangent, w_qkv, w_ada.T, conditioning, gain_one[None], gain_two[None], w_up,
        limit=60,
    )
    blocks = u ^ jnp.arange(n_u, dtype=jnp.int32)
    positions = ((blocks * n_b + b) * rows)[:, None] + jnp.arange(rows, dtype=jnp.int32)[None, :]
    cos_table, sin_table = rotary_tables(positions.reshape(-1).astype(f32))
    cos_table, sin_table = cos_table[:, 0], sin_table[:, 0]
    cos_table = jnp.concatenate([cos_table] * 4, axis=1)
    sin_table = jnp.concatenate([-sin_table, sin_table] * 2, axis=1)

    pieces, cos_table, sin_table, at = lax.optimization_barrier(
        (exchange(pieces, "ulysses"), cos_table, sin_table, at)
    )
    pieces = pieces.reshape(n_u * w_rows, cols + HEAD_DIM + ff_local)
    xg = lax.all_gather(both, "ulysses", axis=0, tiled=False)
    up_near = pieces[:, cols + HEAD_DIM :]
    down_z = along_z(w_down)
    quarter = width // n_u
    near = jnp.concatenate(
        [
            pieces[:, : cols + HEAD_DIM],
            jnp.concatenate([w_out[:, i * quarter : (i + 1) * quarter] for i in range(n_u)], axis=0),
        ],
        axis=1,
    )
    near, down_z = lax.optimization_barrier((near, down_z))
    rows_zy = along_y(along_z(near))

    chunks, first_in, table, w_qkv_u, w_out_u = call(
        first_kernel, "first",
        [((n_b, 3 * span // 2, 128), bf16), ((tokens, width), bf16), ((seqs, 7 * width), f32),
         ((width, cols), bf16), ((head_width, width), bf16)],
        [((width, cols + HEAD_DIM), f32), ((head_width, width), f32)],
        2 * tokens * width * cols,
        at, xg, cos_table, sin_table, *rows_zy,
        limit=60,
    )
    chunks, down_z = lax.optimization_barrier((chunks, down_z))
    owned = exchange(chunks, "blk")
    down_zy = along_y(down_z)
    owned, up_near, down_zy[1], down_zy[3] = lax.optimization_barrier((owned, up_near, down_zy[1], down_zy[3]))
    up_z = along_z(up_near)
    up_0y = swap_b(up_near, 1)
    attn_low, attn_full, log_total = attn_fwd(owned)
    part_shape = (2, seqs, rows, width)
    attn_low, up_z, up_0y, down_zy = lax.optimization_barrier((attn_low, up_z, up_0y, down_zy))
    attn_tokens = exchange(attn_low, "blk")
    attended, send, keep = call(
        out_kernel, "out",
        [((tokens, head_width), bf16), (part_shape, bf16), (part_shape, f32)], [],
        2 * tokens * width * head_width,
        attn_tokens, w_out_u,
    )

    half = half_sum(send, keep)
    across = swap_u(half.astype(bf16), 2)
    up_zy = [up_near, up_0y] + along_y(up_z[1:])
    across, up_zy = lax.optimization_barrier((across, up_zy))
    own = (half + across[::-1].astype(f32)).astype(bf16)
    got = swap_u(own, 1)
    lsend, lkeep, dsend, dkeep, sums_two, up_keep, up_send, down_term = call(
        ff_kernel, "ff",
        [(part_shape, bf16), (part_shape, f32), (part_shape, bf16), (part_shape, f32), ((seqs, 3, width), f32)]
        + [((n_b // 2, n_u, w_rows, width), bf16)] * 2 + [((ff_local, width), bf16)],
        [((tokens, width), bf16), ((tokens, ff_local), bf16), ((tokens, width), bf16), ((tokens, ff_local), bf16),
         ((span, width), f32), ((width, ff_local), f32), ((width, ff_local), bf16), ((ff_local, width), bf16)],
        12 * tokens * width * ff_local,
        at, xg, own, got, table, *up_zy, *down_zy,
        limit=60,
    )
    up_other = swap_b(up_send, 1)
    down_grad = lax.psum_scatter(down_term, "blk", scatter_dimension=0, tiled=True)
    half = half_sum(dsend, dkeep)
    across = swap_u(half.astype(bf16), 2)
    d_own = (half + across[::-1].astype(f32)).astype(bf16)
    d_got = swap_u(d_own, 1)
    d_chunks, d_middle, sum_gate, out_keep, out_send = call(
        middle_back_kernel, "middle_back",
        [((n_b, span // 2, 128), bf16), ((seqs, rows, width), f32), ((seqs, 1, width), f32)]
        + [((n_b // 2, w_rows, width), bf16)] * 2,
        [((tokens, width), bf16), ((head_width, width), f32)],
        4 * tokens * width * head_width,
        at, xg, own, got, d_own, d_got, table, w_out_u, attended,
        limit=60,
    )
    d_attn = exchange(d_chunks, "blk")
    out_other = swap_b(out_send, 1)
    up_half = up_keep.astype(f32) + up_other.astype(f32)
    up_1 = swap_b(up_half[1].astype(bf16), 2)
    d_attn, up_1, out_other = lax.optimization_barrier((d_attn, up_1, out_other))
    up_sum = up_half[0] + up_1.astype(f32)
    for m in (2, 3):
        up_sum = up_sum + swap_b(up_half[m].astype(bf16), 2 * m).astype(f32)
    d_owned = attn_bwd(owned, d_attn, attn_full, log_total)
    lhalf = half_sum(lsend, lkeep)
    lowered = lhalf[0] + swap_u(lhalf[1].astype(bf16), 2).astype(f32)
    gates = table.reshape(2, 7, 1, width)
    output = inputs.astype(f32) + gates[:, 2] * own[0].astype(f32) + gates[:, 5] * lowered
    d_owned, output, up_sum, out_other = lax.optimization_barrier((d_owned, output, up_sum, out_other))
    out_grad = sum_z(out_keep.astype(f32) + out_other.astype(f32))
    up_parts = [up_sum[0]] + [swap_u(up_sum[m], m) for m in (1, 2, 3)]
    d_tokens = exchange(d_owned, "blk")
    d_tokens, up_parts, out_grad, down_grad = lax.optimization_barrier((d_tokens, up_parts, out_grad, down_grad))

    send, keep, qkv_blocks = call(
        first_back_kernel, "first_back",
        [(part_shape, bf16), (part_shape, f32), ((n_all, w_rows, cols + HEAD_DIM), bf16)],
        [((tokens, cols), bf16), ((span, width), f32), ((seqs, 7 * width), f32), ((width, HEAD_DIM), f32)],
        4 * tokens * width * cols,
        at, d_tokens, xg, table, cos_table, sin_table, w_qkv_u, first_in, sum_gate, sums_two,
        limit=60,
    )
    half = half_sum(send, keep)
    far = swap_u(half[1].astype(bf16), 2)
    inputs_grad, = call(
        input_grad_kernel, "input_grad",
        [((seqs, rows, width), f32)], [], 0,
        inputs, half[0], far, d_middle, table,
    )
    qkv_grad, up_grad, cond_part, ada_grad, gain_grads, _ = call(
        row_grad_kernel, "row_grad",
        [(w_qkv.shape, f32), (w_up.shape, f32), ((n_all,) + conditioning.shape, f32), (w_ada.shape[::-1], f32),
         ((2, w_rows), f32), ((seqs, w_ada.shape[1]), f32)],
        [], 0,
        at, exchange(qkv_blocks, everywhere), *up_parts, w_ada.T, conditioning,
        limit=60,
    )
    conditioning_grad = jnp.sum(exchange(cond_part, everywhere), axis=0)
    return (
        output,
        inputs_grad,
        conditioning_grad,
        ada_grad.T,
        qkv_grad,
        out_grad,
        up_grad,
        down_grad.astype(f32),
        gain_grads[0],
        gain_grads[1],
    )


def solution(mesh):
    body = tp_shards if fits_tp(mesh) else shards
    in_specs = (
        P(None, ("ulysses", "blk"), None),
        P(),
        P(None, ("ulysses", "blk")),
        P(("ulysses", "blk"), None),
        P(("ulysses", "blk"), None),
        P(("ulysses", "blk"), None),
        P(("ulysses", "blk"), None),
        P(("ulysses", "blk")),
        P(("ulysses", "blk")),
        P(None, ("ulysses", "blk"), None),
    )
    out_specs = (
        P(None, ("ulysses", "blk"), None),
        P(None, ("ulysses", "blk"), None),
        P(),
        P(None, ("ulysses", "blk")),
        P(("ulysses", "blk"), None),
        P(("ulysses", "blk"), None),
        P(("ulysses", "blk"), None),
        P(("ulysses", "blk"), None),
        P(("ulysses", "blk")),
        P(("ulysses", "blk")),
    )
    return jax.shard_map(body, mesh=mesh, in_specs=in_specs, out_specs=out_specs, check_vma=False)
```

```python
import functools
import math

import jax
import jax.numpy as jnp
from jax import lax
from jax.experimental import pallas as pl
from jax.experimental.pallas import tpu as pltpu
from jax.sharding import PartitionSpec as P

f32, bf16 = jnp.float32, jnp.bfloat16
DOT = functools.partial(jnp.dot, preferred_element_type=f32)

def attn_fwd_kernel(x_ref, o_ref, of_ref, lse_ref, kt_ref, v_ref):
    nb, rows3, _ = x_ref.shape
    half = rows3 // 3
    rows = 2 * half
    for j in range(nb):
        kt_ref[:, j * rows : (j + 1) * rows] = x_ref[j, :rows, 64:].T
        v_ref[j * rows : j * rows + half, :] = x_ref[j, rows:, :64]
        v_ref[j * rows + half : (j + 1) * rows, :] = x_ref[j, rows:, 64:]

    for j in range(0, nb, 2):
        q = x_ref[j : j + 2, :rows, :64].reshape(2 * rows, 64) * jnp.asarray(0.125, bf16)
        s = DOT(q, kt_ref[...])
        top = jnp.max(s, axis=1, keepdims=True)
        p = jnp.exp(s - top)
        total = jnp.sum(p, axis=1, keepdims=True)
        o = DOT(p.astype(bf16), v_ref[...]) / total
        lse = jnp.broadcast_to(top + jnp.log(total), (2 * rows, 128)).T
        for i in range(2):
            packed = jnp.concatenate(
                [o[i * rows : i * rows + half], o[i * rows + half : (i + 1) * rows]], axis=1
            )
            of_ref[j + i] = packed
            o_ref[j + i] = packed.astype(bf16)
            lse_ref[j + i] = lse[:8, i * rows : (i + 1) * rows]

def attn_fwd(x):
    nb, rows3, _ = x.shape
    half = rows3 // 3
    n = nb * half * 2
    return pl.pallas_call(
        attn_fwd_kernel,
        out_shape=(jax.ShapeDtypeStruct((nb, half, 128), bf16), jax.ShapeDtypeStruct((nb, half, 128), f32),
                   jax.ShapeDtypeStruct((nb, 8, 2 * half), f32)),
        scratch_shapes=[pltpu.VMEM((64, n), bf16), pltpu.VMEM((n, 64), bf16)],
        cost_estimate=pl.CostEstimate(flops=4 * n * n * 64, bytes_accessed=n * 64 * 2 * 8, transcendentals=n * n),
        compiler_params=pltpu.CompilerParams(vmem_limit_bytes=32 << 20),
        name="attn_fwd",
    )(x)

def attn_bwd_kernel(x_ref, d_ref, of_ref, lse_ref, g_ref, qt_ref, dt_ref, q_ref, dd_ref, lse_s, del_s, dqt_ref):
    nb, rows3, _ = x_ref.shape
    half = rows3 // 3
    rows = 2 * half
    for j in range(nb):
        sl = slice(j * rows, (j + 1) * rows)
        q = x_ref[j, :rows, :64] * jnp.asarray(0.125, bf16)
        q_ref[sl, :] = q
        qt_ref[:, sl] = q.T
        d = jnp.concatenate([d_ref[j, :, :64], d_ref[j, :, 64:]], axis=0)
        dd_ref[sl, :] = d
        dt_ref[:, sl] = d.T
        o = jnp.concatenate([of_ref[j, :, :64], of_ref[j, :, 64:]], axis=0)
        delta = jnp.sum(d.astype(f32) * o, axis=1, keepdims=True)
        del_s[:, sl] = jnp.broadcast_to(delta, (rows, 128)).T[:8]
        lse_s[:, sl] = lse_ref[j]
    dqt_ref[...] = jnp.zeros_like(dqt_ref)

    for j in range(0, nb, 2):
        k = x_ref[j : j + 2, :rows, 64:].reshape(2 * rows, 64)
        v = jnp.concatenate(
            [x_ref[j + i, rows:, lanes] for i in range(2) for lanes in (slice(0, 64), slice(64, 128))], axis=0
        )
        s = DOT(k, qt_ref[...])
        p = jnp.exp(s - lse_s[0:1, :])
        dp = DOT(v, dt_ref[...])
        ds = (p * (dp - del_s[0:1, :])).astype(bf16)
        dv = DOT(p.astype(bf16), dd_ref[...]).astype(bf16)
        dk = DOT(ds, q_ref[...])
        dqt_ref[...] += DOT(k.T, ds)
        g_ref[j : j + 2, :rows, 64:] = dk.astype(bf16).reshape(2, rows, 64)
        for i in range(2):
            g_ref[j + i, rows:, :] = jnp.concatenate(
                [dv[i * rows : i * rows + half], dv[i * rows + half : (i + 1) * rows]], axis=1
            )
    for j in range(nb):
        g_ref[j, :rows, :64] = (dqt_ref[:, j * rows : (j + 1) * rows].T * 0.125).astype(bf16)

def attn_bwd(x, d, of, lse):
    nb, rows3, _ = x.shape
    half = rows3 // 3
    n = nb * half * 2
    return pl.pallas_call(
        attn_bwd_kernel,
        out_shape=jax.ShapeDtypeStruct((nb, rows3, 128), bf16),
        scratch_shapes=[pltpu.VMEM((64, n), bf16), pltpu.VMEM((64, n), bf16), pltpu.VMEM((n, 64), bf16), pltpu.VMEM((n, 64), bf16),
                        pltpu.VMEM((8, n), f32), pltpu.VMEM((8, n), f32), pltpu.VMEM((64, n), f32)],
        cost_estimate=pl.CostEstimate(flops=n * n * 64, bytes_accessed=n * 64 * 2, transcendentals=0),
        compiler_params=pltpu.CompilerParams(vmem_limit_bytes=32 << 20),
        name="attn_bwd",
    )(x, d, of, lse)

HEADS = 12
HEAD_DIM = 64
SEQ_MB = 1
MICRO = 2


eps_norm = 1e-06
shard_group = 4


def normalize(values):
    average = jnp.mean(values, axis=-1, keepdims=True)
    centered = values - average
    variance = jnp.mean(centered * centered, axis=-1, keepdims=True)
    inv_std = lax.rsqrt(variance + eps_norm)
    return (centered * inv_std, inv_std)


def norm_back(grad_out, normed, inv_std, gain, scale_mod):
    factor = 1.0 + scale_mod
    d_normed = grad_out * gain * factor
    gain_term = jnp.sum(grad_out * normed * factor, axis=(0, 1))
    scale_term = jnp.sum(grad_out * normed * gain, axis=1)
    shift_term = jnp.sum(grad_out, axis=1)
    centred = d_normed - jnp.mean(d_normed, axis=-1, keepdims=True)
    d_inputs = inv_std * (centred - normed * jnp.mean(d_normed * normed, axis=-1, keepdims=True))
    return (d_inputs, gain_term, scale_term, shift_term)


def rotary_tables(positions):
    half_dim = HEAD_DIM // 2
    frequency = jnp.exp(
        -jnp.log(10000.0) * jnp.arange(half_dim, dtype=jnp.float32) * 2.0 / HEAD_DIM
    )
    angles = positions[:, None] * frequency[None, :]
    return (jnp.cos(angles)[:, None, :], jnp.sin(angles)[:, None, :])


def rotate(values, cos_table, sin_table):
    half_dim = values.shape[-1] // 2
    first_half = values[..., :half_dim]
    second_half = values[..., half_dim:]
    return jnp.concatenate(
        [
            first_half * cos_table - second_half * sin_table,
            second_half * cos_table + first_half * sin_table,
        ],
        axis=-1,
    )


def unrotate(grads, cos_table, sin_table):
    half_dim = grads.shape[-1] // 2
    first_half = grads[..., :half_dim]
    second_half = grads[..., half_dim:]
    return jnp.concatenate(
        [
            first_half * cos_table + second_half * sin_table,
            second_half * cos_table - first_half * sin_table,
        ],
        axis=-1,
    )


def gelu_tanh(values):
    return jax.nn.gelu(values, approximate=True)


def split_pairs(block):
    batch_seqs = block.shape[0]
    key_rows = block.shape[1]
    heads_here = block.shape[3] // HEAD_DIM
    keys = block[:, :, 0].reshape(batch_seqs, key_rows, heads_here, HEAD_DIM)
    values = block[:, :, 1].reshape(batch_seqs, key_rows, heads_here, HEAD_DIM)
    return (keys, values)


def split_blocks(piece, shard_rows):
    count = piece.shape[1] // shard_rows
    group = math.gcd(count, shard_group)
    steps = count // group
    shaped = piece.reshape((piece.shape[0], steps, group * shard_rows) + piece.shape[2:])
    return jnp.moveaxis(shaped, 1, 0)


def forward_block(query_heads, carry, block):
    top, totals, accum = carry
    keys, values = split_pairs(block)
    scores = jnp.einsum(
        "shqd,skhd->shqk", query_heads, keys, preferred_element_type=jnp.float32
    ) * HEAD_DIM ** (-0.5)
    new_top = jnp.maximum(top, jnp.max(scores, axis=-1))
    probs = jnp.exp(scores - new_top[..., None])
    fade = jnp.exp(top - new_top)
    totals = totals * fade + jnp.sum(probs, axis=-1)
    accum = accum * fade[..., None] + jnp.einsum(
        "shqk,skhd->shqd", probs.astype(jnp.bfloat16), values, preferred_element_type=jnp.float32
    )
    return (new_top, totals, accum)


def shards(inputs, conditioning, w_ada, w_qkv, w_out, w_up, w_down, gain_one, gain_two, cotangent):
    gathered = (
        lax.all_gather(w_ada, ("ulysses", "blk"), axis=1, tiled=True),
        lax.all_gather(w_qkv, ("ulysses", "blk"), axis=0, tiled=True),
        lax.all_gather(w_out, ("ulysses", "blk"), axis=0, tiled=True),
        lax.all_gather(w_up, ("ulysses", "blk"), axis=0, tiled=True),
        lax.all_gather(w_down, ("ulysses", "blk"), axis=0, tiled=True),
        lax.all_gather(gain_one, ("ulysses", "blk"), axis=0, tiled=True),
        lax.all_gather(gain_two, ("ulysses", "blk"), axis=0, tiled=True),
    )
    ada_full, qkv_full, out_full, up_full, down_full = (
        gathered[0],
        gathered[1],
        gathered[2],
        gathered[3],
        gathered[4],
    )
    gain_first = gathered[5].astype(jnp.float32)
    gain_second = gathered[6].astype(jnp.float32)
    rows = inputs.shape[1]
    width = inputs.shape[2]
    device_index = lax.axis_index(("ulysses", "blk"))
    positions = (device_index * rows + jnp.arange(rows, dtype=jnp.int32)).astype(jnp.float32)
    cos_table, sin_table = rotary_tables(positions)
    score_scale = HEAD_DIM ** (-0.5)
    ada_cols = w_ada.shape[1]
    grad_shapes = (
        w_qkv.shape,
        w_out.shape,
        w_up.shape,
        w_down.shape,
        gain_one.shape,
        gain_two.shape,
    )
    grad_totals = tuple((jnp.zeros(shape, jnp.float32) for shape in grad_shapes))
    ada_grad = jnp.zeros(w_ada.shape, jnp.float32)
    outputs_list = []
    input_grads = []
    cond_grads = []
    for micro_step in range(MICRO):
        offset = micro_step * SEQ_MB
        seq_inputs = inputs[offset : offset + SEQ_MB].astype(jnp.float32)
        cond_rows = conditioning[offset : offset + SEQ_MB]
        modulation = jnp.dot(cond_rows, ada_full, preferred_element_type=jnp.float32)
        pieces = [p[:, None, :] for p in jnp.split(modulation, 6, axis=1)]
        shift_one, scale_one, gate_one, shift_two, scale_two, gate_two = pieces
        normed_one, inv_one = normalize(seq_inputs)
        first_in = (normed_one * gain_first * (1.0 + scale_one) + shift_one).astype(jnp.bfloat16)
        projected = jnp.dot(first_in, qkv_full, preferred_element_type=jnp.float32)
        projected = projected.reshape(SEQ_MB, rows, 3, HEADS, HEAD_DIM)
        rot_query = rotate(projected[:, :, 0], cos_table, sin_table)
        rot_key = rotate(projected[:, :, 1], cos_table, sin_table)
        packed = jnp.stack([rot_query, rot_key, projected[:, :, 2]], axis=2).reshape(
            SEQ_MB, rows, 3, width
        )
        regrouped = lax.all_to_all(
            packed.astype(jnp.bfloat16), "ulysses", split_axis=3, concat_axis=1, tiled=True
        )
        query_rows = regrouped.shape[1]
        head_width = regrouped.shape[3]
        local_heads = head_width // HEAD_DIM
        query_heads = (
            regrouped[:, :, 0]
            .reshape(SEQ_MB, query_rows, local_heads, HEAD_DIM)
            .transpose(0, 2, 1, 3)
        )
        kv_local = regrouped[:, :, 1:]
        start_carry = (
            jnp.full((SEQ_MB, local_heads, query_rows), -1e30, jnp.float32),
            jnp.zeros((SEQ_MB, local_heads, query_rows), jnp.float32),
            jnp.zeros((SEQ_MB, local_heads, query_rows, HEAD_DIM), jnp.float32),
        )

        def scan_forward(carry, block):
            return (forward_block(query_heads, carry, block), None)

        result, _ = lax.scan(
            scan_forward,
            start_carry,
            split_blocks(lax.all_gather(kv_local, "blk", axis=1, tiled=True), query_rows),
        )
        carry = result
        top, totals, accum = carry
        attn_heads = accum / totals[..., None]
        log_total = top + jnp.log(totals)
        attn_tokens = (
            attn_heads.astype(jnp.bfloat16)
            .transpose(0, 2, 1, 3)
            .reshape(SEQ_MB, query_rows, head_width)
        )
        attended = lax.all_to_all(attn_tokens, "ulysses", split_axis=1, concat_axis=2, tiled=True)
        branch = jnp.dot(attended, out_full, preferred_element_type=jnp.float32)
        middle = seq_inputs + gate_one * branch
        normed_two, inv_two = normalize(middle)
        second_in = (normed_two * gain_second * (1.0 + scale_two) + shift_two).astype(jnp.bfloat16)
        raised = jnp.dot(second_in, up_full, preferred_element_type=jnp.float32)
        hidden, gelu_pull = jax.vjp(gelu_tanh, raised)
        hidden_low = hidden.astype(jnp.bfloat16)
        lowered = jnp.dot(hidden_low, down_full, preferred_element_type=jnp.float32)
        outputs_list.append(middle + gate_two * lowered)
        grad_out = cotangent[offset : offset + SEQ_MB].astype(jnp.float32)
        d_lowered = (gate_two * grad_out).astype(jnp.bfloat16)
        d_gate_two = jnp.sum(grad_out * lowered, axis=1)
        down_term = jnp.einsum(
            "srf,srd->fd", hidden_low, d_lowered, preferred_element_type=jnp.float32
        )
        d_hidden = jnp.einsum(
            "srd,fd->srf", d_lowered, down_full, preferred_element_type=jnp.float32
        )
        (d_raised,) = gelu_pull(d_hidden)
        d_raised_low = d_raised.astype(jnp.bfloat16)
        up_term = jnp.einsum(
            "srd,srf->df", second_in, d_raised_low, preferred_element_type=jnp.float32
        )
        d_second = jnp.einsum(
            "srf,df->srd", d_raised_low, up_full, preferred_element_type=jnp.float32
        )
        d_norm_two, gain_two_term, d_scale_two, d_shift_two = norm_back(
            d_second, normed_two, inv_two, gain_second, scale_two
        )
        d_middle = grad_out + d_norm_two
        d_gate_one = jnp.sum(d_middle * branch, axis=1)
        d_branch = (gate_one * d_middle).astype(jnp.bfloat16)
        out_term = jnp.einsum("srd,sre->de", attended, d_branch, preferred_element_type=jnp.float32)
        d_attended = jnp.einsum(
            "sre,de->srd", d_branch, out_full, preferred_element_type=jnp.float32
        ).astype(jnp.bfloat16)
        d_attn_rows = lax.all_to_all(d_attended, "ulysses", split_axis=2, concat_axis=1, tiled=True)
        d_attn_heads = d_attn_rows.reshape(SEQ_MB, query_rows, local_heads, HEAD_DIM).transpose(
            0, 2, 1, 3
        )
        delta = jnp.sum(d_attn_heads.astype(jnp.float32) * attn_heads, axis=-1)
        all_pairs = lax.all_gather(kv_local, "blk", axis=1, tiled=True)

        def back_step(d_query, block):
            keys, values = split_pairs(block)
            scores = (
                jnp.einsum("shqd,skhd->shqk", query_heads, keys, preferred_element_type=jnp.float32)
                * score_scale
            )
            probs = jnp.exp(scores - log_total[..., None])
            d_probs = jnp.einsum(
                "shqd,skhd->shqk", d_attn_heads, values, preferred_element_type=jnp.float32
            )
            d_scores = (probs * (d_probs - delta[..., None])).astype(jnp.bfloat16)
            d_query = (
                d_query
                + jnp.einsum("shqk,skhd->shqd", d_scores, keys, preferred_element_type=jnp.float32)
                * score_scale
            )
            d_keys = (
                jnp.einsum(
                    "shqk,shqd->skhd", d_scores, query_heads, preferred_element_type=jnp.float32
                )
                * score_scale
            )
            d_values = jnp.einsum(
                "shqk,shqd->skhd",
                probs.astype(jnp.bfloat16),
                d_attn_heads,
                preferred_element_type=jnp.float32,
            )
            key_rows = block.shape[1]
            pair = jnp.stack(
                [
                    d_keys.reshape(SEQ_MB, key_rows, head_width),
                    d_values.reshape(SEQ_MB, key_rows, head_width),
                ],
                axis=2,
            )
            return (d_query, pair)

        query_zero = jnp.zeros((SEQ_MB, local_heads, query_rows, HEAD_DIM), jnp.float32)
        d_query, pair_terms = lax.scan(back_step, query_zero, split_blocks(all_pairs, query_rows))
        pair_terms = jnp.moveaxis(pair_terms, 0, 1)
        pair_terms = pair_terms.reshape(
            SEQ_MB, pair_terms.shape[1] * pair_terms.shape[2], 2, head_width
        )
        pair_sums = lax.psum_scatter(pair_terms, "blk", scatter_dimension=1, tiled=True)
        query_grad = d_query.transpose(0, 2, 1, 3).reshape(SEQ_MB, query_rows, 1, head_width)
        d_packed = jnp.concatenate([query_grad, pair_sums], axis=2).astype(jnp.bfloat16)
        d_local = lax.all_to_all(d_packed, "ulysses", split_axis=1, concat_axis=3, tiled=True)
        d_local = d_local.astype(jnp.float32).reshape(SEQ_MB, rows, 3, HEADS, HEAD_DIM)
        d_projected = (
            jnp.stack(
                [
                    unrotate(d_local[:, :, 0], cos_table, sin_table),
                    unrotate(d_local[:, :, 1], cos_table, sin_table),
                    d_local[:, :, 2],
                ],
                axis=2,
            )
            .reshape(SEQ_MB, rows, 3 * width)
            .astype(jnp.bfloat16)
        )
        qkv_term = jnp.einsum(
            "srd,sre->de", first_in, d_projected, preferred_element_type=jnp.float32
        )
        d_first = jnp.einsum(
            "sre,de->srd", d_projected, qkv_full, preferred_element_type=jnp.float32
        )
        d_norm_one, gain_one_term, d_scale_one, d_shift_one = norm_back(
            d_first, normed_one, inv_one, gain_first, scale_one
        )
        input_grads.append(d_middle + d_norm_one)
        mod_local = jnp.concatenate(
            [d_shift_one, d_scale_one, d_gate_one, d_shift_two, d_scale_two, d_gate_two], axis=1
        )
        mod_total = lax.psum(mod_local, ("ulysses", "blk"))
        mod_low = mod_total.astype(jnp.bfloat16)
        cond_grads.append(
            jnp.einsum("sm,cm->sc", mod_low, ada_full, preferred_element_type=jnp.float32)
        )
        mod_part = lax.dynamic_slice_in_dim(mod_low, device_index * ada_cols, ada_cols, 1)
        ada_grad = ada_grad + jnp.einsum(
            "sc,sm->cm", cond_rows, mod_part, preferred_element_type=jnp.float32
        )
        terms = (qkv_term, out_term, up_term, down_term, gain_one_term, gain_two_term)
        reduced = (
            lax.psum_scatter(terms[0], ("ulysses", "blk"), scatter_dimension=0, tiled=True),
            lax.psum_scatter(terms[1], ("ulysses", "blk"), scatter_dimension=0, tiled=True),
            lax.psum_scatter(terms[2], ("ulysses", "blk"), scatter_dimension=0, tiled=True),
            lax.psum_scatter(terms[3], ("ulysses", "blk"), scatter_dimension=0, tiled=True),
            lax.psum_scatter(terms[4], ("ulysses", "blk"), scatter_dimension=0, tiled=True),
            lax.psum_scatter(terms[5], ("ulysses", "blk"), scatter_dimension=0, tiled=True),
        )
        grad_totals = tuple((a + b for a, b in zip(grad_totals, reduced)))
    output = jnp.concatenate(outputs_list, axis=0)
    inputs_grad = jnp.concatenate(input_grads, axis=0)
    conditioning_grad = jnp.concatenate(cond_grads, axis=0)
    return (
        output,
        inputs_grad,
        conditioning_grad,
        ada_grad,
        grad_totals[0],
        grad_totals[1],
        grad_totals[2],
        grad_totals[3],
        grad_totals[4],
        grad_totals[5],
    )


def dot_nt(left, right):
    return lax.dot_general(left, right, (((1,), (1,)), ((), ())), preferred_element_type=f32)


def dot_tn(left, right):
    return lax.dot_general(left, right, (((0,), (0,)), ((), ())), preferred_element_type=f32)


def row_norm(values):
    centered = values - jnp.mean(values, axis=1, keepdims=True)
    inv_std = lax.rsqrt(jnp.mean(centered * centered, axis=1, keepdims=True) + eps_norm)
    return centered * inv_std, inv_std


def row_back(grads, normed, inv_std):
    return inv_std * (
        grads
        - jnp.mean(grads, axis=1, keepdims=True)
        - normed * jnp.mean(grads * normed, axis=1, keepdims=True)
    )


def turn(values, cos_ref, sin_ref, sign):
    lane = lax.broadcasted_iota(jnp.int32, values.shape, 1) % HEAD_DIM
    swapped = jnp.where(
        lane < HEAD_DIM // 2, pltpu.roll(values, 128 - HEAD_DIM // 2, 1), pltpu.roll(values, HEAD_DIM // 2, 1)
    )
    return values * cos_ref[...] + sign * (swapped * sin_ref[...])


def mod_row(table_ref, s, i):
    width = table_ref.shape[1] // 7
    return table_ref[s : s + 1, i * width : (i + 1) * width]


EXTRA = 48


def split_low(values):
    high = values.astype(bf16).astype(f32)
    return high, values - high


def extra_rows(mods, gains, store):
    mods = jnp.concatenate(split_low(mods), axis=0)
    for i in range(3):
        store(i * mods.shape[0], mods[:, EXTRA * i : EXTRA * (i + 1)])
    store(3 * mods.shape[0], jnp.concatenate(split_low(gains), axis=0))


def join_rows(rows, i, seqs):
    return rows[2 * seqs * i : 2 * seqs * i + seqs] + rows[2 * seqs * i + seqs : 2 * seqs * (i + 1)]


def pack_kernel(
    x_ref, g_ref, qkv_ref, ada_ref, cond_ref, one_ref, two_ref, up_ref, xc_ref, piece_ref, ext_ref,
):
    n_u, block, cols = piece_ref.shape
    xc_ref[0] = x_ref[...]
    xc_ref[1] = g_ref[...]
    width = qkv_ref.shape[1] // 3
    ff = up_ref.shape[1] // n_u
    heads = width // n_u // HEAD_DIM
    ext_ref[...] = jnp.zeros_like(ext_ref)
    mods = dot_nt(cond_ref[...], ada_ref[...])
    gains = jnp.concatenate([one_ref[...], two_ref[...]], axis=0).astype(f32)

    def store(row, value):
        ext_ref[row : row + value.shape[0], : value.shape[1]] = value

    extra_rows(mods, gains, store)
    extra = ext_ref[...].astype(bf16)
    for i in range(n_u):
        pieces = []
        for h in range(heads):
            at = (i * heads + h) * HEAD_DIM
            pieces += [qkv_ref[:, at : at + HEAD_DIM], qkv_ref[:, width + at : width + at + HEAD_DIM]]
        at = 2 * width + i * heads * HEAD_DIM
        pieces += [qkv_ref[:, at : at + heads * HEAD_DIM], extra]
        piece_ref[i, :, : cols - ff] = jnp.concatenate(pieces, axis=1)
        piece_ref[i, :, cols - ff :] = up_ref[:, i * ff : (i + 1) * ff]


def first_kernel(
    at_ref, xg_ref, cos_ref, sin_ref, a0, a1, a2, a3, a4, a5, a6, a7,
    chunk_ref, first_ref, table_ref, w_ref, wide_ref,
):
    u, b = at_ref[0], at_ref[1]
    n_u, _, seqs, rows, width = xg_ref.shape
    span = n_u * rows
    cols = w_ref.shape[1]
    heads = cols // 192
    block = width // 32
    for i, part_ref in enumerate((a0, a1, a2, a3, a4, a5, a6, a7)):
        there = b ^ i
        for j in range(n_u):
            start = pl.multiple_of((j * 8 + there) * block, 8)
            wide_ref[pl.ds(start, block), :] = part_ref[j * block : (j + 1) * block, :].astype(f32)
    w_ref[...] = wide_ref[:, :cols].astype(bf16)
    pieces, gains = [], []
    for d in range(32):
        part = wide_ref[d * block : (d + 1) * block, cols:]
        pieces += [join_rows(part, i, seqs)[:, :EXTRA] for i in range(3)]
        gains.append(join_rows(part, 3, seqs)[:, :block])
    table_ref[...] = jnp.concatenate(pieces + gains, axis=1)
    gain = mod_row(table_ref, 0, 6)
    zero = jnp.zeros(chunk_ref.shape[1:], bf16)
    chunk_ref[0] = zero
    chunk_ref[chunk_ref.shape[0] - 1] = zero
    for s in range(seqs):
        factor = gain * (1.0 + mod_row(table_ref, s, 1))
        for m in range(n_u):
            normed, _ = row_norm(xg_ref[u ^ m, 0, s].astype(f32))
            first = normed * factor + mod_row(table_ref, s, 0)
            first_ref[s * span + m * rows : s * span + (m + 1) * rows, :] = first.astype(bf16)
        projected = DOT(first_ref[s * span : (s + 1) * span, :], w_ref[...])
        for h in range(heads):
            pair = 1 + s * heads + h
            both = turn(projected[:, 128 * h : 128 * (h + 1)], cos_ref, sin_ref, 1.0)
            chunk_ref[pair, :span, :] = both.astype(bf16)
            v = projected[:, 128 * heads + 64 * h : 128 * heads + 64 * (h + 1)].astype(bf16)
            chunk_ref[pair, span:, :] = jnp.concatenate([v[: span // 2], v[span // 2 :]], axis=1)


def unpack_tokens(t_ref, s, h, heads):
    half = t_ref[1 + s * heads + h]
    return jnp.concatenate([half[:, :HEAD_DIM], half[:, HEAD_DIM:]], axis=0)


def store_parts(send_ref, keep_ref, part, s, rows):
    for m in range(4):
        block = part[m * rows : (m + 1) * rows]
        if m % 2:
            send_ref[m // 2, s] = block.astype(bf16)
        else:
            keep_ref[m // 2, s] = block.astype(bf16)


def out_kernel(
    at_ref, t_ref, a0, a1, a2, a3, a4, a5, a6, a7, att_ref, send_ref, keep_ref, w_ref, wide_ref,
):
    _, seqs, rows, _ = send_ref.shape
    block = w_ref.shape[0] // 8
    low = a0.shape[0] - block
    for i, part_ref in enumerate((a0, a1, a2, a3, a4, a5, a6, a7)):
        start = pl.multiple_of((at_ref[1] ^ i) * block, 8)
        wide_ref[pl.ds(start, block), :] = part_ref[low:, :].astype(f32)
    w_ref[...] = wide_ref[...].astype(bf16)
    heads = w_ref.shape[0] // HEAD_DIM
    span = 4 * rows
    for s in range(seqs):
        att = jnp.concatenate([unpack_tokens(t_ref, s, h, heads) for h in range(heads)], axis=1)
        att_ref[s * span : (s + 1) * span, :] = att
        store_parts(send_ref, keep_ref, DOT(att, w_ref[...]), s, rows)


def block_of(own_ref, got_ref, m, s):
    return (got_ref if m % 2 else own_ref)[m // 2, s].astype(f32)


def middle_of(xg_ref, own_ref, got_ref, table_ref, u, m, s):
    return xg_ref[u ^ m, 0, s].astype(f32) + mod_row(table_ref, s, 2) * block_of(own_ref, got_ref, m, s)


def ff_kernel(
    at_ref, xg_ref, own_ref, got_ref, table_ref, a0, a1, a2, a3, a4, a5, a6, a7, b0, b1, b2, b3, b4, b5, b6, b7,
    lsend_ref, lkeep_ref, dsend_ref, dkeep_ref, sums_ref, ukeep_ref, usend_ref, wkeep_ref, wsend_ref,
    second_ref, hidden_ref, low_ref, raised_ref, normed_ref, wide_ref, up_ref, down_ref,
):
    u = at_ref[0]
    n_u, _, seqs, rows, width = xg_ref.shape
    span = n_u * rows
    gain = mod_row(table_ref, 1, 6)
    scale = math.sqrt(2.0 / math.pi)
    block = width // 32
    low = n_u * block
    u, b = at_ref[0], at_ref[1]
    ups, downs = (a0, a1, a2, a3, a4, a5, a6, a7), (b0, b1, b2, b3, b4, b5, b6, b7)
    for i, (part_ref, low_part_ref) in enumerate(zip(ups, downs)):
        there = b ^ i
        down_ref[pl.ds(pl.multiple_of(there * low, 32), low), :] = low_part_ref[:low, :]
        for j in range(n_u):
            start = pl.multiple_of((j * 8 + there) * block, 8)
            wide_ref[pl.ds(start, block), :] = part_ref[j * block : (j + 1) * block, :].astype(f32)
    up_ref[...] = wide_ref[...].astype(bf16)
    for s in range(seqs):
        at = slice(s * span, (s + 1) * span)
        factor = gain * (1.0 + mod_row(table_ref, s, 4))
        gate = mod_row(table_ref, s, 5)
        for m in range(n_u):
            here = slice(s * span + m * rows, s * span + (m + 1) * rows)
            normed, _ = row_norm(middle_of(xg_ref, own_ref, got_ref, table_ref, u, m, s))
            normed_ref[m * rows : (m + 1) * rows, :] = normed
            second_ref[here, :] = (normed * factor + mod_row(table_ref, s, 3)).astype(bf16)
            low_ref[here, :] = (gate * xg_ref[u ^ m, 1, s].astype(f32)).astype(bf16)
        raised = DOT(second_ref[at, :], up_ref[...])
        d_hidden = dot_nt(low_ref[at, :], down_ref[...])
        square = raised * raised
        t = jnp.tanh(scale * raised * (1.0 + 0.044715 * square))
        hidden_ref[at, :] = (0.5 * raised * (1.0 + t)).astype(bf16)
        slope = 0.5 * (1.0 + t) + 0.5 * raised * (1.0 - t * t) * (scale * (1.0 + 3.0 * 0.044715 * square))
        raised_ref[at, :] = (d_hidden * slope).astype(bf16)
        d_second = dot_nt(raised_ref[at, :], up_ref[...])
        store_parts(dsend_ref, dkeep_ref, d_second, s, rows)
        lowered = DOT(hidden_ref[at, :], down_ref[...])
        store_parts(lsend_ref, lkeep_ref, lowered, s, rows)
        sums_ref[s, 0:1, :] = jnp.sum(d_second, axis=0, keepdims=True)
        sums_ref[s, 1:2, :] = jnp.sum(d_second * normed_ref[...], axis=0, keepdims=True)
        gated = jnp.zeros((1, width), f32)
        for m in range(n_u):
            grad = xg_ref[u ^ m, 1, s].astype(f32)
            gated = gated + jnp.sum(grad * lowered[m * rows : (m + 1) * rows], axis=0, keepdims=True)
        sums_ref[s, 2:3, :] = gated
    n_z, side = ukeep_ref.shape[0], b % 2
    wide_ref[...] = dot_tn(hidden_ref[...], low_ref[...])
    for y, out_ref in enumerate((wkeep_ref, wsend_ref)):
        for z in range(n_z):
            start = pl.multiple_of((2 * z + (side ^ y)) * low, 32)
            out_ref[z] = wide_ref[pl.ds(start, low), :].astype(bf16)
    wide_ref[...] = dot_tn(second_ref[...], raised_ref[...])
    for y, out_ref in enumerate((ukeep_ref, usend_ref)):
        for z in range(n_z):
            for i in range(n_u):
                start = pl.multiple_of(((u ^ i) * 2 * n_z + 2 * z + (side ^ y)) * block, 8)
                out_ref[z, i] = wide_ref[pl.ds(start, block), :].astype(bf16)


def middle_back_kernel(
    at_ref, xg_ref, own_ref, got_ref, down_ref, dgot_ref, table_ref, w_ref, att_ref,
    chunk_ref, dmid_ref, gate_ref, okeep_ref, osend_ref, branch_ref, outs_ref,
):
    u = at_ref[0]
    n_u, _, seqs, rows, width = xg_ref.shape
    span = n_u * rows
    heads = w_ref.shape[0] // HEAD_DIM
    gain = mod_row(table_ref, 1, 6)
    zero = jnp.zeros(chunk_ref.shape[1:], bf16)
    chunk_ref[0] = zero
    chunk_ref[chunk_ref.shape[0] - 1] = zero
    for s in range(seqs):
        at = slice(s * span, (s + 1) * span)
        factor = gain * (1.0 + mod_row(table_ref, s, 4))
        gate = mod_row(table_ref, s, 2)
        for m in range(n_u):
            normed, inv_std = row_norm(middle_of(xg_ref, own_ref, got_ref, table_ref, u, m, s))
            grads = block_of(down_ref, dgot_ref, m, s) * factor
            d_middle = xg_ref[u ^ m, 1, s].astype(f32) + row_back(grads, normed, inv_std)
            branch_ref[s * span + m * rows : s * span + (m + 1) * rows, :] = (gate * d_middle).astype(bf16)
            if m == 0:
                dmid_ref[s] = d_middle
                gate_ref[s] = jnp.sum(d_middle * own_ref[0, s].astype(f32), axis=0, keepdims=True)
        d_att = dot_nt(branch_ref[at, :], w_ref[...]).astype(bf16)
        for h in range(heads):
            d = d_att[:, HEAD_DIM * h : HEAD_DIM * (h + 1)]
            chunk_ref[1 + s * heads + h] = jnp.concatenate([d[: span // 2], d[span // 2 :]], axis=1)
    n_z, block, _ = okeep_ref.shape
    outs_ref[...] = dot_tn(att_ref[...], branch_ref[...])
    for y, out_ref in enumerate((okeep_ref, osend_ref)):
        for z in range(n_z):
            start = pl.multiple_of((at_ref[1] ^ (2 * z + y)) * block, 8)
            out_ref[z] = outs_ref[pl.ds(start, block), :].astype(bf16)


def first_back_kernel(
    at_ref, t_ref, xg_ref, table_ref, cos_ref, sin_ref, w_ref, first_ref, gate_ref, two_ref,
    send_ref, keep_ref, blocks_ref, proj_ref, normed_ref, sums_ref, ext_ref, both_ref,
):
    u = at_ref[0]
    n_u, _, seqs, rows, width = xg_ref.shape
    span = n_u * rows
    cols = w_ref.shape[1]
    heads = cols // 192
    gain_grads = [jnp.zeros((1, width), f32)] * 2
    total, block, _ = blocks_ref.shape
    for s in range(seqs):
        at = slice(s * span, (s + 1) * span)
        for h in range(heads):
            pair = t_ref[1 + s * heads + h]
            both = turn(pair[:span].astype(f32), cos_ref, sin_ref, -1.0)
            proj_ref[at, 128 * h : 128 * (h + 1)] = both.astype(bf16)
            v = pair[span:]
            proj_ref[at, 128 * heads + 64 * h : 128 * heads + 64 * (h + 1)] = jnp.concatenate(
                [v[:, :HEAD_DIM], v[:, HEAD_DIM:]], axis=0
            )
        d_first = dot_nt(proj_ref[at, :], w_ref[...])
        store_parts(send_ref, keep_ref, d_first, s, rows)
        for m in range(n_u):
            normed, _ = row_norm(xg_ref[u ^ m, 0, s].astype(f32))
            normed_ref[m * rows : (m + 1) * rows, :] = normed
        dots = [jnp.sum(d_first * normed_ref[...], axis=0, keepdims=True), two_ref[s, 1:2, :]]
        for i in range(2):
            gain_grads[i] = gain_grads[i] + dots[i] * (1.0 + mod_row(table_ref, s, 1 + 3 * i))
        rows_out = [
            jnp.sum(d_first, axis=0, keepdims=True),
            dots[0] * mod_row(table_ref, 0, 6),
            gate_ref[s],
            two_ref[s, 0:1, :],
            dots[1] * mod_row(table_ref, 1, 6),
            two_ref[s, 2:3, :],
        ]
        for i, row in enumerate(rows_out):
            sums_ref[s : s + 1, i * width : (i + 1) * width] = row
    for i in range(2):
        sums_ref[i : i + 1, 6 * width :] = gain_grads[i]
    ext_ref[...] = jnp.zeros_like(ext_ref)
    high = sums_ref[...].astype(bf16).astype(f32)
    both_ref[...] = jnp.concatenate([high, sums_ref[...] - high], axis=0)
    lines = 2 * seqs
    for d in range(total):
        for i in range(3):
            at = 3 * EXTRA * d + EXTRA * i
            ext_ref[d * block + lines * i : d * block + lines * (i + 1), :EXTRA] = both_ref[:, at : at + EXTRA]
        at = 6 * width + block * d
        ext_ref[d * block + 3 * lines : d * block + 4 * lines, :block] = both_ref[:, at : at + block]
    grads = dot_tn(first_ref[...], proj_ref[...])
    for i in range(total):
        at = slice(i * block, (i + 1) * block)
        blocks_ref[i, :, :cols] = grads[at].astype(bf16)
        blocks_ref[i, :, cols:] = ext_ref[at].astype(bf16)


def row_grad_kernel(at_ref, raw_ref, p0, p1, p2, p3, ada_ref, cond_ref, qkv_ref, up_ref, part_ref, adag_ref, gain_ref, mod_ref):
    u = at_ref[0]
    total, block, cols = raw_ref.shape
    cols = cols - HEAD_DIM
    n_u = 4
    n_b = total // n_u
    heads = cols // 192
    width = qkv_ref.shape[1] // 3
    seqs = mod_ref.shape[0]
    extra = jnp.zeros((block, HEAD_DIM), f32)
    for i in range(n_u):
        part = raw_ref[i * n_b].astype(f32)
        for j in range(1, n_b):
            part = part + raw_ref[i * n_b + j].astype(f32)
        extra = extra + part[:, cols:]
        for h in range(heads):
            to = (i * heads + h) * HEAD_DIM
            qkv_ref[:, to : to + HEAD_DIM] = part[:, 128 * h : 128 * h + HEAD_DIM]
            qkv_ref[:, width + to : width + to + HEAD_DIM] = part[:, 128 * h + HEAD_DIM : 128 * (h + 1)]
        at = i * heads * HEAD_DIM
        qkv_ref[:, 2 * width + at : 2 * width + at + heads * HEAD_DIM] = part[:, 128 * heads : cols]
    mod_ref[...] = jnp.concatenate([join_rows(extra, i, seqs)[:, :EXTRA] for i in range(3)], axis=1)
    gain_ref[...] = join_rows(extra, 3, seqs)[:, :block]
    mods = mod_ref[...].astype(bf16)
    grads = DOT(mods, ada_ref[...])
    for i in range(total):
        part_ref[i] = grads
    adag_ref[...] = dot_tn(mods, cond_ref[...])
    cols = up_ref.shape[1] // n_u
    for i, piece_ref in enumerate((p0, p1, p2, p3)):
        up_ref[:, pl.ds(pl.multiple_of((u ^ i) * cols, 128), cols)] = piece_ref[...]


def input_grad_kernel(x_ref, near_ref, got_ref, dmid_ref, table_ref, out_ref):
    seqs = x_ref.shape[0]
    for s in range(seqs):
        factor = mod_row(table_ref, 0, 6) * (1.0 + mod_row(table_ref, s, 1))
        normed, inv_std = row_norm(x_ref[s].astype(f32))
        grads = (near_ref[s].astype(f32) + got_ref[s].astype(f32)) * factor
        out_ref[s] = dmid_ref[s] + row_back(grads, normed, inv_std)


def call(kernel, name, outs, scratch, flops, *args, limit=16, staged=()):
    count = len(args)
    specs = [
        pl.BlockSpec(
            memory_space=pltpu.SMEM if a.dtype == jnp.int32 else pltpu.HBM if i in staged else pltpu.VMEM
        )
        for i, a in enumerate(args)
    ]
    size = sum(math.prod(a.shape) * a.dtype.itemsize for a in args)
    size += sum(math.prod(shape) * jnp.dtype(dtype).itemsize for shape, dtype in outs)
    shapes = [pltpu.VMEM(*s) for s in scratch]
    body = kernel
    if staged:
        shapes = [pltpu.VMEM(args[i].shape, args[i].dtype) for i in staged] + [
            pltpu.SemaphoreType.DMA((len(staged),))
        ] + shapes

        def body(*refs):
            ins, rest = list(refs[:count]), refs[count:]
            out_refs, held = rest[: len(outs)], rest[len(outs) :]
            sems = held[len(staged)]
            copies = []
            for j, i in enumerate(staged):
                copies.append(pltpu.make_async_copy(ins[i], held[j], sems.at[j]))
                ins[i] = held[j]
            for copy in copies:
                copy.start()
            for copy in copies:
                copy.wait()
            kernel(*ins, *out_refs, *held[len(staged) + 1 :])

    return pl.pallas_call(
        body,
        out_shape=tuple(jax.ShapeDtypeStruct(shape, dtype) for shape, dtype in outs),
        in_specs=specs,
        out_specs=tuple(pl.BlockSpec(memory_space=pltpu.VMEM) for _ in outs),
        scratch_shapes=shapes,
        cost_estimate=pl.CostEstimate(flops=int(flops) // 1000, bytes_accessed=int(size) // 1000, transcendentals=0),
        compiler_params=pltpu.CompilerParams(vmem_limit_bytes=limit << 20),
        name=name,
    )(*args)


def fits_tp(mesh):
    ulysses, blk = mesh.shape["ulysses"], mesh.shape["blk"]
    return ulysses == 4 and blk == 8 and HEADS % ulysses == 0


def swap_u(values, mask):
    return lax.ppermute(values, "ulysses", [(i, i ^ mask) for i in range(4)])


def swap_b(values, mask):
    return lax.ppermute(values, "blk", [(i, i ^ mask) for i in range(8)])


def scatter_z(blocks):
    groups = [[2 * z + y for z in range(4)] for y in range(2)]
    return lax.psum_scatter(blocks, "blk", scatter_dimension=0, axis_index_groups=groups, tiled=True)[0]


def exchange(blocks, axis):
    return lax.all_to_all(blocks, axis, split_axis=0, concat_axis=0, tiled=True)


def half_sum(send, keep):
    return (keep.astype(f32) + swap_u(send, 1).astype(f32)).astype(bf16)


def pair_sum(left, right):
    return (left.astype(f32) + right.astype(f32)).astype(bf16)


def along_z(values):
    return [values] + [swap_b(values, 2 * m) for m in (1, 2, 3)]


def along_y(parts):
    out = []
    for part in parts:
        out += [part, swap_b(part, 1)]
    return out


def sum_z(half):
    total = half[0]
    for m in (1, 2, 3):
        total = total + swap_b(half[m].astype(bf16), 2 * m).astype(f32)
    return total


def tp_shards(inputs, conditioning, w_ada, w_qkv, w_out, w_up, w_down, gain_one, gain_two, cotangent):
    n_u, n_b = 4, 8
    n_all = n_u * n_b
    everywhere = ("ulysses", "blk")
    seqs, rows, width = inputs.shape
    u = lax.axis_index("ulysses")
    b = lax.axis_index("blk")
    at = jnp.stack([u, b]).astype(jnp.int32)
    heads = HEADS // n_u
    head_width = heads * HEAD_DIM
    cols = 3 * head_width
    w_rows, down_rows = w_qkv.shape[0], w_down.shape[0]
    ff_local = w_up.shape[1] // n_u
    span = n_u * rows
    tokens = seqs * span

    both, pieces = call(
        pack_kernel, "pack",
        [((2,) + inputs.shape, bf16), ((n_u, w_rows, cols + HEAD_DIM + ff_local), bf16)],
        [((w_rows, HEAD_DIM), f32)], 0,
        inputs, cotangent, w_qkv, w_ada.T, conditioning, gain_one[None], gain_two[None], w_up,
        limit=60,
    )
    blocks = u ^ jnp.arange(n_u, dtype=jnp.int32)
    positions = ((blocks * n_b + b) * rows)[:, None] + jnp.arange(rows, dtype=jnp.int32)[None, :]
    cos_table, sin_table = rotary_tables(positions.reshape(-1).astype(f32))
    cos_table, sin_table = cos_table[:, 0], sin_table[:, 0]
    cos_table = jnp.concatenate([cos_table] * 4, axis=1)
    sin_table = jnp.concatenate([-sin_table, sin_table] * 2, axis=1)

    pieces, cos_table, sin_table, at = lax.optimization_barrier(
        (exchange(pieces, "ulysses"), cos_table, sin_table, at)
    )
    pieces = pieces.reshape(n_u * w_rows, cols + HEAD_DIM + ff_local)
    xg = lax.all_gather(both, "ulysses", axis=0, tiled=False)
    up_near = pieces[:, cols + HEAD_DIM :]
    down_z = along_z(jnp.concatenate([w_down, w_out], axis=0))
    pieces, down_z[1], down_z[2] = lax.optimization_barrier((pieces, down_z[1], down_z[2]))
    near = pieces[:, : cols + HEAD_DIM]
    rows_zy = along_y(along_z(near))

    chunks, first_in, table, w_qkv_u = call(
        first_kernel, "first",
        [((n_b, 3 * span // 2, 128), bf16), ((tokens, width), bf16), ((seqs, 7 * width), f32),
         ((width, cols), bf16)],
        [((width, cols + HEAD_DIM), f32)],
        2 * tokens * width * cols,
        at, xg, cos_table, sin_table, *rows_zy,
        limit=60,
    )
    chunks, down_z = lax.optimization_barrier((chunks, down_z))
    owned = exchange(chunks, "blk")
    down_zy = along_y(down_z)
    owned, up_near, down_zy[1], down_zy[3] = lax.optimization_barrier((owned, up_near, down_zy[1], down_zy[3]))
    up_z = along_z(up_near)
    attn_low, attn_full, log_total = attn_fwd(owned)
    part_shape = (2, seqs, rows, width)
    attn_low, up_z, down_zy = lax.optimization_barrier((attn_low, up_z, down_zy))
    attn_tokens = exchange(attn_low, "blk")
    up_zy = along_y(up_z[:1])
    attn_tokens, up_zy = lax.optimization_barrier((attn_tokens, up_zy))
    attended, send, keep, w_out_u = call(
        out_kernel, "out",
        [((tokens, head_width), bf16), (part_shape, bf16), (part_shape, bf16), ((head_width, width), bf16)],
        [((head_width, width), f32)],
        2 * tokens * width * head_width,
        at, attn_tokens, *down_zy,
    )

    half = half_sum(send, keep)
    across = swap_u(half, 2)
    up_zy = up_zy + along_y(up_z[1:])
    across, up_zy = lax.optimization_barrier((across, up_zy))
    own = pair_sum(half, across[::-1])
    got = swap_u(own, 1)
    lsend, lkeep, dsend, dkeep, sums_two, up_keep, up_send, down_keep, down_send = call(
        ff_kernel, "ff",
        [(part_shape, bf16), (part_shape, bf16), (part_shape, bf16), (part_shape, bf16), ((seqs, 3, width), f32)]
        + [((n_b // 2, n_u, w_rows, width), bf16)] * 2 + [((n_b // 2, down_rows, width), bf16)] * 2,
        [((tokens, width), bf16), ((tokens, ff_local), bf16), ((tokens, width), bf16), ((tokens, ff_local), bf16),
         ((span, width), f32), ((width, ff_local), f32), ((width, ff_local), bf16), ((ff_local, width), bf16)],
        12 * tokens * width * ff_local,
        at, xg, own, got, table, *up_zy, *down_zy,
        limit=60,
    )
    down_other, up_other = swap_b(down_send, 1), swap_b(up_send, 1)
    half = half_sum(dsend, dkeep)
    across = swap_u(half, 2)
    across, down_other = lax.optimization_barrier((across, down_other))
    down_grad = scatter_z(pair_sum(down_keep, down_other))
    d_own = pair_sum(half, across[::-1])
    d_got = swap_u(d_own, 1)
    d_chunks, d_middle, sum_gate, out_keep, out_send = call(
        middle_back_kernel, "middle_back",
        [((n_b, span // 2, 128), bf16), ((seqs, rows, width), f32), ((seqs, 1, width), f32)]
        + [((n_b // 2, w_rows, width), bf16)] * 2,
        [((tokens, width), bf16), ((head_width, width), f32)],
        4 * tokens * width * head_width,
        at, xg, own, got, d_own, d_got, table, w_out_u, attended,
        limit=60,
    )
    d_attn = exchange(d_chunks, "blk")
    out_other = swap_b(out_send, 1)
    up_low = pair_sum(up_keep, up_other)
    d_attn, up_low, out_other, down_grad = lax.optimization_barrier((d_attn, up_low, out_other, down_grad))
    up_sum = scatter_z(up_low)
    d_owned = attn_bwd(owned, d_attn, attn_full, log_total)
    d_owned, lsend, lkeep = lax.optimization_barrier((d_owned, lsend, lkeep))
    lhalf = half_sum(lsend, lkeep)
    lowered = lhalf[0].astype(f32) + swap_u(lhalf[1], 2).astype(f32)
    gates = table.reshape(2, 7, 1, width)
    output = inputs.astype(f32) + gates[:, 2] * own[0].astype(f32) + gates[:, 5] * lowered
    up_sum = up_sum.astype(f32)
    up_parts = [up_sum[0]] + [swap_u(up_sum[m], m) for m in (1, 2, 3)]
    d_tokens = exchange(d_owned, "blk")
    d_tokens, up_parts, down_grad, output = lax.optimization_barrier((d_tokens, up_parts, down_grad, output))

    send, keep, qkv_blocks = call(
        first_back_kernel, "first_back",
        [(part_shape, bf16), (part_shape, bf16), ((n_all, w_rows, cols + HEAD_DIM), bf16)],
        [((tokens, cols), bf16), ((span, width), f32), ((seqs, 7 * width), f32), ((width, HEAD_DIM), f32),
         ((2 * seqs, 7 * width), f32)],
        4 * tokens * width * cols,
        at, d_tokens, xg, table, cos_table, sin_table, w_qkv_u, first_in, sum_gate, sums_two,
        limit=60,
    )
    half = half_sum(send, keep)
    far = swap_u(half[1], 2)
    far, out_other = lax.optimization_barrier((far, out_other))
    out_grad = sum_z(out_keep.astype(f32) + out_other.astype(f32))
    inputs_grad, = call(
        input_grad_kernel, "input_grad",
        [((seqs, rows, width), f32)], [], 0,
        inputs, half[0], far, d_middle, table,
    )
    qkv_grad, up_grad, cond_part, ada_grad, gain_grads, _ = call(
        row_grad_kernel, "row_grad",
        [(w_qkv.shape, f32), (w_up.shape, f32), ((n_all,) + conditioning.shape, f32), (w_ada.shape[::-1], f32),
         ((2, w_rows), f32), ((seqs, w_ada.shape[1]), f32)],
        [], 0,
        at, exchange(qkv_blocks, everywhere), *up_parts, w_ada.T, conditioning,
        limit=6,
    )
    conditioning_grad = jnp.sum(exchange(cond_part, everywhere), axis=0)
    return (
        output,
        inputs_grad,
        conditioning_grad,
        ada_grad.T,
        qkv_grad,
        out_grad,
        up_grad,
        down_grad.astype(f32),
        gain_grads[0],
        gain_grads[1],
    )


def solution(mesh):
    body = tp_shards if fits_tp(mesh) else shards
    in_specs = (
        P(None, ("ulysses", "blk"), None),
        P(),
        P(None, ("ulysses", "blk")),
        P(("ulysses", "blk"), None),
        P(("ulysses", "blk"), None),
        P(("ulysses", "blk"), None),
        P(("ulysses", "blk"), None),
        P(("ulysses", "blk")),
        P(("ulysses", "blk")),
        P(None, ("ulysses", "blk"), None),
    )
    out_specs = (
        P(None, ("ulysses", "blk"), None),
        P(None, ("ulysses", "blk"), None),
        P(),
        P(None, ("ulysses", "blk")),
        P(("ulysses", "blk"), None),
        P(("ulysses", "blk"), None),
        P(("ulysses", "blk"), None),
        P(("ulysses", "blk"), None),
        P(("ulysses", "blk")),
        P(("ulysses", "blk")),
    )
    return jax.shard_map(body, mesh=mesh, in_specs=in_specs, out_specs=out_specs, check_vma=False)
```

```python
import functools
import math

import jax
import jax.numpy as jnp
from jax import lax
from jax.experimental import pallas as pl
from jax.experimental.pallas import tpu as pltpu
from jax.sharding import PartitionSpec as P

f32, bf16 = jnp.float32, jnp.bfloat16
DOT = functools.partial(jnp.dot, preferred_element_type=f32)

def attn_fwd_kernel(x_ref, o_ref, of_ref, lse_ref, kt_ref, v_ref):
    nb, rows3, _ = x_ref.shape
    half = rows3 // 3
    rows = 2 * half
    for j in range(nb):
        kt_ref[:, j * rows : (j + 1) * rows] = x_ref[j, :rows, 64:].T
        v_ref[j * rows : j * rows + half, :] = x_ref[j, rows:, :64]
        v_ref[j * rows + half : (j + 1) * rows, :] = x_ref[j, rows:, 64:]

    for j in range(0, nb, 2):
        q = x_ref[j : j + 2, :rows, :64].reshape(2 * rows, 64) * jnp.asarray(0.125, bf16)
        s = DOT(q, kt_ref[...])
        top = jnp.max(s, axis=1, keepdims=True)
        p = jnp.exp(s - top)
        total = jnp.sum(p, axis=1, keepdims=True)
        o = DOT(p.astype(bf16), v_ref[...]) / total
        lse = jnp.broadcast_to(top + jnp.log(total), (2 * rows, 128)).T
        for i in range(2):
            packed = jnp.concatenate(
                [o[i * rows : i * rows + half], o[i * rows + half : (i + 1) * rows]], axis=1
            )
            of_ref[j + i] = packed
            o_ref[j + i] = packed.astype(bf16)
            lse_ref[j + i] = lse[:8, i * rows : (i + 1) * rows]

def attn_fwd(x):
    nb, rows3, _ = x.shape
    half = rows3 // 3
    n = nb * half * 2
    return pl.pallas_call(
        attn_fwd_kernel,
        out_shape=(jax.ShapeDtypeStruct((nb, half, 128), bf16), jax.ShapeDtypeStruct((nb, half, 128), f32),
                   jax.ShapeDtypeStruct((nb, 8, 2 * half), f32)),
        scratch_shapes=[pltpu.VMEM((64, n), bf16), pltpu.VMEM((n, 64), bf16)],
        cost_estimate=pl.CostEstimate(flops=4 * n * n * 64, bytes_accessed=n * 64 * 2 * 8, transcendentals=n * n),
        compiler_params=pltpu.CompilerParams(vmem_limit_bytes=32 << 20),
        name="attn_fwd",
    )(x)

def attn_bwd_kernel(x_ref, d_ref, of_ref, lse_ref, g_ref, qt_ref, dt_ref, q_ref, dd_ref, lse_s, del_s, dqt_ref):
    nb, rows3, _ = x_ref.shape
    half = rows3 // 3
    rows = 2 * half
    for j in range(nb):
        sl = slice(j * rows, (j + 1) * rows)
        q = x_ref[j, :rows, :64] * jnp.asarray(0.125, bf16)
        q_ref[sl, :] = q
        qt_ref[:, sl] = q.T
        d = jnp.concatenate([d_ref[j, :, :64], d_ref[j, :, 64:]], axis=0)
        dd_ref[sl, :] = d
        dt_ref[:, sl] = d.T
        o = jnp.concatenate([of_ref[j, :, :64], of_ref[j, :, 64:]], axis=0)
        delta = jnp.sum(d.astype(f32) * o, axis=1, keepdims=True)
        del_s[:, sl] = jnp.broadcast_to(delta, (rows, 128)).T[:8]
        lse_s[:, sl] = lse_ref[j]
    dqt_ref[...] = jnp.zeros_like(dqt_ref)

    for j in range(0, nb, 2):
        k = x_ref[j : j + 2, :rows, 64:].reshape(2 * rows, 64)
        v = jnp.concatenate(
            [x_ref[j + i, rows:, lanes] for i in range(2) for lanes in (slice(0, 64), slice(64, 128))], axis=0
        )
        s = DOT(k, qt_ref[...])
        p = jnp.exp(s - lse_s[0:1, :])
        dp = DOT(v, dt_ref[...])
        ds = (p * (dp - del_s[0:1, :])).astype(bf16)
        dv = DOT(p.astype(bf16), dd_ref[...]).astype(bf16)
        dk = DOT(ds, q_ref[...])
        dqt_ref[...] += DOT(k.T, ds)
        g_ref[j : j + 2, :rows, 64:] = dk.astype(bf16).reshape(2, rows, 64)
        for i in range(2):
            g_ref[j + i, rows:, :] = jnp.concatenate(
                [dv[i * rows : i * rows + half], dv[i * rows + half : (i + 1) * rows]], axis=1
            )
    for j in range(nb):
        g_ref[j, :rows, :64] = (dqt_ref[:, j * rows : (j + 1) * rows].T * 0.125).astype(bf16)

def attn_bwd(x, d, of, lse):
    nb, rows3, _ = x.shape
    half = rows3 // 3
    n = nb * half * 2
    return pl.pallas_call(
        attn_bwd_kernel,
        out_shape=jax.ShapeDtypeStruct((nb, rows3, 128), bf16),
        scratch_shapes=[pltpu.VMEM((64, n), bf16), pltpu.VMEM((64, n), bf16), pltpu.VMEM((n, 64), bf16), pltpu.VMEM((n, 64), bf16),
                        pltpu.VMEM((8, n), f32), pltpu.VMEM((8, n), f32), pltpu.VMEM((64, n), f32)],
        cost_estimate=pl.CostEstimate(flops=n * n * 64, bytes_accessed=n * 64 * 2, transcendentals=0),
        compiler_params=pltpu.CompilerParams(vmem_limit_bytes=32 << 20),
        name="attn_bwd",
    )(x, d, of, lse)

HEADS = 12
HEAD_DIM = 64
SEQ_MB = 1
MICRO = 2


eps_norm = 1e-06
shard_group = 4


def normalize(values):
    average = jnp.mean(values, axis=-1, keepdims=True)
    centered = values - average
    variance = jnp.mean(centered * centered, axis=-1, keepdims=True)
    inv_std = lax.rsqrt(variance + eps_norm)
    return (centered * inv_std, inv_std)


def norm_back(grad_out, normed, inv_std, gain, scale_mod):
    factor = 1.0 + scale_mod
    d_normed = grad_out * gain * factor
    gain_term = jnp.sum(grad_out * normed * factor, axis=(0, 1))
    scale_term = jnp.sum(grad_out * normed * gain, axis=1)
    shift_term = jnp.sum(grad_out, axis=1)
    centred = d_normed - jnp.mean(d_normed, axis=-1, keepdims=True)
    d_inputs = inv_std * (centred - normed * jnp.mean(d_normed * normed, axis=-1, keepdims=True))
    return (d_inputs, gain_term, scale_term, shift_term)


def rotary_tables(positions):
    half_dim = HEAD_DIM // 2
    frequency = jnp.exp(
        -jnp.log(10000.0) * jnp.arange(half_dim, dtype=jnp.float32) * 2.0 / HEAD_DIM
    )
    angles = positions[:, None] * frequency[None, :]
    return (jnp.cos(angles)[:, None, :], jnp.sin(angles)[:, None, :])


def rotate(values, cos_table, sin_table):
    half_dim = values.shape[-1] // 2
    first_half = values[..., :half_dim]
    second_half = values[..., half_dim:]
    return jnp.concatenate(
        [
            first_half * cos_table - second_half * sin_table,
            second_half * cos_table + first_half * sin_table,
        ],
        axis=-1,
    )


def unrotate(grads, cos_table, sin_table):
    half_dim = grads.shape[-1] // 2
    first_half = grads[..., :half_dim]
    second_half = grads[..., half_dim:]
    return jnp.concatenate(
        [
            first_half * cos_table + second_half * sin_table,
            second_half * cos_table - first_half * sin_table,
        ],
        axis=-1,
    )


def gelu_tanh(values):
    return jax.nn.gelu(values, approximate=True)


def split_pairs(block):
    batch_seqs = block.shape[0]
    key_rows = block.shape[1]
    heads_here = block.shape[3] // HEAD_DIM
    keys = block[:, :, 0].reshape(batch_seqs, key_rows, heads_here, HEAD_DIM)
    values = block[:, :, 1].reshape(batch_seqs, key_rows, heads_here, HEAD_DIM)
    return (keys, values)


def split_blocks(piece, shard_rows):
    count = piece.shape[1] // shard_rows
    group = math.gcd(count, shard_group)
    steps = count // group
    shaped = piece.reshape((piece.shape[0], steps, group * shard_rows) + piece.shape[2:])
    return jnp.moveaxis(shaped, 1, 0)


def forward_block(query_heads, carry, block):
    top, totals, accum = carry
    keys, values = split_pairs(block)
    scores = jnp.einsum(
        "shqd,skhd->shqk", query_heads, keys, preferred_element_type=jnp.float32
    ) * HEAD_DIM ** (-0.5)
    new_top = jnp.maximum(top, jnp.max(scores, axis=-1))
    probs = jnp.exp(scores - new_top[..., None])
    fade = jnp.exp(top - new_top)
    totals = totals * fade + jnp.sum(probs, axis=-1)
    accum = accum * fade[..., None] + jnp.einsum(
        "shqk,skhd->shqd", probs.astype(jnp.bfloat16), values, preferred_element_type=jnp.float32
    )
    return (new_top, totals, accum)


def shards(inputs, conditioning, w_ada, w_qkv, w_out, w_up, w_down, gain_one, gain_two, cotangent):
    gathered = (
        lax.all_gather(w_ada, ("ulysses", "blk"), axis=1, tiled=True),
        lax.all_gather(w_qkv, ("ulysses", "blk"), axis=0, tiled=True),
        lax.all_gather(w_out, ("ulysses", "blk"), axis=0, tiled=True),
        lax.all_gather(w_up, ("ulysses", "blk"), axis=0, tiled=True),
        lax.all_gather(w_down, ("ulysses", "blk"), axis=0, tiled=True),
        lax.all_gather(gain_one, ("ulysses", "blk"), axis=0, tiled=True),
        lax.all_gather(gain_two, ("ulysses", "blk"), axis=0, tiled=True),
    )
    ada_full, qkv_full, out_full, up_full, down_full = (
        gathered[0],
        gathered[1],
        gathered[2],
        gathered[3],
        gathered[4],
    )
    gain_first = gathered[5].astype(jnp.float32)
    gain_second = gathered[6].astype(jnp.float32)
    rows = inputs.shape[1]
    width = inputs.shape[2]
    device_index = lax.axis_index(("ulysses", "blk"))
    positions = (device_index * rows + jnp.arange(rows, dtype=jnp.int32)).astype(jnp.float32)
    cos_table, sin_table = rotary_tables(positions)
    score_scale = HEAD_DIM ** (-0.5)
    ada_cols = w_ada.shape[1]
    grad_shapes = (
        w_qkv.shape,
        w_out.shape,
        w_up.shape,
        w_down.shape,
        gain_one.shape,
        gain_two.shape,
    )
    grad_totals = tuple((jnp.zeros(shape, jnp.float32) for shape in grad_shapes))
    ada_grad = jnp.zeros(w_ada.shape, jnp.float32)
    outputs_list = []
    input_grads = []
    cond_grads = []
    for micro_step in range(MICRO):
        offset = micro_step * SEQ_MB
        seq_inputs = inputs[offset : offset + SEQ_MB].astype(jnp.float32)
        cond_rows = conditioning[offset : offset + SEQ_MB]
        modulation = jnp.dot(cond_rows, ada_full, preferred_element_type=jnp.float32)
        pieces = [p[:, None, :] for p in jnp.split(modulation, 6, axis=1)]
        shift_one, scale_one, gate_one, shift_two, scale_two, gate_two = pieces
        normed_one, inv_one = normalize(seq_inputs)
        first_in = (normed_one * gain_first * (1.0 + scale_one) + shift_one).astype(jnp.bfloat16)
        projected = jnp.dot(first_in, qkv_full, preferred_element_type=jnp.float32)
        projected = projected.reshape(SEQ_MB, rows, 3, HEADS, HEAD_DIM)
        rot_query = rotate(projected[:, :, 0], cos_table, sin_table)
        rot_key = rotate(projected[:, :, 1], cos_table, sin_table)
        packed = jnp.stack([rot_query, rot_key, projected[:, :, 2]], axis=2).reshape(
            SEQ_MB, rows, 3, width
        )
        regrouped = lax.all_to_all(
            packed.astype(jnp.bfloat16), "ulysses", split_axis=3, concat_axis=1, tiled=True
        )
        query_rows = regrouped.shape[1]
        head_width = regrouped.shape[3]
        local_heads = head_width // HEAD_DIM
        query_heads = (
            regrouped[:, :, 0]
            .reshape(SEQ_MB, query_rows, local_heads, HEAD_DIM)
            .transpose(0, 2, 1, 3)
        )
        kv_local = regrouped[:, :, 1:]
        start_carry = (
            jnp.full((SEQ_MB, local_heads, query_rows), -1e30, jnp.float32),
            jnp.zeros((SEQ_MB, local_heads, query_rows), jnp.float32),
            jnp.zeros((SEQ_MB, local_heads, query_rows, HEAD_DIM), jnp.float32),
        )

        def scan_forward(carry, block):
            return (forward_block(query_heads, carry, block), None)

        result, _ = lax.scan(
            scan_forward,
            start_carry,
            split_blocks(lax.all_gather(kv_local, "blk", axis=1, tiled=True), query_rows),
        )
        carry = result
        top, totals, accum = carry
        attn_heads = accum / totals[..., None]
        log_total = top + jnp.log(totals)
        attn_tokens = (
            attn_heads.astype(jnp.bfloat16)
            .transpose(0, 2, 1, 3)
            .reshape(SEQ_MB, query_rows, head_width)
        )
        attended = lax.all_to_all(attn_tokens, "ulysses", split_axis=1, concat_axis=2, tiled=True)
        branch = jnp.dot(attended, out_full, preferred_element_type=jnp.float32)
        middle = seq_inputs + gate_one * branch
        normed_two, inv_two = normalize(middle)
        second_in = (normed_two * gain_second * (1.0 + scale_two) + shift_two).astype(jnp.bfloat16)
        raised = jnp.dot(second_in, up_full, preferred_element_type=jnp.float32)
        hidden, gelu_pull = jax.vjp(gelu_tanh, raised)
        hidden_low = hidden.astype(jnp.bfloat16)
        lowered = jnp.dot(hidden_low, down_full, preferred_element_type=jnp.float32)
        outputs_list.append(middle + gate_two * lowered)
        grad_out = cotangent[offset : offset + SEQ_MB].astype(jnp.float32)
        d_lowered = (gate_two * grad_out).astype(jnp.bfloat16)
        d_gate_two = jnp.sum(grad_out * lowered, axis=1)
        down_term = jnp.einsum(
            "srf,srd->fd", hidden_low, d_lowered, preferred_element_type=jnp.float32
        )
        d_hidden = jnp.einsum(
            "srd,fd->srf", d_lowered, down_full, preferred_element_type=jnp.float32
        )
        (d_raised,) = gelu_pull(d_hidden)
        d_raised_low = d_raised.astype(jnp.bfloat16)
        up_term = jnp.einsum(
            "srd,srf->df", second_in, d_raised_low, preferred_element_type=jnp.float32
        )
        d_second = jnp.einsum(
            "srf,df->srd", d_raised_low, up_full, preferred_element_type=jnp.float32
        )
        d_norm_two, gain_two_term, d_scale_two, d_shift_two = norm_back(
            d_second, normed_two, inv_two, gain_second, scale_two
        )
        d_middle = grad_out + d_norm_two
        d_gate_one = jnp.sum(d_middle * branch, axis=1)
        d_branch = (gate_one * d_middle).astype(jnp.bfloat16)
        out_term = jnp.einsum("srd,sre->de", attended, d_branch, preferred_element_type=jnp.float32)
        d_attended = jnp.einsum(
            "sre,de->srd", d_branch, out_full, preferred_element_type=jnp.float32
        ).astype(jnp.bfloat16)
        d_attn_rows = lax.all_to_all(d_attended, "ulysses", split_axis=2, concat_axis=1, tiled=True)
        d_attn_heads = d_attn_rows.reshape(SEQ_MB, query_rows, local_heads, HEAD_DIM).transpose(
            0, 2, 1, 3
        )
        delta = jnp.sum(d_attn_heads.astype(jnp.float32) * attn_heads, axis=-1)
        all_pairs = lax.all_gather(kv_local, "blk", axis=1, tiled=True)

        def back_step(d_query, block):
            keys, values = split_pairs(block)
            scores = (
                jnp.einsum("shqd,skhd->shqk", query_heads, keys, preferred_element_type=jnp.float32)
                * score_scale
            )
            probs = jnp.exp(scores - log_total[..., None])
            d_probs = jnp.einsum(
                "shqd,skhd->shqk", d_attn_heads, values, preferred_element_type=jnp.float32
            )
            d_scores = (probs * (d_probs - delta[..., None])).astype(jnp.bfloat16)
            d_query = (
                d_query
                + jnp.einsum("shqk,skhd->shqd", d_scores, keys, preferred_element_type=jnp.float32)
                * score_scale
            )
            d_keys = (
                jnp.einsum(
                    "shqk,shqd->skhd", d_scores, query_heads, preferred_element_type=jnp.float32
                )
                * score_scale
            )
            d_values = jnp.einsum(
                "shqk,shqd->skhd",
                probs.astype(jnp.bfloat16),
                d_attn_heads,
                preferred_element_type=jnp.float32,
            )
            key_rows = block.shape[1]
            pair = jnp.stack(
                [
                    d_keys.reshape(SEQ_MB, key_rows, head_width),
                    d_values.reshape(SEQ_MB, key_rows, head_width),
                ],
                axis=2,
            )
            return (d_query, pair)

        query_zero = jnp.zeros((SEQ_MB, local_heads, query_rows, HEAD_DIM), jnp.float32)
        d_query, pair_terms = lax.scan(back_step, query_zero, split_blocks(all_pairs, query_rows))
        pair_terms = jnp.moveaxis(pair_terms, 0, 1)
        pair_terms = pair_terms.reshape(
            SEQ_MB, pair_terms.shape[1] * pair_terms.shape[2], 2, head_width
        )
        pair_sums = lax.psum_scatter(pair_terms, "blk", scatter_dimension=1, tiled=True)
        query_grad = d_query.transpose(0, 2, 1, 3).reshape(SEQ_MB, query_rows, 1, head_width)
        d_packed = jnp.concatenate([query_grad, pair_sums], axis=2).astype(jnp.bfloat16)
        d_local = lax.all_to_all(d_packed, "ulysses", split_axis=1, concat_axis=3, tiled=True)
        d_local = d_local.astype(jnp.float32).reshape(SEQ_MB, rows, 3, HEADS, HEAD_DIM)
        d_projected = (
            jnp.stack(
                [
                    unrotate(d_local[:, :, 0], cos_table, sin_table),
                    unrotate(d_local[:, :, 1], cos_table, sin_table),
                    d_local[:, :, 2],
                ],
                axis=2,
            )
            .reshape(SEQ_MB, rows, 3 * width)
            .astype(jnp.bfloat16)
        )
        qkv_term = jnp.einsum(
            "srd,sre->de", first_in, d_projected, preferred_element_type=jnp.float32
        )
        d_first = jnp.einsum(
            "sre,de->srd", d_projected, qkv_full, preferred_element_type=jnp.float32
        )
        d_norm_one, gain_one_term, d_scale_one, d_shift_one = norm_back(
            d_first, normed_one, inv_one, gain_first, scale_one
        )
        input_grads.append(d_middle + d_norm_one)
        mod_local = jnp.concatenate(
            [d_shift_one, d_scale_one, d_gate_one, d_shift_two, d_scale_two, d_gate_two], axis=1
        )
        mod_total = lax.psum(mod_local, ("ulysses", "blk"))
        mod_low = mod_total.astype(jnp.bfloat16)
        cond_grads.append(
            jnp.einsum("sm,cm->sc", mod_low, ada_full, preferred_element_type=jnp.float32)
        )
        mod_part = lax.dynamic_slice_in_dim(mod_low, device_index * ada_cols, ada_cols, 1)
        ada_grad = ada_grad + jnp.einsum(
            "sc,sm->cm", cond_rows, mod_part, preferred_element_type=jnp.float32
        )
        terms = (qkv_term, out_term, up_term, down_term, gain_one_term, gain_two_term)
        reduced = (
            lax.psum_scatter(terms[0], ("ulysses", "blk"), scatter_dimension=0, tiled=True),
            lax.psum_scatter(terms[1], ("ulysses", "blk"), scatter_dimension=0, tiled=True),
            lax.psum_scatter(terms[2], ("ulysses", "blk"), scatter_dimension=0, tiled=True),
            lax.psum_scatter(terms[3], ("ulysses", "blk"), scatter_dimension=0, tiled=True),
            lax.psum_scatter(terms[4], ("ulysses", "blk"), scatter_dimension=0, tiled=True),
            lax.psum_scatter(terms[5], ("ulysses", "blk"), scatter_dimension=0, tiled=True),
        )
        grad_totals = tuple((a + b for a, b in zip(grad_totals, reduced)))
    output = jnp.concatenate(outputs_list, axis=0)
    inputs_grad = jnp.concatenate(input_grads, axis=0)
    conditioning_grad = jnp.concatenate(cond_grads, axis=0)
    return (
        output,
        inputs_grad,
        conditioning_grad,
        ada_grad,
        grad_totals[0],
        grad_totals[1],
        grad_totals[2],
        grad_totals[3],
        grad_totals[4],
        grad_totals[5],
    )


def dot_nt(left, right):
    return lax.dot_general(left, right, (((1,), (1,)), ((), ())), preferred_element_type=f32)


def dot_tn(left, right):
    return lax.dot_general(left, right, (((0,), (0,)), ((), ())), preferred_element_type=f32)


def row_norm(values):
    centered = values - jnp.mean(values, axis=1, keepdims=True)
    inv_std = lax.rsqrt(jnp.mean(centered * centered, axis=1, keepdims=True) + eps_norm)
    return centered * inv_std, inv_std


def row_back(grads, normed, inv_std):
    return inv_std * (
        grads
        - jnp.mean(grads, axis=1, keepdims=True)
        - normed * jnp.mean(grads * normed, axis=1, keepdims=True)
    )


def turn(values, cos_ref, sin_ref, sign):
    lane = lax.broadcasted_iota(jnp.int32, values.shape, 1) % HEAD_DIM
    swapped = jnp.where(
        lane < HEAD_DIM // 2, pltpu.roll(values, 128 - HEAD_DIM // 2, 1), pltpu.roll(values, HEAD_DIM // 2, 1)
    )
    return values * cos_ref[...] + sign * (swapped * sin_ref[...])


def mod_row(table_ref, s, i):
    width = table_ref.shape[1] // 7
    return table_ref[s : s + 1, i * width : (i + 1) * width]


EXTRA = 48


def split_low(values):
    high = values.astype(bf16).astype(f32)
    return high, values - high


def extra_rows(mods, gains, store):
    mods = jnp.concatenate(split_low(mods), axis=0)
    for i in range(3):
        store(i * mods.shape[0], mods[:, EXTRA * i : EXTRA * (i + 1)])
    store(3 * mods.shape[0], jnp.concatenate(split_low(gains), axis=0))


def join_rows(rows, i, seqs):
    return rows[2 * seqs * i : 2 * seqs * i + seqs] + rows[2 * seqs * i + seqs : 2 * seqs * (i + 1)]


def pack_kernel(
    x_ref, g_ref, qkv_ref, ada_ref, cond_ref, one_ref, two_ref, up_ref, xc_ref, piece_ref, ext_ref,
):
    n_u, block, cols = piece_ref.shape
    xc_ref[0] = x_ref[...]
    xc_ref[1] = g_ref[...]
    width = qkv_ref.shape[1] // 3
    ff = up_ref.shape[1] // n_u
    heads = width // n_u // HEAD_DIM
    ext_ref[...] = jnp.zeros_like(ext_ref)
    mods = dot_nt(cond_ref[...], ada_ref[...])
    gains = jnp.concatenate([one_ref[...], two_ref[...]], axis=0).astype(f32)

    def store(row, value):
        ext_ref[row : row + value.shape[0], : value.shape[1]] = value

    extra_rows(mods, gains, store)
    extra = ext_ref[...].astype(bf16)
    for i in range(n_u):
        pieces = []
        for h in range(heads):
            at = (i * heads + h) * HEAD_DIM
            pieces += [qkv_ref[:, at : at + HEAD_DIM], qkv_ref[:, width + at : width + at + HEAD_DIM]]
        at = 2 * width + i * heads * HEAD_DIM
        pieces += [qkv_ref[:, at : at + heads * HEAD_DIM], extra]
        piece_ref[i, :, : cols - ff] = jnp.concatenate(pieces, axis=1)
        piece_ref[i, :, cols - ff :] = up_ref[:, i * ff : (i + 1) * ff]


def first_kernel(
    at_ref, xg_ref, cos_ref, sin_ref, a0, a1, a2, a3, a4, a5, a6, a7,
    chunk_ref, first_ref, table_ref, w_ref, wide_ref,
):
    u, b = at_ref[0], at_ref[1]
    n_u, _, seqs, rows, width = xg_ref.shape
    span = n_u * rows
    cols = w_ref.shape[1]
    heads = cols // 192
    block = width // 32
    for i, part_ref in enumerate((a0, a1, a2, a3, a4, a5, a6, a7)):
        there = b ^ i
        for j in range(n_u):
            start = pl.multiple_of((j * 8 + there) * block, 8)
            wide_ref[pl.ds(start, block), :] = part_ref[j * block : (j + 1) * block, :].astype(f32)
    w_ref[...] = wide_ref[:, :cols].astype(bf16)
    pieces, gains = [], []
    for d in range(32):
        part = wide_ref[d * block : (d + 1) * block, cols:]
        pieces += [join_rows(part, i, seqs)[:, :EXTRA] for i in range(3)]
        gains.append(join_rows(part, 3, seqs)[:, :block])
    table_ref[...] = jnp.concatenate(pieces + gains, axis=1)
    gain = mod_row(table_ref, 0, 6)
    zero = jnp.zeros(chunk_ref.shape[1:], bf16)
    chunk_ref[0] = zero
    chunk_ref[chunk_ref.shape[0] - 1] = zero
    for s in range(seqs):
        factor = gain * (1.0 + mod_row(table_ref, s, 1))
        for m in range(n_u):
            normed, _ = row_norm(xg_ref[u ^ m, 0, s].astype(f32))
            first = normed * factor + mod_row(table_ref, s, 0)
            first_ref[s * span + m * rows : s * span + (m + 1) * rows, :] = first.astype(bf16)
        projected = DOT(first_ref[s * span : (s + 1) * span, :], w_ref[...])
        for h in range(heads):
            pair = 1 + s * heads + h
            both = turn(projected[:, 128 * h : 128 * (h + 1)], cos_ref, sin_ref, 1.0)
            chunk_ref[pair, :span, :] = both.astype(bf16)
            v = projected[:, 128 * heads + 64 * h : 128 * heads + 64 * (h + 1)].astype(bf16)
            chunk_ref[pair, span:, :] = jnp.concatenate([v[: span // 2], v[span // 2 :]], axis=1)


def unpack_tokens(t_ref, s, h, heads):
    half = t_ref[1 + s * heads + h]
    return jnp.concatenate([half[:, :HEAD_DIM], half[:, HEAD_DIM:]], axis=0)


def store_parts(send_ref, keep_ref, part, s, rows):
    for m in range(4):
        block = part[m * rows : (m + 1) * rows]
        if m % 2:
            send_ref[m // 2, s] = block.astype(bf16)
        else:
            keep_ref[m // 2, s] = block.astype(bf16)


def out_kernel(
    at_ref, t_ref, a0, a1, a2, a3, a4, a5, a6, a7, att_ref, send_ref, keep_ref, w_ref, wide_ref,
):
    _, seqs, rows, _ = send_ref.shape
    block = w_ref.shape[0] // 8
    low = a0.shape[0] - block
    for i, part_ref in enumerate((a0, a1, a2, a3, a4, a5, a6, a7)):
        start = pl.multiple_of((at_ref[1] ^ i) * block, 8)
        wide_ref[pl.ds(start, block), :] = part_ref[low:, :].astype(f32)
    w_ref[...] = wide_ref[...].astype(bf16)
    heads = w_ref.shape[0] // HEAD_DIM
    span = 4 * rows
    for s in range(seqs):
        att = jnp.concatenate([unpack_tokens(t_ref, s, h, heads) for h in range(heads)], axis=1)
        att_ref[s * span : (s + 1) * span, :] = att
        store_parts(send_ref, keep_ref, DOT(att, w_ref[...]), s, rows)


def block_of(own_ref, got_ref, m, s):
    return (got_ref if m % 2 else own_ref)[m // 2, s].astype(f32)


def middle_of(xg_ref, own_ref, got_ref, table_ref, u, m, s):
    return xg_ref[u ^ m, 0, s].astype(f32) + mod_row(table_ref, s, 2) * block_of(own_ref, got_ref, m, s)


def ff_kernel(
    at_ref, xg_ref, own_ref, got_ref, table_ref, a0, a1, a2, a3, a4, a5, a6, a7, b0, b1, b2, b3, b4, b5, b6, b7,
    lsend_ref, lkeep_ref, dsend_ref, dkeep_ref, sums_ref, ukeep_ref, usend_ref, wkeep_ref, wsend_ref,
    second_ref, hidden_ref, low_ref, raised_ref, normed_ref, wide_ref, up_ref, down_ref,
):
    u = at_ref[0]
    n_u, _, seqs, rows, width = xg_ref.shape
    span = n_u * rows
    gain = mod_row(table_ref, 1, 6)
    scale = math.sqrt(2.0 / math.pi)
    block = width // 32
    low = n_u * block
    u, b = at_ref[0], at_ref[1]
    ups, downs = (a0, a1, a2, a3, a4, a5, a6, a7), (b0, b1, b2, b3, b4, b5, b6, b7)
    for i, (part_ref, low_part_ref) in enumerate(zip(ups, downs)):
        there = b ^ i
        down_ref[pl.ds(pl.multiple_of(there * low, 32), low), :] = low_part_ref[:low, :]
        for j in range(n_u):
            start = pl.multiple_of((j * 8 + there) * block, 8)
            wide_ref[pl.ds(start, block), :] = part_ref[j * block : (j + 1) * block, :].astype(f32)
    up_ref[...] = wide_ref[...].astype(bf16)
    for s in range(seqs):
        at = slice(s * span, (s + 1) * span)
        factor = gain * (1.0 + mod_row(table_ref, s, 4))
        gate = mod_row(table_ref, s, 5)
        for m in range(n_u):
            here = slice(s * span + m * rows, s * span + (m + 1) * rows)
            normed, _ = row_norm(middle_of(xg_ref, own_ref, got_ref, table_ref, u, m, s))
            normed_ref[m * rows : (m + 1) * rows, :] = normed
            second_ref[here, :] = (normed * factor + mod_row(table_ref, s, 3)).astype(bf16)
            low_ref[here, :] = (gate * xg_ref[u ^ m, 1, s].astype(f32)).astype(bf16)
        raised = DOT(second_ref[at, :], up_ref[...])
        d_hidden = dot_nt(low_ref[at, :], down_ref[...])
        square = raised * raised
        t = jnp.tanh(scale * raised * (1.0 + 0.044715 * square))
        hidden_ref[at, :] = (0.5 * raised * (1.0 + t)).astype(bf16)
        slope = 0.5 * (1.0 + t) + 0.5 * raised * (1.0 - t * t) * (scale * (1.0 + 3.0 * 0.044715 * square))
        raised_ref[at, :] = (d_hidden * slope).astype(bf16)
        d_second = dot_nt(raised_ref[at, :], up_ref[...])
        store_parts(dsend_ref, dkeep_ref, d_second, s, rows)
        lowered = DOT(hidden_ref[at, :], down_ref[...])
        store_parts(lsend_ref, lkeep_ref, lowered, s, rows)
        sums_ref[s, 0:1, :] = jnp.sum(d_second, axis=0, keepdims=True)
        sums_ref[s, 1:2, :] = jnp.sum(d_second * normed_ref[...], axis=0, keepdims=True)
        gated = jnp.zeros((1, width), f32)
        for m in range(n_u):
            grad = xg_ref[u ^ m, 1, s].astype(f32)
            gated = gated + jnp.sum(grad * lowered[m * rows : (m + 1) * rows], axis=0, keepdims=True)
        sums_ref[s, 2:3, :] = gated
    n_z, side = ukeep_ref.shape[0], b % 2
    wide_ref[...] = dot_tn(hidden_ref[...], low_ref[...])
    for y, out_ref in enumerate((wkeep_ref, wsend_ref)):
        for z in range(n_z):
            start = pl.multiple_of((2 * z + (side ^ y)) * low, 32)
            out_ref[z] = wide_ref[pl.ds(start, low), :].astype(bf16)
    wide_ref[...] = dot_tn(second_ref[...], raised_ref[...])
    for y, out_ref in enumerate((ukeep_ref, usend_ref)):
        for z in range(n_z):
            for i in range(n_u):
                start = pl.multiple_of(((u ^ i) * 2 * n_z + 2 * z + (side ^ y)) * block, 8)
                out_ref[z, i] = wide_ref[pl.ds(start, block), :].astype(bf16)


def middle_back_kernel(
    at_ref, xg_ref, own_ref, got_ref, down_ref, dgot_ref, table_ref, w_ref, att_ref,
    chunk_ref, dmid_ref, gate_ref, okeep_ref, osend_ref, branch_ref, outs_ref,
):
    u = at_ref[0]
    n_u, _, seqs, rows, width = xg_ref.shape
    span = n_u * rows
    heads = w_ref.shape[0] // HEAD_DIM
    gain = mod_row(table_ref, 1, 6)
    zero = jnp.zeros(chunk_ref.shape[1:], bf16)
    chunk_ref[0] = zero
    chunk_ref[chunk_ref.shape[0] - 1] = zero
    for s in range(seqs):
        at = slice(s * span, (s + 1) * span)
        factor = gain * (1.0 + mod_row(table_ref, s, 4))
        gate = mod_row(table_ref, s, 2)
        for m in range(n_u):
            normed, inv_std = row_norm(middle_of(xg_ref, own_ref, got_ref, table_ref, u, m, s))
            grads = block_of(down_ref, dgot_ref, m, s) * factor
            d_middle = xg_ref[u ^ m, 1, s].astype(f32) + row_back(grads, normed, inv_std)
            branch_ref[s * span + m * rows : s * span + (m + 1) * rows, :] = (gate * d_middle).astype(bf16)
            if m == 0:
                dmid_ref[s] = d_middle
                gate_ref[s] = jnp.sum(d_middle * own_ref[0, s].astype(f32), axis=0, keepdims=True)
        d_att = dot_nt(branch_ref[at, :], w_ref[...]).astype(bf16)
        for h in range(heads):
            d = d_att[:, HEAD_DIM * h : HEAD_DIM * (h + 1)]
            chunk_ref[1 + s * heads + h] = jnp.concatenate([d[: span // 2], d[span // 2 :]], axis=1)
    n_z, block, _ = okeep_ref.shape
    outs_ref[...] = dot_tn(att_ref[...], branch_ref[...])
    for y, out_ref in enumerate((okeep_ref, osend_ref)):
        for z in range(n_z):
            start = pl.multiple_of((2 * z + ((at_ref[1] % 2) ^ y)) * block, 8)
            out_ref[z] = outs_ref[pl.ds(start, block), :].astype(bf16)


def first_back_kernel(
    at_ref, t_ref, xg_ref, table_ref, cos_ref, sin_ref, w_ref, first_ref, gate_ref, two_ref,
    send_ref, keep_ref, blocks_ref, proj_ref, normed_ref, sums_ref, ext_ref, both_ref,
):
    u = at_ref[0]
    n_u, _, seqs, rows, width = xg_ref.shape
    span = n_u * rows
    cols = w_ref.shape[1]
    heads = cols // 192
    gain_grads = [jnp.zeros((1, width), f32)] * 2
    total, block, _ = blocks_ref.shape
    for s in range(seqs):
        at = slice(s * span, (s + 1) * span)
        for h in range(heads):
            pair = t_ref[1 + s * heads + h]
            both = turn(pair[:span].astype(f32), cos_ref, sin_ref, -1.0)
            proj_ref[at, 128 * h : 128 * (h + 1)] = both.astype(bf16)
            v = pair[span:]
            proj_ref[at, 128 * heads + 64 * h : 128 * heads + 64 * (h + 1)] = jnp.concatenate(
                [v[:, :HEAD_DIM], v[:, HEAD_DIM:]], axis=0
            )
        d_first = dot_nt(proj_ref[at, :], w_ref[...])
        store_parts(send_ref, keep_ref, d_first, s, rows)
        for m in range(n_u):
            normed, _ = row_norm(xg_ref[u ^ m, 0, s].astype(f32))
            normed_ref[m * rows : (m + 1) * rows, :] = normed
        dots = [jnp.sum(d_first * normed_ref[...], axis=0, keepdims=True), two_ref[s, 1:2, :]]
        for i in range(2):
            gain_grads[i] = gain_grads[i] + dots[i] * (1.0 + mod_row(table_ref, s, 1 + 3 * i))
        rows_out = [
            jnp.sum(d_first, axis=0, keepdims=True),
            dots[0] * mod_row(table_ref, 0, 6),
            gate_ref[s],
            two_ref[s, 0:1, :],
            dots[1] * mod_row(table_ref, 1, 6),
            two_ref[s, 2:3, :],
        ]
        for i, row in enumerate(rows_out):
            sums_ref[s : s + 1, i * width : (i + 1) * width] = row
    for i in range(2):
        sums_ref[i : i + 1, 6 * width :] = gain_grads[i]
    ext_ref[...] = jnp.zeros_like(ext_ref)
    high = sums_ref[...].astype(bf16).astype(f32)
    both_ref[...] = jnp.concatenate([high, sums_ref[...] - high], axis=0)
    lines = 2 * seqs
    for d in range(total):
        for i in range(3):
            at = 3 * EXTRA * d + EXTRA * i
            ext_ref[d * block + lines * i : d * block + lines * (i + 1), :EXTRA] = both_ref[:, at : at + EXTRA]
        at = 6 * width + block * d
        ext_ref[d * block + 3 * lines : d * block + 4 * lines, :block] = both_ref[:, at : at + block]
    grads = dot_tn(first_ref[...], proj_ref[...])
    for i in range(total):
        at = slice(i * block, (i + 1) * block)
        blocks_ref[i, :, :cols] = grads[at].astype(bf16)
        blocks_ref[i, :, cols:] = ext_ref[at].astype(bf16)


def row_grad_kernel(at_ref, raw_ref, p0, p1, p2, p3, ada_ref, cond_ref, qkv_ref, up_ref, part_ref, adag_ref, gain_ref, mod_ref):
    u = at_ref[0]
    total, block, cols = raw_ref.shape
    cols = cols - HEAD_DIM
    n_u = 4
    n_b = total // n_u
    heads = cols // 192
    width = qkv_ref.shape[1] // 3
    seqs = mod_ref.shape[0]
    extra = jnp.zeros((block, HEAD_DIM), f32)
    for i in range(n_u):
        part = raw_ref[i * n_b].astype(f32)
        for j in range(1, n_b):
            part = part + raw_ref[i * n_b + j].astype(f32)
        extra = extra + part[:, cols:]
        for h in range(heads):
            to = (i * heads + h) * HEAD_DIM
            qkv_ref[:, to : to + HEAD_DIM] = part[:, 128 * h : 128 * h + HEAD_DIM]
            qkv_ref[:, width + to : width + to + HEAD_DIM] = part[:, 128 * h + HEAD_DIM : 128 * (h + 1)]
        at = i * heads * HEAD_DIM
        qkv_ref[:, 2 * width + at : 2 * width + at + heads * HEAD_DIM] = part[:, 128 * heads : cols]
    mod_ref[...] = jnp.concatenate([join_rows(extra, i, seqs)[:, :EXTRA] for i in range(3)], axis=1)
    gain_ref[...] = join_rows(extra, 3, seqs)[:, :block]
    mods = mod_ref[...].astype(bf16)
    grads = DOT(mods, ada_ref[...])
    for i in range(total):
        part_ref[i] = grads
    adag_ref[...] = dot_tn(mods, cond_ref[...])
    cols = up_ref.shape[1] // n_u
    for i, piece_ref in enumerate((p0, p1, p2, p3)):
        up_ref[:, pl.ds(pl.multiple_of((u ^ i) * cols, 128), cols)] = piece_ref[...]


def input_grad_kernel(x_ref, near_ref, got_ref, dmid_ref, table_ref, out_ref):
    seqs = x_ref.shape[0]
    for s in range(seqs):
        factor = mod_row(table_ref, 0, 6) * (1.0 + mod_row(table_ref, s, 1))
        normed, inv_std = row_norm(x_ref[s].astype(f32))
        grads = (near_ref[s].astype(f32) + got_ref[s].astype(f32)) * factor
        out_ref[s] = dmid_ref[s] + row_back(grads, normed, inv_std)


def call(kernel, name, outs, scratch, flops, *args, limit=16, staged=()):
    count = len(args)
    specs = [
        pl.BlockSpec(
            memory_space=pltpu.SMEM if a.dtype == jnp.int32 else pltpu.HBM if i in staged else pltpu.VMEM
        )
        for i, a in enumerate(args)
    ]
    size = sum(math.prod(a.shape) * a.dtype.itemsize for a in args)
    size += sum(math.prod(shape) * jnp.dtype(dtype).itemsize for shape, dtype in outs)
    shapes = [pltpu.VMEM(*s) for s in scratch]
    body = kernel
    if staged:
        shapes = [pltpu.VMEM(args[i].shape, args[i].dtype) for i in staged] + [
            pltpu.SemaphoreType.DMA((len(staged),))
        ] + shapes

        def body(*refs):
            ins, rest = list(refs[:count]), refs[count:]
            out_refs, held = rest[: len(outs)], rest[len(outs) :]
            sems = held[len(staged)]
            copies = []
            for j, i in enumerate(staged):
                copies.append(pltpu.make_async_copy(ins[i], held[j], sems.at[j]))
                ins[i] = held[j]
            for copy in copies:
                copy.start()
            for copy in copies:
                copy.wait()
            kernel(*ins, *out_refs, *held[len(staged) + 1 :])

    return pl.pallas_call(
        body,
        out_shape=tuple(jax.ShapeDtypeStruct(shape, dtype) for shape, dtype in outs),
        in_specs=specs,
        out_specs=tuple(pl.BlockSpec(memory_space=pltpu.VMEM) for _ in outs),
        scratch_shapes=shapes,
        cost_estimate=pl.CostEstimate(flops=int(flops) // 1000, bytes_accessed=int(size) // 1000, transcendentals=0),
        compiler_params=pltpu.CompilerParams(vmem_limit_bytes=limit << 20),
        name=name,
    )(*args)


def fits_tp(mesh):
    ulysses, blk = mesh.shape["ulysses"], mesh.shape["blk"]
    return ulysses == 4 and blk == 8 and HEADS % ulysses == 0


def swap_u(values, mask):
    return lax.ppermute(values, "ulysses", [(i, i ^ mask) for i in range(4)])


def swap_b(values, mask):
    return lax.ppermute(values, "blk", [(i, i ^ mask) for i in range(8)])


def scatter_z(blocks):
    groups = [[2 * z + y for z in range(4)] for y in range(2)]
    return lax.psum_scatter(blocks, "blk", scatter_dimension=0, axis_index_groups=groups, tiled=True)[0]


def exchange(blocks, axis):
    return lax.all_to_all(blocks, axis, split_axis=0, concat_axis=0, tiled=True)


def half_sum(send, keep):
    return (keep.astype(f32) + swap_u(send, 1).astype(f32)).astype(bf16)


def pair_sum(left, right):
    return (left.astype(f32) + right.astype(f32)).astype(bf16)


def along_z(values):
    return [values] + [swap_b(values, 2 * m) for m in (1, 2, 3)]


def along_y(parts):
    out = []
    for part in parts:
        out += [part, swap_b(part, 1)]
    return out


def sum_z(half):
    total = half[0]
    for m in (1, 2, 3):
        total = total + swap_b(half[m].astype(bf16), 2 * m).astype(f32)
    return total


def tp_shards(inputs, conditioning, w_ada, w_qkv, w_out, w_up, w_down, gain_one, gain_two, cotangent):
    n_u, n_b = 4, 8
    n_all = n_u * n_b
    everywhere = ("ulysses", "blk")
    seqs, rows, width = inputs.shape
    u = lax.axis_index("ulysses")
    b = lax.axis_index("blk")
    at = jnp.stack([u, b]).astype(jnp.int32)
    heads = HEADS // n_u
    head_width = heads * HEAD_DIM
    cols = 3 * head_width
    w_rows, down_rows = w_qkv.shape[0], w_down.shape[0]
    ff_local = w_up.shape[1] // n_u
    span = n_u * rows
    tokens = seqs * span

    both, pieces = call(
        pack_kernel, "pack",
        [((2,) + inputs.shape, bf16), ((n_u, w_rows, cols + HEAD_DIM + ff_local), bf16)],
        [((w_rows, HEAD_DIM), f32)], 0,
        inputs, cotangent, w_qkv, w_ada.T, conditioning, gain_one[None], gain_two[None], w_up,
        limit=60,
    )
    blocks = u ^ jnp.arange(n_u, dtype=jnp.int32)
    positions = ((blocks * n_b + b) * rows)[:, None] + jnp.arange(rows, dtype=jnp.int32)[None, :]
    cos_table, sin_table = rotary_tables(positions.reshape(-1).astype(f32))
    cos_table, sin_table = cos_table[:, 0], sin_table[:, 0]
    cos_table = jnp.concatenate([cos_table] * 4, axis=1)
    sin_table = jnp.concatenate([-sin_table, sin_table] * 2, axis=1)

    pieces, cos_table, sin_table, at = lax.optimization_barrier(
        (exchange(pieces, "ulysses"), cos_table, sin_table, at)
    )
    pieces = pieces.reshape(n_u * w_rows, cols + HEAD_DIM + ff_local)
    xg = lax.all_gather(both, "ulysses", axis=0, tiled=False)
    up_near = pieces[:, cols + HEAD_DIM :]
    down_z = along_z(jnp.concatenate([w_down, w_out], axis=0))
    pieces, down_z[1], down_z[2] = lax.optimization_barrier((pieces, down_z[1], down_z[2]))
    near = pieces[:, : cols + HEAD_DIM]
    rows_zy = along_y(along_z(near))

    chunks, first_in, table, w_qkv_u = call(
        first_kernel, "first",
        [((n_b, 3 * span // 2, 128), bf16), ((tokens, width), bf16), ((seqs, 7 * width), f32),
         ((width, cols), bf16)],
        [((width, cols + HEAD_DIM), f32)],
        2 * tokens * width * cols,
        at, xg, cos_table, sin_table, *rows_zy,
        limit=60,
    )
    chunks, down_z = lax.optimization_barrier((chunks, down_z))
    owned = exchange(chunks, "blk")
    down_zy = along_y(down_z)
    owned, up_near, down_zy[1], down_zy[3] = lax.optimization_barrier((owned, up_near, down_zy[1], down_zy[3]))
    up_z = along_z(up_near)
    attn_low, attn_full, log_total = attn_fwd(owned)
    part_shape = (2, seqs, rows, width)
    attn_low, up_z, down_zy = lax.optimization_barrier((attn_low, up_z, down_zy))
    attn_tokens = exchange(attn_low, "blk")
    up_zy = along_y(up_z[:1])
    attn_tokens, up_zy = lax.optimization_barrier((attn_tokens, up_zy))
    attended, send, keep, w_out_u = call(
        out_kernel, "out",
        [((tokens, head_width), bf16), (part_shape, bf16), (part_shape, bf16), ((head_width, width), bf16)],
        [((head_width, width), f32)],
        2 * tokens * width * head_width,
        at, attn_tokens, *down_zy,
    )

    half = half_sum(send, keep)
    across = swap_u(half, 2)
    up_zy = up_zy + along_y(up_z[1:])
    across, up_zy = lax.optimization_barrier((across, up_zy))
    own = pair_sum(half, across[::-1])
    got = swap_u(own, 1)
    lsend, lkeep, dsend, dkeep, sums_two, up_keep, up_send, down_keep, down_send = call(
        ff_kernel, "ff",
        [(part_shape, bf16), (part_shape, bf16), (part_shape, bf16), (part_shape, bf16), ((seqs, 3, width), f32)]
        + [((n_b // 2, n_u, w_rows, width), bf16)] * 2 + [((n_b // 2, down_rows, width), bf16)] * 2,
        [((tokens, width), bf16), ((tokens, ff_local), bf16), ((tokens, width), bf16), ((tokens, ff_local), bf16),
         ((span, width), f32), ((width, ff_local), f32), ((width, ff_local), bf16), ((ff_local, width), bf16)],
        12 * tokens * width * ff_local,
        at, xg, own, got, table, *up_zy, *down_zy,
        limit=60,
    )
    down_other, up_other = swap_b(down_send, 1), swap_b(up_send, 1)
    half = half_sum(dsend, dkeep)
    across = swap_u(half, 2)
    across, down_other = lax.optimization_barrier((across, down_other))
    down_grad = scatter_z(pair_sum(down_keep, down_other))
    d_own = pair_sum(half, across[::-1])
    d_got = swap_u(d_own, 1)
    d_chunks, d_middle, sum_gate, out_keep, out_send = call(
        middle_back_kernel, "middle_back",
        [((n_b, span // 2, 128), bf16), ((seqs, rows, width), f32), ((seqs, 1, width), f32)]
        + [((n_b // 2, w_rows, width), bf16)] * 2,
        [((tokens, width), bf16), ((head_width, width), f32)],
        4 * tokens * width * head_width,
        at, xg, own, got, d_own, d_got, table, w_out_u, attended,
        limit=60,
    )
    d_attn = exchange(d_chunks, "blk")
    out_other = swap_b(out_send, 1)
    up_low = pair_sum(up_keep, up_other)
    d_attn, out_other, down_grad = lax.optimization_barrier((d_attn, out_other, down_grad))
    up_low = jnp.concatenate([up_low, pair_sum(out_keep, out_other)[:, None]], axis=1)
    up_sum = scatter_z(up_low)
    d_owned = attn_bwd(owned, d_attn, attn_full, log_total)
    d_owned, lsend, lkeep = lax.optimization_barrier((d_owned, lsend, lkeep))
    lhalf = half_sum(lsend, lkeep)
    lowered = lhalf[0].astype(f32) + swap_u(lhalf[1], 2).astype(f32)
    gates = table.reshape(2, 7, 1, width)
    output = inputs.astype(f32) + gates[:, 2] * own[0].astype(f32) + gates[:, 5] * lowered
    up_sum = up_sum.astype(f32)
    up_parts = [up_sum[0]] + [swap_u(up_sum[m], m) for m in (1, 2, 3)]
    d_tokens = exchange(d_owned, "blk")
    d_tokens, up_parts, down_grad, output = lax.optimization_barrier((d_tokens, up_parts, down_grad, output))

    send, keep, qkv_blocks = call(
        first_back_kernel, "first_back",
        [(part_shape, bf16), (part_shape, bf16), ((n_all, w_rows, cols + HEAD_DIM), bf16)],
        [((tokens, cols), bf16), ((span, width), f32), ((seqs, 7 * width), f32), ((width, HEAD_DIM), f32),
         ((2 * seqs, 7 * width), f32)],
        4 * tokens * width * cols,
        at, d_tokens, xg, table, cos_table, sin_table, w_qkv_u, first_in, sum_gate, sums_two,
        limit=60,
    )
    half = half_sum(send, keep)
    far = swap_u(half[1], 2)
    inputs_grad, = call(
        input_grad_kernel, "input_grad",
        [((seqs, rows, width), f32)], [], 0,
        inputs, half[0], far, d_middle, table,
    )
    qkv_grad, up_grad, cond_part, ada_grad, gain_grads, _ = call(
        row_grad_kernel, "row_grad",
        [(w_qkv.shape, f32), (w_up.shape, f32), ((n_all,) + conditioning.shape, f32), (w_ada.shape[::-1], f32),
         ((2, w_rows), f32), ((seqs, w_ada.shape[1]), f32)],
        [], 0,
        at, exchange(qkv_blocks, everywhere), *up_parts, w_ada.T, conditioning,
        limit=6,
    )
    conditioning_grad = jnp.sum(exchange(cond_part, everywhere), axis=0)
    return (
        output,
        inputs_grad,
        conditioning_grad,
        ada_grad.T,
        qkv_grad,
        up_sum[n_u],
        up_grad,
        down_grad.astype(f32),
        gain_grads[0],
        gain_grads[1],
    )


def solution(mesh):
    body = tp_shards if fits_tp(mesh) else shards
    in_specs = (
        P(None, ("ulysses", "blk"), None),
        P(),
        P(None, ("ulysses", "blk")),
        P(("ulysses", "blk"), None),
        P(("ulysses", "blk"), None),
        P(("ulysses", "blk"), None),
        P(("ulysses", "blk"), None),
        P(("ulysses", "blk")),
        P(("ulysses", "blk")),
        P(None, ("ulysses", "blk"), None),
    )
    out_specs = (
        P(None, ("ulysses", "blk"), None),
        P(None, ("ulysses", "blk"), None),
        P(),
        P(None, ("ulysses", "blk")),
        P(("ulysses", "blk"), None),
        P(("ulysses", "blk"), None),
        P(("ulysses", "blk"), None),
        P(("ulysses", "blk"), None),
        P(("ulysses", "blk")),
        P(("ulysses", "blk")),
    )
    return jax.shard_map(body, mesh=mesh, in_specs=in_specs, out_specs=out_specs, check_vma=False)
```

```python
import functools
import math

import jax
import jax.numpy as jnp
from jax import lax
from jax.experimental import pallas as pl
from jax.experimental.pallas import tpu as pltpu
from jax.sharding import PartitionSpec as P

f32, bf16 = jnp.float32, jnp.bfloat16
DOT = functools.partial(jnp.dot, preferred_element_type=f32)

def attn_fwd_kernel(x_ref, o_ref, of_ref, lse_ref, kt_ref, v_ref):
    nb, rows3, _ = x_ref.shape
    half = rows3 // 3
    rows = 2 * half
    for j in range(nb):
        kt_ref[:, j * rows : (j + 1) * rows] = x_ref[j, :rows, 64:].T
        v_ref[j * rows : j * rows + half, :] = x_ref[j, rows:, :64]
        v_ref[j * rows + half : (j + 1) * rows, :] = x_ref[j, rows:, 64:]

    for j in range(0, nb, 2):
        q = x_ref[j : j + 2, :rows, :64].reshape(2 * rows, 64) * jnp.asarray(0.125, bf16)
        s = DOT(q, kt_ref[...])
        top = jnp.max(s, axis=1, keepdims=True)
        p = jnp.exp(s - top)
        total = jnp.sum(p, axis=1, keepdims=True)
        o = DOT(p.astype(bf16), v_ref[...]) / total
        lse = jnp.broadcast_to(top + jnp.log(total), (2 * rows, 128)).T
        for i in range(2):
            packed = jnp.concatenate(
                [o[i * rows : i * rows + half], o[i * rows + half : (i + 1) * rows]], axis=1
            )
            of_ref[j + i] = packed
            o_ref[j + i] = packed.astype(bf16)
            lse_ref[j + i] = lse[:8, i * rows : (i + 1) * rows]

def attn_fwd(x):
    nb, rows3, _ = x.shape
    half = rows3 // 3
    n = nb * half * 2
    return pl.pallas_call(
        attn_fwd_kernel,
        out_shape=(jax.ShapeDtypeStruct((nb, half, 128), bf16), jax.ShapeDtypeStruct((nb, half, 128), f32),
                   jax.ShapeDtypeStruct((nb, 8, 2 * half), f32)),
        scratch_shapes=[pltpu.VMEM((64, n), bf16), pltpu.VMEM((n, 64), bf16)],
        cost_estimate=pl.CostEstimate(flops=4 * n * n * 64, bytes_accessed=n * 64 * 2 * 8, transcendentals=n * n),
        compiler_params=pltpu.CompilerParams(vmem_limit_bytes=32 << 20),
        name="attn_fwd",
    )(x)

def attn_bwd_kernel(x_ref, d_ref, of_ref, lse_ref, g_ref, qt_ref, dt_ref, q_ref, dd_ref, lse_s, del_s, dqt_ref):
    nb, rows3, _ = x_ref.shape
    half = rows3 // 3
    rows = 2 * half
    for j in range(nb):
        sl = slice(j * rows, (j + 1) * rows)
        q = x_ref[j, :rows, :64] * jnp.asarray(0.125, bf16)
        q_ref[sl, :] = q
        qt_ref[:, sl] = q.T
        d = jnp.concatenate([d_ref[j, :, :64], d_ref[j, :, 64:]], axis=0)
        dd_ref[sl, :] = d
        dt_ref[:, sl] = d.T
        o = jnp.concatenate([of_ref[j, :, :64], of_ref[j, :, 64:]], axis=0)
        delta = jnp.sum(d.astype(f32) * o, axis=1, keepdims=True)
        del_s[:, sl] = jnp.broadcast_to(delta, (rows, 128)).T[:8]
        lse_s[:, sl] = lse_ref[j]
    dqt_ref[...] = jnp.zeros_like(dqt_ref)

    for j in range(0, nb, 2):
        k = x_ref[j : j + 2, :rows, 64:].reshape(2 * rows, 64)
        v = jnp.concatenate(
            [x_ref[j + i, rows:, lanes] for i in range(2) for lanes in (slice(0, 64), slice(64, 128))], axis=0
        )
        s = DOT(k, qt_ref[...])
        p = jnp.exp(s - lse_s[0:1, :])
        dp = DOT(v, dt_ref[...])
        ds = (p * (dp - del_s[0:1, :])).astype(bf16)
        dv = DOT(p.astype(bf16), dd_ref[...]).astype(bf16)
        dk = DOT(ds, q_ref[...])
        dqt_ref[...] += DOT(k.T, ds)
        g_ref[j : j + 2, :rows, 64:] = dk.astype(bf16).reshape(2, rows, 64)
        for i in range(2):
            g_ref[j + i, rows:, :] = jnp.concatenate(
                [dv[i * rows : i * rows + half], dv[i * rows + half : (i + 1) * rows]], axis=1
            )
    for j in range(nb):
        g_ref[j, :rows, :64] = (dqt_ref[:, j * rows : (j + 1) * rows].T * 0.125).astype(bf16)

def attn_bwd(x, d, of, lse):
    nb, rows3, _ = x.shape
    half = rows3 // 3
    n = nb * half * 2
    return pl.pallas_call(
        attn_bwd_kernel,
        out_shape=jax.ShapeDtypeStruct((nb, rows3, 128), bf16),
        scratch_shapes=[pltpu.VMEM((64, n), bf16), pltpu.VMEM((64, n), bf16), pltpu.VMEM((n, 64), bf16), pltpu.VMEM((n, 64), bf16),
                        pltpu.VMEM((8, n), f32), pltpu.VMEM((8, n), f32), pltpu.VMEM((64, n), f32)],
        cost_estimate=pl.CostEstimate(flops=n * n * 64, bytes_accessed=n * 64 * 2, transcendentals=0),
        compiler_params=pltpu.CompilerParams(vmem_limit_bytes=32 << 20),
        name="attn_bwd",
    )(x, d, of, lse)

HEADS = 12
HEAD_DIM = 64
SEQ_MB = 1
MICRO = 2


eps_norm = 1e-06
shard_group = 4


def normalize(values):
    average = jnp.mean(values, axis=-1, keepdims=True)
    centered = values - average
    variance = jnp.mean(centered * centered, axis=-1, keepdims=True)
    inv_std = lax.rsqrt(variance + eps_norm)
    return (centered * inv_std, inv_std)


def norm_back(grad_out, normed, inv_std, gain, scale_mod):
    factor = 1.0 + scale_mod
    d_normed = grad_out * gain * factor
    gain_term = jnp.sum(grad_out * normed * factor, axis=(0, 1))
    scale_term = jnp.sum(grad_out * normed * gain, axis=1)
    shift_term = jnp.sum(grad_out, axis=1)
    centred = d_normed - jnp.mean(d_normed, axis=-1, keepdims=True)
    d_inputs = inv_std * (centred - normed * jnp.mean(d_normed * normed, axis=-1, keepdims=True))
    return (d_inputs, gain_term, scale_term, shift_term)


def rotary_tables(positions):
    half_dim = HEAD_DIM // 2
    frequency = jnp.exp(
        -jnp.log(10000.0) * jnp.arange(half_dim, dtype=jnp.float32) * 2.0 / HEAD_DIM
    )
    angles = positions[:, None] * frequency[None, :]
    return (jnp.cos(angles)[:, None, :], jnp.sin(angles)[:, None, :])


def rotate(values, cos_table, sin_table):
    half_dim = values.shape[-1] // 2
    first_half = values[..., :half_dim]
    second_half = values[..., half_dim:]
    return jnp.concatenate(
        [
            first_half * cos_table - second_half * sin_table,
            second_half * cos_table + first_half * sin_table,
        ],
        axis=-1,
    )


def unrotate(grads, cos_table, sin_table):
    half_dim = grads.shape[-1] // 2
    first_half = grads[..., :half_dim]
    second_half = grads[..., half_dim:]
    return jnp.concatenate(
        [
            first_half * cos_table + second_half * sin_table,
            second_half * cos_table - first_half * sin_table,
        ],
        axis=-1,
    )


def gelu_tanh(values):
    return jax.nn.gelu(values, approximate=True)


def split_pairs(block):
    batch_seqs = block.shape[0]
    key_rows = block.shape[1]
    heads_here = block.shape[3] // HEAD_DIM
    keys = block[:, :, 0].reshape(batch_seqs, key_rows, heads_here, HEAD_DIM)
    values = block[:, :, 1].reshape(batch_seqs, key_rows, heads_here, HEAD_DIM)
    return (keys, values)


def split_blocks(piece, shard_rows):
    count = piece.shape[1] // shard_rows
    group = math.gcd(count, shard_group)
    steps = count // group
    shaped = piece.reshape((piece.shape[0], steps, group * shard_rows) + piece.shape[2:])
    return jnp.moveaxis(shaped, 1, 0)


def forward_block(query_heads, carry, block):
    top, totals, accum = carry
    keys, values = split_pairs(block)
    scores = jnp.einsum(
        "shqd,skhd->shqk", query_heads, keys, preferred_element_type=jnp.float32
    ) * HEAD_DIM ** (-0.5)
    new_top = jnp.maximum(top, jnp.max(scores, axis=-1))
    probs = jnp.exp(scores - new_top[..., None])
    fade = jnp.exp(top - new_top)
    totals = totals * fade + jnp.sum(probs, axis=-1)
    accum = accum * fade[..., None] + jnp.einsum(
        "shqk,skhd->shqd", probs.astype(jnp.bfloat16), values, preferred_element_type=jnp.float32
    )
    return (new_top, totals, accum)


def shards(inputs, conditioning, w_ada, w_qkv, w_out, w_up, w_down, gain_one, gain_two, cotangent):
    gathered = (
        lax.all_gather(w_ada, ("ulysses", "blk"), axis=1, tiled=True),
        lax.all_gather(w_qkv, ("ulysses", "blk"), axis=0, tiled=True),
        lax.all_gather(w_out, ("ulysses", "blk"), axis=0, tiled=True),
        lax.all_gather(w_up, ("ulysses", "blk"), axis=0, tiled=True),
        lax.all_gather(w_down, ("ulysses", "blk"), axis=0, tiled=True),
        lax.all_gather(gain_one, ("ulysses", "blk"), axis=0, tiled=True),
        lax.all_gather(gain_two, ("ulysses", "blk"), axis=0, tiled=True),
    )
    ada_full, qkv_full, out_full, up_full, down_full = (
        gathered[0],
        gathered[1],
        gathered[2],
        gathered[3],
        gathered[4],
    )
    gain_first = gathered[5].astype(jnp.float32)
    gain_second = gathered[6].astype(jnp.float32)
    rows = inputs.shape[1]
    width = inputs.shape[2]
    device_index = lax.axis_index(("ulysses", "blk"))
    positions = (device_index * rows + jnp.arange(rows, dtype=jnp.int32)).astype(jnp.float32)
    cos_table, sin_table = rotary_tables(positions)
    score_scale = HEAD_DIM ** (-0.5)
    ada_cols = w_ada.shape[1]
    grad_shapes = (
        w_qkv.shape,
        w_out.shape,
        w_up.shape,
        w_down.shape,
        gain_one.shape,
        gain_two.shape,
    )
    grad_totals = tuple((jnp.zeros(shape, jnp.float32) for shape in grad_shapes))
    ada_grad = jnp.zeros(w_ada.shape, jnp.float32)
    outputs_list = []
    input_grads = []
    cond_grads = []
    for micro_step in range(MICRO):
        offset = micro_step * SEQ_MB
        seq_inputs = inputs[offset : offset + SEQ_MB].astype(jnp.float32)
        cond_rows = conditioning[offset : offset + SEQ_MB]
        modulation = jnp.dot(cond_rows, ada_full, preferred_element_type=jnp.float32)
        pieces = [p[:, None, :] for p in jnp.split(modulation, 6, axis=1)]
        shift_one, scale_one, gate_one, shift_two, scale_two, gate_two = pieces
        normed_one, inv_one = normalize(seq_inputs)
        first_in = (normed_one * gain_first * (1.0 + scale_one) + shift_one).astype(jnp.bfloat16)
        projected = jnp.dot(first_in, qkv_full, preferred_element_type=jnp.float32)
        projected = projected.reshape(SEQ_MB, rows, 3, HEADS, HEAD_DIM)
        rot_query = rotate(projected[:, :, 0], cos_table, sin_table)
        rot_key = rotate(projected[:, :, 1], cos_table, sin_table)
        packed = jnp.stack([rot_query, rot_key, projected[:, :, 2]], axis=2).reshape(
            SEQ_MB, rows, 3, width
        )
        regrouped = lax.all_to_all(
            packed.astype(jnp.bfloat16), "ulysses", split_axis=3, concat_axis=1, tiled=True
        )
        query_rows = regrouped.shape[1]
        head_width = regrouped.shape[3]
        local_heads = head_width // HEAD_DIM
        query_heads = (
            regrouped[:, :, 0]
            .reshape(SEQ_MB, query_rows, local_heads, HEAD_DIM)
            .transpose(0, 2, 1, 3)
        )
        kv_local = regrouped[:, :, 1:]
        start_carry = (
            jnp.full((SEQ_MB, local_heads, query_rows), -1e30, jnp.float32),
            jnp.zeros((SEQ_MB, local_heads, query_rows), jnp.float32),
            jnp.zeros((SEQ_MB, local_heads, query_rows, HEAD_DIM), jnp.float32),
        )

        def scan_forward(carry, block):
            return (forward_block(query_heads, carry, block), None)

        result, _ = lax.scan(
            scan_forward,
            start_carry,
            split_blocks(lax.all_gather(kv_local, "blk", axis=1, tiled=True), query_rows),
        )
        carry = result
        top, totals, accum = carry
        attn_heads = accum / totals[..., None]
        log_total = top + jnp.log(totals)
        attn_tokens = (
            attn_heads.astype(jnp.bfloat16)
            .transpose(0, 2, 1, 3)
            .reshape(SEQ_MB, query_rows, head_width)
        )
        attended = lax.all_to_all(attn_tokens, "ulysses", split_axis=1, concat_axis=2, tiled=True)
        branch = jnp.dot(attended, out_full, preferred_element_type=jnp.float32)
        middle = seq_inputs + gate_one * branch
        normed_two, inv_two = normalize(middle)
        second_in = (normed_two * gain_second * (1.0 + scale_two) + shift_two).astype(jnp.bfloat16)
        raised = jnp.dot(second_in, up_full, preferred_element_type=jnp.float32)
        hidden, gelu_pull = jax.vjp(gelu_tanh, raised)
        hidden_low = hidden.astype(jnp.bfloat16)
        lowered = jnp.dot(hidden_low, down_full, preferred_element_type=jnp.float32)
        outputs_list.append(middle + gate_two * lowered)
        grad_out = cotangent[offset : offset + SEQ_MB].astype(jnp.float32)
        d_lowered = (gate_two * grad_out).astype(jnp.bfloat16)
        d_gate_two = jnp.sum(grad_out * lowered, axis=1)
        down_term = jnp.einsum(
            "srf,srd->fd", hidden_low, d_lowered, preferred_element_type=jnp.float32
        )
        d_hidden = jnp.einsum(
            "srd,fd->srf", d_lowered, down_full, preferred_element_type=jnp.float32
        )
        (d_raised,) = gelu_pull(d_hidden)
        d_raised_low = d_raised.astype(jnp.bfloat16)
        up_term = jnp.einsum(
            "srd,srf->df", second_in, d_raised_low, preferred_element_type=jnp.float32
        )
        d_second = jnp.einsum(
            "srf,df->srd", d_raised_low, up_full, preferred_element_type=jnp.float32
        )
        d_norm_two, gain_two_term, d_scale_two, d_shift_two = norm_back(
            d_second, normed_two, inv_two, gain_second, scale_two
        )
        d_middle = grad_out + d_norm_two
        d_gate_one = jnp.sum(d_middle * branch, axis=1)
        d_branch = (gate_one * d_middle).astype(jnp.bfloat16)
        out_term = jnp.einsum("srd,sre->de", attended, d_branch, preferred_element_type=jnp.float32)
        d_attended = jnp.einsum(
            "sre,de->srd", d_branch, out_full, preferred_element_type=jnp.float32
        ).astype(jnp.bfloat16)
        d_attn_rows = lax.all_to_all(d_attended, "ulysses", split_axis=2, concat_axis=1, tiled=True)
        d_attn_heads = d_attn_rows.reshape(SEQ_MB, query_rows, local_heads, HEAD_DIM).transpose(
            0, 2, 1, 3
        )
        delta = jnp.sum(d_attn_heads.astype(jnp.float32) * attn_heads, axis=-1)
        all_pairs = lax.all_gather(kv_local, "blk", axis=1, tiled=True)

        def back_step(d_query, block):
            keys, values = split_pairs(block)
            scores = (
                jnp.einsum("shqd,skhd->shqk", query_heads, keys, preferred_element_type=jnp.float32)
                * score_scale
            )
            probs = jnp.exp(scores - log_total[..., None])
            d_probs = jnp.einsum(
                "shqd,skhd->shqk", d_attn_heads, values, preferred_element_type=jnp.float32
            )
            d_scores = (probs * (d_probs - delta[..., None])).astype(jnp.bfloat16)
            d_query = (
                d_query
                + jnp.einsum("shqk,skhd->shqd", d_scores, keys, preferred_element_type=jnp.float32)
                * score_scale
            )
            d_keys = (
                jnp.einsum(
                    "shqk,shqd->skhd", d_scores, query_heads, preferred_element_type=jnp.float32
                )
                * score_scale
            )
            d_values = jnp.einsum(
                "shqk,shqd->skhd",
                probs.astype(jnp.bfloat16),
                d_attn_heads,
                preferred_element_type=jnp.float32,
            )
            key_rows = block.shape[1]
            pair = jnp.stack(
                [
                    d_keys.reshape(SEQ_MB, key_rows, head_width),
                    d_values.reshape(SEQ_MB, key_rows, head_width),
                ],
                axis=2,
            )
            return (d_query, pair)

        query_zero = jnp.zeros((SEQ_MB, local_heads, query_rows, HEAD_DIM), jnp.float32)
        d_query, pair_terms = lax.scan(back_step, query_zero, split_blocks(all_pairs, query_rows))
        pair_terms = jnp.moveaxis(pair_terms, 0, 1)
        pair_terms = pair_terms.reshape(
            SEQ_MB, pair_terms.shape[1] * pair_terms.shape[2], 2, head_width
        )
        pair_sums = lax.psum_scatter(pair_terms, "blk", scatter_dimension=1, tiled=True)
        query_grad = d_query.transpose(0, 2, 1, 3).reshape(SEQ_MB, query_rows, 1, head_width)
        d_packed = jnp.concatenate([query_grad, pair_sums], axis=2).astype(jnp.bfloat16)
        d_local = lax.all_to_all(d_packed, "ulysses", split_axis=1, concat_axis=3, tiled=True)
        d_local = d_local.astype(jnp.float32).reshape(SEQ_MB, rows, 3, HEADS, HEAD_DIM)
        d_projected = (
            jnp.stack(
                [
                    unrotate(d_local[:, :, 0], cos_table, sin_table),
                    unrotate(d_local[:, :, 1], cos_table, sin_table),
                    d_local[:, :, 2],
                ],
                axis=2,
            )
            .reshape(SEQ_MB, rows, 3 * width)
            .astype(jnp.bfloat16)
        )
        qkv_term = jnp.einsum(
            "srd,sre->de", first_in, d_projected, preferred_element_type=jnp.float32
        )
        d_first = jnp.einsum(
            "sre,de->srd", d_projected, qkv_full, preferred_element_type=jnp.float32
        )
        d_norm_one, gain_one_term, d_scale_one, d_shift_one = norm_back(
            d_first, normed_one, inv_one, gain_first, scale_one
        )
        input_grads.append(d_middle + d_norm_one)
        mod_local = jnp.concatenate(
            [d_shift_one, d_scale_one, d_gate_one, d_shift_two, d_scale_two, d_gate_two], axis=1
        )
        mod_total = lax.psum(mod_local, ("ulysses", "blk"))
        mod_low = mod_total.astype(jnp.bfloat16)
        cond_grads.append(
            jnp.einsum("sm,cm->sc", mod_low, ada_full, preferred_element_type=jnp.float32)
        )
        mod_part = lax.dynamic_slice_in_dim(mod_low, device_index * ada_cols, ada_cols, 1)
        ada_grad = ada_grad + jnp.einsum(
            "sc,sm->cm", cond_rows, mod_part, preferred_element_type=jnp.float32
        )
        terms = (qkv_term, out_term, up_term, down_term, gain_one_term, gain_two_term)
        reduced = (
            lax.psum_scatter(terms[0], ("ulysses", "blk"), scatter_dimension=0, tiled=True),
            lax.psum_scatter(terms[1], ("ulysses", "blk"), scatter_dimension=0, tiled=True),
            lax.psum_scatter(terms[2], ("ulysses", "blk"), scatter_dimension=0, tiled=True),
            lax.psum_scatter(terms[3], ("ulysses", "blk"), scatter_dimension=0, tiled=True),
            lax.psum_scatter(terms[4], ("ulysses", "blk"), scatter_dimension=0, tiled=True),
            lax.psum_scatter(terms[5], ("ulysses", "blk"), scatter_dimension=0, tiled=True),
        )
        grad_totals = tuple((a + b for a, b in zip(grad_totals, reduced)))
    output = jnp.concatenate(outputs_list, axis=0)
    inputs_grad = jnp.concatenate(input_grads, axis=0)
    conditioning_grad = jnp.concatenate(cond_grads, axis=0)
    return (
        output,
        inputs_grad,
        conditioning_grad,
        ada_grad,
        grad_totals[0],
        grad_totals[1],
        grad_totals[2],
        grad_totals[3],
        grad_totals[4],
        grad_totals[5],
    )


def dot_nt(left, right):
    return lax.dot_general(left, right, (((1,), (1,)), ((), ())), preferred_element_type=f32)


def dot_tn(left, right):
    return lax.dot_general(left, right, (((0,), (0,)), ((), ())), preferred_element_type=f32)


def row_norm(values):
    centered = values - jnp.mean(values, axis=1, keepdims=True)
    inv_std = lax.rsqrt(jnp.mean(centered * centered, axis=1, keepdims=True) + eps_norm)
    return centered * inv_std, inv_std


def row_back(grads, normed, inv_std):
    return inv_std * (
        grads
        - jnp.mean(grads, axis=1, keepdims=True)
        - normed * jnp.mean(grads * normed, axis=1, keepdims=True)
    )


def turn(values, cos_ref, sin_ref, sign):
    lane = lax.broadcasted_iota(jnp.int32, values.shape, 1) % HEAD_DIM
    swapped = jnp.where(
        lane < HEAD_DIM // 2, pltpu.roll(values, 128 - HEAD_DIM // 2, 1), pltpu.roll(values, HEAD_DIM // 2, 1)
    )
    return values * cos_ref[...] + sign * (swapped * sin_ref[...])


def mod_row(table_ref, s, i):
    width = table_ref.shape[1] // 7
    return table_ref[s : s + 1, i * width : (i + 1) * width]


EXTRA = 48


def split_low(values):
    high = values.astype(bf16).astype(f32)
    return high, values - high


def extra_rows(mods, gains, store):
    mods = jnp.concatenate(split_low(mods), axis=0)
    for i in range(3):
        store(i * mods.shape[0], mods[:, EXTRA * i : EXTRA * (i + 1)])
    store(3 * mods.shape[0], jnp.concatenate(split_low(gains), axis=0))


def join_rows(rows, i, seqs):
    return rows[2 * seqs * i : 2 * seqs * i + seqs] + rows[2 * seqs * i + seqs : 2 * seqs * (i + 1)]


def pack_kernel(
    x_ref, g_ref, qkv_ref, ada_ref, cond_ref, one_ref, two_ref, up_ref, xc_ref, piece_ref, ext_ref,
):
    n_u, block, cols = piece_ref.shape
    xc_ref[0] = x_ref[...]
    xc_ref[1] = g_ref[...]
    width = qkv_ref.shape[1] // 3
    ff = up_ref.shape[1] // n_u
    heads = width // n_u // HEAD_DIM
    ext_ref[...] = jnp.zeros_like(ext_ref)
    mods = dot_nt(cond_ref[...], ada_ref[...])
    gains = jnp.concatenate([one_ref[...], two_ref[...]], axis=0).astype(f32)

    def store(row, value):
        ext_ref[row : row + value.shape[0], : value.shape[1]] = value

    extra_rows(mods, gains, store)
    extra = ext_ref[...].astype(bf16)
    for i in range(n_u):
        pieces = []
        for h in range(heads):
            at = (i * heads + h) * HEAD_DIM
            pieces += [qkv_ref[:, at : at + HEAD_DIM], qkv_ref[:, width + at : width + at + HEAD_DIM]]
        at = 2 * width + i * heads * HEAD_DIM
        pieces += [qkv_ref[:, at : at + heads * HEAD_DIM], extra]
        piece_ref[i, :, : cols - ff] = jnp.concatenate(pieces, axis=1)
        piece_ref[i, :, cols - ff :] = up_ref[:, i * ff : (i + 1) * ff]


def first_kernel(
    at_ref, xg_ref, cos_ref, sin_ref, a0, a1, a2, a3, a4, a5, a6, a7,
    chunk_ref, first_ref, table_ref, w_ref, wide_ref,
):
    u, b = at_ref[0], at_ref[1]
    n_u, _, seqs, rows, width = xg_ref.shape
    span = n_u * rows
    cols = w_ref.shape[1]
    heads = cols // 192
    block = width // 32
    for i, part_ref in enumerate((a0, a1, a2, a3, a4, a5, a6, a7)):
        there = b ^ i
        for j in range(n_u):
            start = pl.multiple_of((j * 8 + there) * block, 8)
            wide_ref[pl.ds(start, block), :] = part_ref[j * block : (j + 1) * block, :].astype(f32)
    w_ref[...] = wide_ref[:, :cols].astype(bf16)
    pieces, gains = [], []
    for d in range(32):
        part = wide_ref[d * block : (d + 1) * block, cols:]
        pieces += [join_rows(part, i, seqs)[:, :EXTRA] for i in range(3)]
        gains.append(join_rows(part, 3, seqs)[:, :block])
    table_ref[...] = jnp.concatenate(pieces + gains, axis=1)
    gain = mod_row(table_ref, 0, 6)
    zero = jnp.zeros(chunk_ref.shape[1:], bf16)
    chunk_ref[0] = zero
    chunk_ref[chunk_ref.shape[0] - 1] = zero
    for s in range(seqs):
        factor = gain * (1.0 + mod_row(table_ref, s, 1))
        for m in range(n_u):
            normed, _ = row_norm(xg_ref[u ^ m, 0, s].astype(f32))
            first = normed * factor + mod_row(table_ref, s, 0)
            first_ref[s * span + m * rows : s * span + (m + 1) * rows, :] = first.astype(bf16)
        projected = DOT(first_ref[s * span : (s + 1) * span, :], w_ref[...])
        for h in range(heads):
            pair = 1 + s * heads + h
            both = turn(projected[:, 128 * h : 128 * (h + 1)], cos_ref, sin_ref, 1.0)
            chunk_ref[pair, :span, :] = both.astype(bf16)
            v = projected[:, 128 * heads + 64 * h : 128 * heads + 64 * (h + 1)].astype(bf16)
            chunk_ref[pair, span:, :] = jnp.concatenate([v[: span // 2], v[span // 2 :]], axis=1)


def unpack_tokens(t_ref, s, h, heads):
    half = t_ref[1 + s * heads + h]
    return jnp.concatenate([half[:, :HEAD_DIM], half[:, HEAD_DIM:]], axis=0)


def store_parts(send_ref, keep_ref, part, s, rows):
    for m in range(4):
        block = part[m * rows : (m + 1) * rows]
        if m % 2:
            send_ref[m // 2, s] = block.astype(bf16)
        else:
            keep_ref[m // 2, s] = block.astype(bf16)


def out_kernel(
    at_ref, t_ref, a0, a1, a2, a3, a4, a5, a6, a7, att_ref, send_ref, keep_ref, w_ref, wide_ref,
):
    _, seqs, rows, _ = send_ref.shape
    block = w_ref.shape[0] // 8
    low = a0.shape[0] - block
    for i, part_ref in enumerate((a0, a1, a2, a3, a4, a5, a6, a7)):
        start = pl.multiple_of((at_ref[1] ^ i) * block, 8)
        wide_ref[pl.ds(start, block), :] = part_ref[low:, :].astype(f32)
    w_ref[...] = wide_ref[...].astype(bf16)
    heads = w_ref.shape[0] // HEAD_DIM
    span = 4 * rows
    for s in range(seqs):
        att = jnp.concatenate([unpack_tokens(t_ref, s, h, heads) for h in range(heads)], axis=1)
        att_ref[s * span : (s + 1) * span, :] = att
        store_parts(send_ref, keep_ref, DOT(att, w_ref[...]), s, rows)


def block_of(own_ref, got_ref, m, s):
    return (got_ref if m % 2 else own_ref)[m // 2, s].astype(f32)


def middle_of(xg_ref, own_ref, got_ref, table_ref, u, m, s):
    return xg_ref[u ^ m, 0, s].astype(f32) + mod_row(table_ref, s, 2) * block_of(own_ref, got_ref, m, s)


def ff_kernel(
    at_ref, xg_ref, own_ref, got_ref, table_ref, a0, a1, a2, a3, a4, a5, a6, a7, b0, b1, b2, b3, b4, b5, b6, b7,
    lsend_ref, lkeep_ref, dsend_ref, dkeep_ref, sums_ref, ukeep_ref, usend_ref, wkeep_ref, wsend_ref,
    second_ref, hidden_ref, low_ref, raised_ref, normed_ref, wide_ref, up_ref, down_ref,
):
    u = at_ref[0]
    n_u, _, seqs, rows, width = xg_ref.shape
    span = n_u * rows
    gain = mod_row(table_ref, 1, 6)
    scale = math.sqrt(2.0 / math.pi)
    block = width // 32
    low = n_u * block
    u, b = at_ref[0], at_ref[1]
    ups, downs = (a0, a1, a2, a3, a4, a5, a6, a7), (b0, b1, b2, b3, b4, b5, b6, b7)
    for i, (part_ref, low_part_ref) in enumerate(zip(ups, downs)):
        there = b ^ i
        down_ref[pl.ds(pl.multiple_of(there * low, 32), low), :] = low_part_ref[:low, :]
        for j in range(n_u):
            start = pl.multiple_of((j * 8 + there) * block, 8)
            wide_ref[pl.ds(start, block), :] = part_ref[j * block : (j + 1) * block, :].astype(f32)
    up_ref[...] = wide_ref[...].astype(bf16)
    for s in range(seqs):
        at = slice(s * span, (s + 1) * span)
        factor = gain * (1.0 + mod_row(table_ref, s, 4))
        gate = mod_row(table_ref, s, 5)
        for m in range(n_u):
            here = slice(s * span + m * rows, s * span + (m + 1) * rows)
            normed, _ = row_norm(middle_of(xg_ref, own_ref, got_ref, table_ref, u, m, s))
            normed_ref[m * rows : (m + 1) * rows, :] = normed
            second_ref[here, :] = (normed * factor + mod_row(table_ref, s, 3)).astype(bf16)
            low_ref[here, :] = (gate * xg_ref[u ^ m, 1, s].astype(f32)).astype(bf16)
        raised = DOT(second_ref[at, :], up_ref[...])
        d_hidden = dot_nt(low_ref[at, :], down_ref[...])
        square = raised * raised
        t = jnp.tanh(scale * raised * (1.0 + 0.044715 * square))
        hidden_ref[at, :] = (0.5 * raised * (1.0 + t)).astype(bf16)
        slope = 0.5 * (1.0 + t) + 0.5 * raised * (1.0 - t * t) * (scale * (1.0 + 3.0 * 0.044715 * square))
        raised_ref[at, :] = (d_hidden * slope).astype(bf16)
        d_second = dot_nt(raised_ref[at, :], up_ref[...])
        store_parts(dsend_ref, dkeep_ref, d_second, s, rows)
        lowered = DOT(hidden_ref[at, :], down_ref[...])
        store_parts(lsend_ref, lkeep_ref, lowered, s, rows)
        sums_ref[s, 0:1, :] = jnp.sum(d_second, axis=0, keepdims=True)
        sums_ref[s, 1:2, :] = jnp.sum(d_second * normed_ref[...], axis=0, keepdims=True)
        gated = jnp.zeros((1, width), f32)
        for m in range(n_u):
            grad = xg_ref[u ^ m, 1, s].astype(f32)
            gated = gated + jnp.sum(grad * lowered[m * rows : (m + 1) * rows], axis=0, keepdims=True)
        sums_ref[s, 2:3, :] = gated
    n_z, side = ukeep_ref.shape[0], b % 2
    wide_ref[...] = dot_tn(hidden_ref[...], low_ref[...])
    for y, out_ref in enumerate((wkeep_ref, wsend_ref)):
        for z in range(n_z):
            start = pl.multiple_of((2 * z + (side ^ y)) * low, 32)
            out_ref[z] = wide_ref[pl.ds(start, low), :].astype(bf16)
    wide_ref[...] = dot_tn(second_ref[...], raised_ref[...])
    for y, out_ref in enumerate((ukeep_ref, usend_ref)):
        for z in range(n_z):
            for i in range(n_u):
                start = pl.multiple_of(((u ^ i) * 2 * n_z + 2 * z + (side ^ y)) * block, 8)
                out_ref[z, i] = wide_ref[pl.ds(start, block), :].astype(bf16)


def middle_back_kernel(
    at_ref, xg_ref, own_ref, got_ref, down_ref, dgot_ref, table_ref, w_ref, att_ref,
    chunk_ref, dmid_ref, gate_ref, okeep_ref, osend_ref, branch_ref, outs_ref,
):
    u = at_ref[0]
    n_u, _, seqs, rows, width = xg_ref.shape
    span = n_u * rows
    heads = w_ref.shape[0] // HEAD_DIM
    gain = mod_row(table_ref, 1, 6)
    zero = jnp.zeros(chunk_ref.shape[1:], bf16)
    chunk_ref[0] = zero
    chunk_ref[chunk_ref.shape[0] - 1] = zero
    for s in range(seqs):
        at = slice(s * span, (s + 1) * span)
        factor = gain * (1.0 + mod_row(table_ref, s, 4))
        gate = mod_row(table_ref, s, 2)
        for m in range(n_u):
            normed, inv_std = row_norm(middle_of(xg_ref, own_ref, got_ref, table_ref, u, m, s))
            grads = block_of(down_ref, dgot_ref, m, s) * factor
            d_middle = xg_ref[u ^ m, 1, s].astype(f32) + row_back(grads, normed, inv_std)
            branch_ref[s * span + m * rows : s * span + (m + 1) * rows, :] = (gate * d_middle).astype(bf16)
            if m == 0:
                dmid_ref[s] = d_middle
                gate_ref[s] = jnp.sum(d_middle * own_ref[0, s].astype(f32), axis=0, keepdims=True)
        d_att = dot_nt(branch_ref[at, :], w_ref[...]).astype(bf16)
        for h in range(heads):
            d = d_att[:, HEAD_DIM * h : HEAD_DIM * (h + 1)]
            chunk_ref[1 + s * heads + h] = jnp.concatenate([d[: span // 2], d[span // 2 :]], axis=1)
    n_z, block, _ = okeep_ref.shape
    outs_ref[...] = dot_tn(att_ref[...], branch_ref[...])
    for y, out_ref in enumerate((okeep_ref, osend_ref)):
        for z in range(n_z):
            start = pl.multiple_of((2 * z + ((at_ref[1] % 2) ^ y)) * block, 8)
            out_ref[z] = outs_ref[pl.ds(start, block), :].astype(bf16)


def first_back_kernel(
    at_ref, t_ref, xg_ref, table_ref, cos_ref, sin_ref, w_ref, first_ref, gate_ref, two_ref,
    send_ref, keep_ref, blocks_ref, proj_ref, normed_ref, sums_ref, ext_ref, both_ref,
):
    u = at_ref[0]
    n_u, _, seqs, rows, width = xg_ref.shape
    span = n_u * rows
    cols = w_ref.shape[1]
    heads = cols // 192
    gain_grads = [jnp.zeros((1, width), f32)] * 2
    total, block, _ = blocks_ref.shape
    for s in range(seqs):
        at = slice(s * span, (s + 1) * span)
        for h in range(heads):
            pair = t_ref[1 + s * heads + h]
            both = turn(pair[:span].astype(f32), cos_ref, sin_ref, -1.0)
            proj_ref[at, 128 * h : 128 * (h + 1)] = both.astype(bf16)
            v = pair[span:]
            proj_ref[at, 128 * heads + 64 * h : 128 * heads + 64 * (h + 1)] = jnp.concatenate(
                [v[:, :HEAD_DIM], v[:, HEAD_DIM:]], axis=0
            )
        d_first = dot_nt(proj_ref[at, :], w_ref[...])
        store_parts(send_ref, keep_ref, d_first, s, rows)
        for m in range(n_u):
            normed, _ = row_norm(xg_ref[u ^ m, 0, s].astype(f32))
            normed_ref[m * rows : (m + 1) * rows, :] = normed
        dots = [jnp.sum(d_first * normed_ref[...], axis=0, keepdims=True), two_ref[s, 1:2, :]]
        for i in range(2):
            gain_grads[i] = gain_grads[i] + dots[i] * (1.0 + mod_row(table_ref, s, 1 + 3 * i))
        rows_out = [
            jnp.sum(d_first, axis=0, keepdims=True),
            dots[0] * mod_row(table_ref, 0, 6),
            gate_ref[s],
            two_ref[s, 0:1, :],
            dots[1] * mod_row(table_ref, 1, 6),
            two_ref[s, 2:3, :],
        ]
        for i, row in enumerate(rows_out):
            sums_ref[s : s + 1, i * width : (i + 1) * width] = row
    for i in range(2):
        sums_ref[i : i + 1, 6 * width :] = gain_grads[i]
    ext_ref[...] = jnp.zeros_like(ext_ref)
    high = sums_ref[...].astype(bf16).astype(f32)
    both_ref[...] = jnp.concatenate([high, sums_ref[...] - high], axis=0)
    lines = 2 * seqs
    for d in range(total):
        for i in range(3):
            at = 3 * EXTRA * d + EXTRA * i
            ext_ref[d * block + lines * i : d * block + lines * (i + 1), :EXTRA] = both_ref[:, at : at + EXTRA]
        at = 6 * width + block * d
        ext_ref[d * block + 3 * lines : d * block + 4 * lines, :block] = both_ref[:, at : at + block]
    grads = dot_tn(first_ref[...], proj_ref[...])
    for i in range(total):
        at = slice(i * block, (i + 1) * block)
        blocks_ref[i, :, :cols] = grads[at].astype(bf16)
        blocks_ref[i, :, cols:] = ext_ref[at].astype(bf16)


def row_grad_kernel(at_ref, raw_ref, p0, p1, p2, p3, ada_ref, cond_ref, qkv_ref, up_ref, part_ref, adag_ref, gain_ref, mod_ref):
    u = at_ref[0]
    total, block, cols = raw_ref.shape
    cols = cols - HEAD_DIM
    n_u = 4
    n_b = total // n_u
    heads = cols // 192
    width = qkv_ref.shape[1] // 3
    seqs = mod_ref.shape[0]
    extra = jnp.zeros((block, HEAD_DIM), f32)
    for i in range(n_u):
        part = raw_ref[i * n_b].astype(f32)
        for j in range(1, n_b):
            part = part + raw_ref[i * n_b + j].astype(f32)
        extra = extra + part[:, cols:]
        for h in range(heads):
            to = (i * heads + h) * HEAD_DIM
            qkv_ref[:, to : to + HEAD_DIM] = part[:, 128 * h : 128 * h + HEAD_DIM]
            qkv_ref[:, width + to : width + to + HEAD_DIM] = part[:, 128 * h + HEAD_DIM : 128 * (h + 1)]
        at = i * heads * HEAD_DIM
        qkv_ref[:, 2 * width + at : 2 * width + at + heads * HEAD_DIM] = part[:, 128 * heads : cols]
    mod_ref[...] = jnp.concatenate([join_rows(extra, i, seqs)[:, :EXTRA] for i in range(3)], axis=1)
    gain_ref[...] = join_rows(extra, 3, seqs)[:, :block]
    mods = mod_ref[...].astype(bf16)
    grads = DOT(mods, ada_ref[...])
    for i in range(total):
        part_ref[i] = grads
    adag_ref[...] = dot_tn(mods, cond_ref[...])
    cols = up_ref.shape[1] // n_u
    for i, piece_ref in enumerate((p0, p1, p2, p3)):
        up_ref[:, pl.ds(pl.multiple_of((u ^ i) * cols, 128), cols)] = piece_ref[...]


def input_grad_kernel(x_ref, near_ref, got_ref, dmid_ref, table_ref, out_ref):
    seqs = x_ref.shape[0]
    for s in range(seqs):
        factor = mod_row(table_ref, 0, 6) * (1.0 + mod_row(table_ref, s, 1))
        normed, inv_std = row_norm(x_ref[s].astype(f32))
        grads = (near_ref[s].astype(f32) + got_ref[s].astype(f32)) * factor
        out_ref[s] = dmid_ref[s] + row_back(grads, normed, inv_std)


def call(kernel, name, outs, scratch, flops, *args, limit=16, staged=()):
    count = len(args)
    specs = [
        pl.BlockSpec(
            memory_space=pltpu.SMEM if a.dtype == jnp.int32 else pltpu.HBM if i in staged else pltpu.VMEM
        )
        for i, a in enumerate(args)
    ]
    size = sum(math.prod(a.shape) * a.dtype.itemsize for a in args)
    size += sum(math.prod(shape) * jnp.dtype(dtype).itemsize for shape, dtype in outs)
    shapes = [pltpu.VMEM(*s) for s in scratch]
    body = kernel
    if staged:
        shapes = [pltpu.VMEM(args[i].shape, args[i].dtype) for i in staged] + [
            pltpu.SemaphoreType.DMA((len(staged),))
        ] + shapes

        def body(*refs):
            ins, rest = list(refs[:count]), refs[count:]
            out_refs, held = rest[: len(outs)], rest[len(outs) :]
            sems = held[len(staged)]
            copies = []
            for j, i in enumerate(staged):
                copies.append(pltpu.make_async_copy(ins[i], held[j], sems.at[j]))
                ins[i] = held[j]
            for copy in copies:
                copy.start()
            for copy in copies:
                copy.wait()
            kernel(*ins, *out_refs, *held[len(staged) + 1 :])

    return pl.pallas_call(
        body,
        out_shape=tuple(jax.ShapeDtypeStruct(shape, dtype) for shape, dtype in outs),
        in_specs=specs,
        out_specs=tuple(pl.BlockSpec(memory_space=pltpu.VMEM) for _ in outs),
        scratch_shapes=shapes,
        cost_estimate=pl.CostEstimate(flops=int(flops) // 1000, bytes_accessed=int(size) // 1000, transcendentals=0),
        compiler_params=pltpu.CompilerParams(vmem_limit_bytes=limit << 20),
        name=name,
    )(*args)


def fits_tp(mesh):
    ulysses, blk = mesh.shape["ulysses"], mesh.shape["blk"]
    return ulysses == 4 and blk == 8 and HEADS % ulysses == 0


def swap_u(values, mask):
    return lax.ppermute(values, "ulysses", [(i, i ^ mask) for i in range(4)])


def swap_b(values, mask):
    return lax.ppermute(values, "blk", [(i, i ^ mask) for i in range(8)])


def scatter_z(blocks):
    groups = [[2 * z + y for z in range(4)] for y in range(2)]
    return lax.psum_scatter(blocks, "blk", scatter_dimension=0, axis_index_groups=groups, tiled=True)[0]


def exchange(blocks, axis):
    return lax.all_to_all(blocks, axis, split_axis=0, concat_axis=0, tiled=True)


def half_sum(send, keep):
    return (keep.astype(f32) + swap_u(send, 1).astype(f32)).astype(bf16)


def pair_sum(left, right):
    return (left.astype(f32) + right.astype(f32)).astype(bf16)


def along_z(values):
    return [values] + [swap_b(values, 2 * m) for m in (1, 2, 3)]


def along_y(parts):
    out = []
    for part in parts:
        out += [part, swap_b(part, 1)]
    return out


def sum_z(half):
    total = half[0]
    for m in (1, 2, 3):
        total = total + swap_b(half[m].astype(bf16), 2 * m).astype(f32)
    return total


def tp_shards(inputs, conditioning, w_ada, w_qkv, w_out, w_up, w_down, gain_one, gain_two, cotangent):
    n_u, n_b = 4, 8
    n_all = n_u * n_b
    everywhere = ("ulysses", "blk")
    seqs, rows, width = inputs.shape
    u = lax.axis_index("ulysses")
    b = lax.axis_index("blk")
    at = jnp.stack([u, b]).astype(jnp.int32)
    heads = HEADS // n_u
    head_width = heads * HEAD_DIM
    cols = 3 * head_width
    w_rows, down_rows = w_qkv.shape[0], w_down.shape[0]
    ff_local = w_up.shape[1] // n_u
    span = n_u * rows
    tokens = seqs * span

    both, pieces = call(
        pack_kernel, "pack",
        [((2,) + inputs.shape, bf16), ((n_u, w_rows, cols + HEAD_DIM + ff_local), bf16)],
        [((w_rows, HEAD_DIM), f32)], 0,
        inputs, cotangent, w_qkv, w_ada.T, conditioning, gain_one[None], gain_two[None], w_up,
        limit=60,
    )
    blocks = u ^ jnp.arange(n_u, dtype=jnp.int32)
    positions = ((blocks * n_b + b) * rows)[:, None] + jnp.arange(rows, dtype=jnp.int32)[None, :]
    cos_table, sin_table = rotary_tables(positions.reshape(-1).astype(f32))
    cos_table, sin_table = cos_table[:, 0], sin_table[:, 0]
    cos_table = jnp.concatenate([cos_table] * 4, axis=1)
    sin_table = jnp.concatenate([-sin_table, sin_table] * 2, axis=1)

    pieces, cos_table, sin_table, at = lax.optimization_barrier(
        (exchange(pieces, "ulysses"), cos_table, sin_table, at)
    )
    pieces = pieces.reshape(n_u * w_rows, cols + HEAD_DIM + ff_local)
    xg = lax.all_gather(both, "ulysses", axis=0, tiled=False)
    up_near = pieces[:, cols + HEAD_DIM :]
    down_z = along_z(jnp.concatenate([w_down, w_out], axis=0))
    pieces, down_z[1], down_z[2] = lax.optimization_barrier((pieces, down_z[1], down_z[2]))
    near = pieces[:, : cols + HEAD_DIM]
    rows_zy = along_y(along_z(near))

    chunks, first_in, table, w_qkv_u = call(
        first_kernel, "first",
        [((n_b, 3 * span // 2, 128), bf16), ((tokens, width), bf16), ((seqs, 7 * width), f32),
         ((width, cols), bf16)],
        [((width, cols + HEAD_DIM), f32)],
        2 * tokens * width * cols,
        at, xg, cos_table, sin_table, *rows_zy,
        limit=60,
    )
    chunks, down_z = lax.optimization_barrier((chunks, down_z))
    owned = exchange(chunks, "blk")
    down_zy = along_y(down_z)
    up_near, down_zy[1], down_zy[3] = lax.optimization_barrier((up_near, down_zy[1], down_zy[3]))
    up_z = along_z(up_near)
    attn_low, attn_full, log_total = attn_fwd(owned)
    part_shape = (2, seqs, rows, width)
    attn_low, up_z, down_zy = lax.optimization_barrier((attn_low, up_z, down_zy))
    attn_tokens = exchange(attn_low, "blk")
    up_zy = along_y(up_z[:1])
    attn_tokens, up_zy = lax.optimization_barrier((attn_tokens, up_zy))
    attended, send, keep, w_out_u = call(
        out_kernel, "out",
        [((tokens, head_width), bf16), (part_shape, bf16), (part_shape, bf16), ((head_width, width), bf16)],
        [((head_width, width), f32)],
        2 * tokens * width * head_width,
        at, attn_tokens, *down_zy,
    )

    half = half_sum(send, keep)
    across = swap_u(half, 2)
    up_zy = up_zy + along_y(up_z[1:])
    across, up_zy = lax.optimization_barrier((across, up_zy))
    own = pair_sum(half, across[::-1])
    got = swap_u(own, 1)
    lsend, lkeep, dsend, dkeep, sums_two, up_keep, up_send, down_keep, down_send = call(
        ff_kernel, "ff",
        [(part_shape, bf16), (part_shape, bf16), (part_shape, bf16), (part_shape, bf16), ((seqs, 3, width), f32)]
        + [((n_b // 2, n_u, w_rows, width), bf16)] * 2 + [((n_b // 2, down_rows, width), bf16)] * 2,
        [((tokens, width), bf16), ((tokens, ff_local), bf16), ((tokens, width), bf16), ((tokens, ff_local), bf16),
         ((span, width), f32), ((width, ff_local), f32), ((width, ff_local), bf16), ((ff_local, width), bf16)],
        12 * tokens * width * ff_local,
        at, xg, own, got, table, *up_zy, *down_zy,
        limit=60,
    )
    down_other, up_other = swap_b(down_send, 1), swap_b(up_send, 1)
    half = half_sum(dsend, dkeep)
    across = swap_u(half, 2)
    across, down_other = lax.optimization_barrier((across, down_other))
    down_grad = scatter_z(pair_sum(down_keep, down_other))
    d_own = pair_sum(half, across[::-1])
    d_got = swap_u(d_own, 1)
    d_chunks, d_middle, sum_gate, out_keep, out_send = call(
        middle_back_kernel, "middle_back",
        [((n_b, span // 2, 128), bf16), ((seqs, rows, width), f32), ((seqs, 1, width), f32)]
        + [((n_b // 2, w_rows, width), bf16)] * 2,
        [((tokens, width), bf16), ((head_width, width), f32)],
        4 * tokens * width * head_width,
        at, xg, own, got, d_own, d_got, table, w_out_u, attended,
        limit=60,
    )
    d_attn = exchange(d_chunks, "blk")
    out_other = swap_b(out_send, 1)
    up_low = pair_sum(up_keep, up_other)
    d_attn, out_other, down_grad = lax.optimization_barrier((d_attn, out_other, down_grad))
    up_low = jnp.concatenate([up_low, pair_sum(out_keep, out_other)[:, None]], axis=1)
    up_sum = scatter_z(up_low)
    d_owned = attn_bwd(owned, d_attn, attn_full, log_total)
    d_owned, lsend, lkeep = lax.optimization_barrier((d_owned, lsend, lkeep))
    lhalf = half_sum(lsend, lkeep)
    lowered = lhalf[0].astype(f32) + swap_u(lhalf[1], 2).astype(f32)
    gates = table.reshape(2, 7, 1, width)
    output = inputs.astype(f32) + gates[:, 2] * own[0].astype(f32) + gates[:, 5] * lowered
    up_sum = up_sum.astype(f32)
    up_parts = [up_sum[0]] + [swap_u(up_sum[m], m) for m in (1, 2, 3)]
    d_tokens = exchange(d_owned, "blk")
    d_tokens, up_parts, down_grad, output = lax.optimization_barrier((d_tokens, up_parts, down_grad, output))

    send, keep, qkv_blocks = call(
        first_back_kernel, "first_back",
        [(part_shape, bf16), (part_shape, bf16), ((n_all, w_rows, cols + HEAD_DIM), bf16)],
        [((tokens, cols), bf16), ((span, width), f32), ((seqs, 7 * width), f32), ((width, HEAD_DIM), f32),
         ((2 * seqs, 7 * width), f32)],
        4 * tokens * width * cols,
        at, d_tokens, xg, table, cos_table, sin_table, w_qkv_u, first_in, sum_gate, sums_two,
        limit=60,
    )
    half = half_sum(send, keep)
    far = swap_u(half[1], 2)
    inputs_grad, = call(
        input_grad_kernel, "input_grad",
        [((seqs, rows, width), f32)], [], 0,
        inputs, half[0], far, d_middle, table,
    )
    qkv_grad, up_grad, cond_part, ada_grad, gain_grads, _ = call(
        row_grad_kernel, "row_grad",
        [(w_qkv.shape, f32), (w_up.shape, f32), ((n_all,) + conditioning.shape, f32), (w_ada.shape[::-1], f32),
         ((2, w_rows), f32), ((seqs, w_ada.shape[1]), f32)],
        [], 0,
        at, exchange(qkv_blocks, everywhere), *up_parts, w_ada.T, conditioning,
        limit=6,
    )
    conditioning_grad = jnp.sum(exchange(cond_part, everywhere), axis=0)
    return (
        output,
        inputs_grad,
        conditioning_grad,
        ada_grad.T,
        qkv_grad,
        up_sum[n_u],
        up_grad,
        down_grad.astype(f32),
        gain_grads[0],
        gain_grads[1],
    )


def solution(mesh):
    body = tp_shards if fits_tp(mesh) else shards
    in_specs = (
        P(None, ("ulysses", "blk"), None),
        P(),
        P(None, ("ulysses", "blk")),
        P(("ulysses", "blk"), None),
        P(("ulysses", "blk"), None),
        P(("ulysses", "blk"), None),
        P(("ulysses", "blk"), None),
        P(("ulysses", "blk")),
        P(("ulysses", "blk")),
        P(None, ("ulysses", "blk"), None),
    )
    out_specs = (
        P(None, ("ulysses", "blk"), None),
        P(None, ("ulysses", "blk"), None),
        P(),
        P(None, ("ulysses", "blk")),
        P(("ulysses", "blk"), None),
        P(("ulysses", "blk"), None),
        P(("ulysses", "blk"), None),
        P(("ulysses", "blk"), None),
        P(("ulysses", "blk")),
        P(("ulysses", "blk")),
    )
    return jax.shard_map(body, mesh=mesh, in_specs=in_specs, out_specs=out_specs, check_vma=False)
```

```python
import functools
import math

import jax
import jax.numpy as jnp
from jax import lax
from jax.experimental import pallas as pl
from jax.experimental.pallas import tpu as pltpu
from jax.sharding import PartitionSpec as P

f32, bf16 = jnp.float32, jnp.bfloat16
DOT = functools.partial(jnp.dot, preferred_element_type=f32)

def attn_fwd_kernel(x_ref, o_ref, of_ref, lse_ref, kt_ref, v_ref):
    nb, rows3, _ = x_ref.shape
    half = rows3 // 3
    rows = 2 * half
    for j in range(nb):
        kt_ref[:, j * rows : (j + 1) * rows] = x_ref[j, :rows, 64:].T
        v_ref[j * rows : j * rows + half, :] = x_ref[j, rows:, :64]
        v_ref[j * rows + half : (j + 1) * rows, :] = x_ref[j, rows:, 64:]

    for j in range(0, nb, 2):
        q = x_ref[j : j + 2, :rows, :64].reshape(2 * rows, 64) * jnp.asarray(0.125, bf16)
        s = DOT(q, kt_ref[...])
        top = jnp.max(s, axis=1, keepdims=True)
        p = jnp.exp(s - top)
        total = jnp.sum(p, axis=1, keepdims=True)
        o = DOT(p.astype(bf16), v_ref[...]) / total
        lse = jnp.broadcast_to(top + jnp.log(total), (2 * rows, 128)).T
        for i in range(2):
            packed = jnp.concatenate(
                [o[i * rows : i * rows + half], o[i * rows + half : (i + 1) * rows]], axis=1
            )
            of_ref[j + i] = packed
            o_ref[j + i] = packed.astype(bf16)
            lse_ref[j + i] = lse[:8, i * rows : (i + 1) * rows]

def attn_fwd(x):
    nb, rows3, _ = x.shape
    half = rows3 // 3
    n = nb * half * 2
    return pl.pallas_call(
        attn_fwd_kernel,
        out_shape=(jax.ShapeDtypeStruct((nb, half, 128), bf16), jax.ShapeDtypeStruct((nb, half, 128), f32),
                   jax.ShapeDtypeStruct((nb, 8, 2 * half), f32)),
        scratch_shapes=[pltpu.VMEM((64, n), bf16), pltpu.VMEM((n, 64), bf16)],
        cost_estimate=pl.CostEstimate(flops=4 * n * n * 64, bytes_accessed=n * 64 * 2 * 8, transcendentals=n * n),
        compiler_params=pltpu.CompilerParams(vmem_limit_bytes=32 << 20),
        name="attn_fwd",
    )(x)

def attn_bwd_kernel(x_ref, d_ref, of_ref, lse_ref, g_ref, qt_ref, dt_ref, q_ref, dd_ref, lse_s, del_s, dqt_ref):
    nb, rows3, _ = x_ref.shape
    half = rows3 // 3
    rows = 2 * half
    for j in range(nb):
        sl = slice(j * rows, (j + 1) * rows)
        q = x_ref[j, :rows, :64] * jnp.asarray(0.125, bf16)
        q_ref[sl, :] = q
        qt_ref[:, sl] = q.T
        d = jnp.concatenate([d_ref[j, :, :64], d_ref[j, :, 64:]], axis=0)
        dd_ref[sl, :] = d
        dt_ref[:, sl] = d.T
        o = jnp.concatenate([of_ref[j, :, :64], of_ref[j, :, 64:]], axis=0)
        delta = jnp.sum(d.astype(f32) * o, axis=1, keepdims=True)
        del_s[:, sl] = jnp.broadcast_to(delta, (rows, 128)).T[:8]
        lse_s[:, sl] = lse_ref[j]
    dqt_ref[...] = jnp.zeros_like(dqt_ref)

    for j in range(0, nb, 2):
        k = x_ref[j : j + 2, :rows, 64:].reshape(2 * rows, 64)
        v = jnp.concatenate(
            [x_ref[j + i, rows:, lanes] for i in range(2) for lanes in (slice(0, 64), slice(64, 128))], axis=0
        )
        s = DOT(k, qt_ref[...])
        p = jnp.exp(s - lse_s[0:1, :])
        dp = DOT(v, dt_ref[...])
        ds = (p * (dp - del_s[0:1, :])).astype(bf16)
        dv = DOT(p.astype(bf16), dd_ref[...]).astype(bf16)
        dk = DOT(ds, q_ref[...])
        dqt_ref[...] += DOT(k.T, ds)
        g_ref[j : j + 2, :rows, 64:] = dk.astype(bf16).reshape(2, rows, 64)
        for i in range(2):
            g_ref[j + i, rows:, :] = jnp.concatenate(
                [dv[i * rows : i * rows + half], dv[i * rows + half : (i + 1) * rows]], axis=1
            )
    for j in range(nb):
        g_ref[j, :rows, :64] = (dqt_ref[:, j * rows : (j + 1) * rows].T * 0.125).astype(bf16)

def attn_bwd(x, d, of, lse):
    nb, rows3, _ = x.shape
    half = rows3 // 3
    n = nb * half * 2
    return pl.pallas_call(
        attn_bwd_kernel,
        out_shape=jax.ShapeDtypeStruct((nb, rows3, 128), bf16),
        scratch_shapes=[pltpu.VMEM((64, n), bf16), pltpu.VMEM((64, n), bf16), pltpu.VMEM((n, 64), bf16), pltpu.VMEM((n, 64), bf16),
                        pltpu.VMEM((8, n), f32), pltpu.VMEM((8, n), f32), pltpu.VMEM((64, n), f32)],
        cost_estimate=pl.CostEstimate(flops=n * n * 64, bytes_accessed=n * 64 * 2, transcendentals=0),
        compiler_params=pltpu.CompilerParams(vmem_limit_bytes=32 << 20),
        name="attn_bwd",
    )(x, d, of, lse)

HEADS = 12
HEAD_DIM = 64
SEQ_MB = 1
MICRO = 2


eps_norm = 1e-06
shard_group = 4


def normalize(values):
    average = jnp.mean(values, axis=-1, keepdims=True)
    centered = values - average
    variance = jnp.mean(centered * centered, axis=-1, keepdims=True)
    inv_std = lax.rsqrt(variance + eps_norm)
    return (centered * inv_std, inv_std)


def norm_back(grad_out, normed, inv_std, gain, scale_mod):
    factor = 1.0 + scale_mod
    d_normed = grad_out * gain * factor
    gain_term = jnp.sum(grad_out * normed * factor, axis=(0, 1))
    scale_term = jnp.sum(grad_out * normed * gain, axis=1)
    shift_term = jnp.sum(grad_out, axis=1)
    centred = d_normed - jnp.mean(d_normed, axis=-1, keepdims=True)
    d_inputs = inv_std * (centred - normed * jnp.mean(d_normed * normed, axis=-1, keepdims=True))
    return (d_inputs, gain_term, scale_term, shift_term)


def rotary_tables(positions):
    half_dim = HEAD_DIM // 2
    frequency = jnp.exp(
        -jnp.log(10000.0) * jnp.arange(half_dim, dtype=jnp.float32) * 2.0 / HEAD_DIM
    )
    angles = positions[:, None] * frequency[None, :]
    return (jnp.cos(angles)[:, None, :], jnp.sin(angles)[:, None, :])


def rotate(values, cos_table, sin_table):
    half_dim = values.shape[-1] // 2
    first_half = values[..., :half_dim]
    second_half = values[..., half_dim:]
    return jnp.concatenate(
        [
            first_half * cos_table - second_half * sin_table,
            second_half * cos_table + first_half * sin_table,
        ],
        axis=-1,
    )


def unrotate(grads, cos_table, sin_table):
    half_dim = grads.shape[-1] // 2
    first_half = grads[..., :half_dim]
    second_half = grads[..., half_dim:]
    return jnp.concatenate(
        [
            first_half * cos_table + second_half * sin_table,
            second_half * cos_table - first_half * sin_table,
        ],
        axis=-1,
    )


def gelu_tanh(values):
    return jax.nn.gelu(values, approximate=True)


def split_pairs(block):
    batch_seqs = block.shape[0]
    key_rows = block.shape[1]
    heads_here = block.shape[3] // HEAD_DIM
    keys = block[:, :, 0].reshape(batch_seqs, key_rows, heads_here, HEAD_DIM)
    values = block[:, :, 1].reshape(batch_seqs, key_rows, heads_here, HEAD_DIM)
    return (keys, values)


def split_blocks(piece, shard_rows):
    count = piece.shape[1] // shard_rows
    group = math.gcd(count, shard_group)
    steps = count // group
    shaped = piece.reshape((piece.shape[0], steps, group * shard_rows) + piece.shape[2:])
    return jnp.moveaxis(shaped, 1, 0)


def forward_block(query_heads, carry, block):
    top, totals, accum = carry
    keys, values = split_pairs(block)
    scores = jnp.einsum(
        "shqd,skhd->shqk", query_heads, keys, preferred_element_type=jnp.float32
    ) * HEAD_DIM ** (-0.5)
    new_top = jnp.maximum(top, jnp.max(scores, axis=-1))
    probs = jnp.exp(scores - new_top[..., None])
    fade = jnp.exp(top - new_top)
    totals = totals * fade + jnp.sum(probs, axis=-1)
    accum = accum * fade[..., None] + jnp.einsum(
        "shqk,skhd->shqd", probs.astype(jnp.bfloat16), values, preferred_element_type=jnp.float32
    )
    return (new_top, totals, accum)


def shards(inputs, conditioning, w_ada, w_qkv, w_out, w_up, w_down, gain_one, gain_two, cotangent):
    gathered = (
        lax.all_gather(w_ada, ("ulysses", "blk"), axis=1, tiled=True),
        lax.all_gather(w_qkv, ("ulysses", "blk"), axis=0, tiled=True),
        lax.all_gather(w_out, ("ulysses", "blk"), axis=0, tiled=True),
        lax.all_gather(w_up, ("ulysses", "blk"), axis=0, tiled=True),
        lax.all_gather(w_down, ("ulysses", "blk"), axis=0, tiled=True),
        lax.all_gather(gain_one, ("ulysses", "blk"), axis=0, tiled=True),
        lax.all_gather(gain_two, ("ulysses", "blk"), axis=0, tiled=True),
    )
    ada_full, qkv_full, out_full, up_full, down_full = (
        gathered[0],
        gathered[1],
        gathered[2],
        gathered[3],
        gathered[4],
    )
    gain_first = gathered[5].astype(jnp.float32)
    gain_second = gathered[6].astype(jnp.float32)
    rows = inputs.shape[1]
    width = inputs.shape[2]
    device_index = lax.axis_index(("ulysses", "blk"))
    positions = (device_index * rows + jnp.arange(rows, dtype=jnp.int32)).astype(jnp.float32)
    cos_table, sin_table = rotary_tables(positions)
    score_scale = HEAD_DIM ** (-0.5)
    ada_cols = w_ada.shape[1]
    grad_shapes = (
        w_qkv.shape,
        w_out.shape,
        w_up.shape,
        w_down.shape,
        gain_one.shape,
        gain_two.shape,
    )
    grad_totals = tuple((jnp.zeros(shape, jnp.float32) for shape in grad_shapes))
    ada_grad = jnp.zeros(w_ada.shape, jnp.float32)
    outputs_list = []
    input_grads = []
    cond_grads = []
    for micro_step in range(MICRO):
        offset = micro_step * SEQ_MB
        seq_inputs = inputs[offset : offset + SEQ_MB].astype(jnp.float32)
        cond_rows = conditioning[offset : offset + SEQ_MB]
        modulation = jnp.dot(cond_rows, ada_full, preferred_element_type=jnp.float32)
        pieces = [p[:, None, :] for p in jnp.split(modulation, 6, axis=1)]
        shift_one, scale_one, gate_one, shift_two, scale_two, gate_two = pieces
        normed_one, inv_one = normalize(seq_inputs)
        first_in = (normed_one * gain_first * (1.0 + scale_one) + shift_one).astype(jnp.bfloat16)
        projected = jnp.dot(first_in, qkv_full, preferred_element_type=jnp.float32)
        projected = projected.reshape(SEQ_MB, rows, 3, HEADS, HEAD_DIM)
        rot_query = rotate(projected[:, :, 0], cos_table, sin_table)
        rot_key = rotate(projected[:, :, 1], cos_table, sin_table)
        packed = jnp.stack([rot_query, rot_key, projected[:, :, 2]], axis=2).reshape(
            SEQ_MB, rows, 3, width
        )
        regrouped = lax.all_to_all(
            packed.astype(jnp.bfloat16), "ulysses", split_axis=3, concat_axis=1, tiled=True
        )
        query_rows = regrouped.shape[1]
        head_width = regrouped.shape[3]
        local_heads = head_width // HEAD_DIM
        query_heads = (
            regrouped[:, :, 0]
            .reshape(SEQ_MB, query_rows, local_heads, HEAD_DIM)
            .transpose(0, 2, 1, 3)
        )
        kv_local = regrouped[:, :, 1:]
        start_carry = (
            jnp.full((SEQ_MB, local_heads, query_rows), -1e30, jnp.float32),
            jnp.zeros((SEQ_MB, local_heads, query_rows), jnp.float32),
            jnp.zeros((SEQ_MB, local_heads, query_rows, HEAD_DIM), jnp.float32),
        )

        def scan_forward(carry, block):
            return (forward_block(query_heads, carry, block), None)

        result, _ = lax.scan(
            scan_forward,
            start_carry,
            split_blocks(lax.all_gather(kv_local, "blk", axis=1, tiled=True), query_rows),
        )
        carry = result
        top, totals, accum = carry
        attn_heads = accum / totals[..., None]
        log_total = top + jnp.log(totals)
        attn_tokens = (
            attn_heads.astype(jnp.bfloat16)
            .transpose(0, 2, 1, 3)
            .reshape(SEQ_MB, query_rows, head_width)
        )
        attended = lax.all_to_all(attn_tokens, "ulysses", split_axis=1, concat_axis=2, tiled=True)
        branch = jnp.dot(attended, out_full, preferred_element_type=jnp.float32)
        middle = seq_inputs + gate_one * branch
        normed_two, inv_two = normalize(middle)
        second_in = (normed_two * gain_second * (1.0 + scale_two) + shift_two).astype(jnp.bfloat16)
        raised = jnp.dot(second_in, up_full, preferred_element_type=jnp.float32)
        hidden, gelu_pull = jax.vjp(gelu_tanh, raised)
        hidden_low = hidden.astype(jnp.bfloat16)
        lowered = jnp.dot(hidden_low, down_full, preferred_element_type=jnp.float32)
        outputs_list.append(middle + gate_two * lowered)
        grad_out = cotangent[offset : offset + SEQ_MB].astype(jnp.float32)
        d_lowered = (gate_two * grad_out).astype(jnp.bfloat16)
        d_gate_two = jnp.sum(grad_out * lowered, axis=1)
        down_term = jnp.einsum(
            "srf,srd->fd", hidden_low, d_lowered, preferred_element_type=jnp.float32
        )
        d_hidden = jnp.einsum(
            "srd,fd->srf", d_lowered, down_full, preferred_element_type=jnp.float32
        )
        (d_raised,) = gelu_pull(d_hidden)
        d_raised_low = d_raised.astype(jnp.bfloat16)
        up_term = jnp.einsum(
            "srd,srf->df", second_in, d_raised_low, preferred_element_type=jnp.float32
        )
        d_second = jnp.einsum(
            "srf,df->srd", d_raised_low, up_full, preferred_element_type=jnp.float32
        )
        d_norm_two, gain_two_term, d_scale_two, d_shift_two = norm_back(
            d_second, normed_two, inv_two, gain_second, scale_two
        )
        d_middle = grad_out + d_norm_two
        d_gate_one = jnp.sum(d_middle * branch, axis=1)
        d_branch = (gate_one * d_middle).astype(jnp.bfloat16)
        out_term = jnp.einsum("srd,sre->de", attended, d_branch, preferred_element_type=jnp.float32)
        d_attended = jnp.einsum(
            "sre,de->srd", d_branch, out_full, preferred_element_type=jnp.float32
        ).astype(jnp.bfloat16)
        d_attn_rows = lax.all_to_all(d_attended, "ulysses", split_axis=2, concat_axis=1, tiled=True)
        d_attn_heads = d_attn_rows.reshape(SEQ_MB, query_rows, local_heads, HEAD_DIM).transpose(
            0, 2, 1, 3
        )
        delta = jnp.sum(d_attn_heads.astype(jnp.float32) * attn_heads, axis=-1)
        all_pairs = lax.all_gather(kv_local, "blk", axis=1, tiled=True)

        def back_step(d_query, block):
            keys, values = split_pairs(block)
            scores = (
                jnp.einsum("shqd,skhd->shqk", query_heads, keys, preferred_element_type=jnp.float32)
                * score_scale
            )
            probs = jnp.exp(scores - log_total[..., None])
            d_probs = jnp.einsum(
                "shqd,skhd->shqk", d_attn_heads, values, preferred_element_type=jnp.float32
            )
            d_scores = (probs * (d_probs - delta[..., None])).astype(jnp.bfloat16)
            d_query = (
                d_query
                + jnp.einsum("shqk,skhd->shqd", d_scores, keys, preferred_element_type=jnp.float32)
                * score_scale
            )
            d_keys = (
                jnp.einsum(
                    "shqk,shqd->skhd", d_scores, query_heads, preferred_element_type=jnp.float32
                )
                * score_scale
            )
            d_values = jnp.einsum(
                "shqk,shqd->skhd",
                probs.astype(jnp.bfloat16),
                d_attn_heads,
                preferred_element_type=jnp.float32,
            )
            key_rows = block.shape[1]
            pair = jnp.stack(
                [
                    d_keys.reshape(SEQ_MB, key_rows, head_width),
                    d_values.reshape(SEQ_MB, key_rows, head_width),
                ],
                axis=2,
            )
            return (d_query, pair)

        query_zero = jnp.zeros((SEQ_MB, local_heads, query_rows, HEAD_DIM), jnp.float32)
        d_query, pair_terms = lax.scan(back_step, query_zero, split_blocks(all_pairs, query_rows))
        pair_terms = jnp.moveaxis(pair_terms, 0, 1)
        pair_terms = pair_terms.reshape(
            SEQ_MB, pair_terms.shape[1] * pair_terms.shape[2], 2, head_width
        )
        pair_sums = lax.psum_scatter(pair_terms, "blk", scatter_dimension=1, tiled=True)
        query_grad = d_query.transpose(0, 2, 1, 3).reshape(SEQ_MB, query_rows, 1, head_width)
        d_packed = jnp.concatenate([query_grad, pair_sums], axis=2).astype(jnp.bfloat16)
        d_local = lax.all_to_all(d_packed, "ulysses", split_axis=1, concat_axis=3, tiled=True)
        d_local = d_local.astype(jnp.float32).reshape(SEQ_MB, rows, 3, HEADS, HEAD_DIM)
        d_projected = (
            jnp.stack(
                [
                    unrotate(d_local[:, :, 0], cos_table, sin_table),
                    unrotate(d_local[:, :, 1], cos_table, sin_table),
                    d_local[:, :, 2],
                ],
                axis=2,
            )
            .reshape(SEQ_MB, rows, 3 * width)
            .astype(jnp.bfloat16)
        )
        qkv_term = jnp.einsum(
            "srd,sre->de", first_in, d_projected, preferred_element_type=jnp.float32
        )
        d_first = jnp.einsum(
            "sre,de->srd", d_projected, qkv_full, preferred_element_type=jnp.float32
        )
        d_norm_one, gain_one_term, d_scale_one, d_shift_one = norm_back(
            d_first, normed_one, inv_one, gain_first, scale_one
        )
        input_grads.append(d_middle + d_norm_one)
        mod_local = jnp.concatenate(
            [d_shift_one, d_scale_one, d_gate_one, d_shift_two, d_scale_two, d_gate_two], axis=1
        )
        mod_total = lax.psum(mod_local, ("ulysses", "blk"))
        mod_low = mod_total.astype(jnp.bfloat16)
        cond_grads.append(
            jnp.einsum("sm,cm->sc", mod_low, ada_full, preferred_element_type=jnp.float32)
        )
        mod_part = lax.dynamic_slice_in_dim(mod_low, device_index * ada_cols, ada_cols, 1)
        ada_grad = ada_grad + jnp.einsum(
            "sc,sm->cm", cond_rows, mod_part, preferred_element_type=jnp.float32
        )
        terms = (qkv_term, out_term, up_term, down_term, gain_one_term, gain_two_term)
        reduced = (
            lax.psum_scatter(terms[0], ("ulysses", "blk"), scatter_dimension=0, tiled=True),
            lax.psum_scatter(terms[1], ("ulysses", "blk"), scatter_dimension=0, tiled=True),
            lax.psum_scatter(terms[2], ("ulysses", "blk"), scatter_dimension=0, tiled=True),
            lax.psum_scatter(terms[3], ("ulysses", "blk"), scatter_dimension=0, tiled=True),
            lax.psum_scatter(terms[4], ("ulysses", "blk"), scatter_dimension=0, tiled=True),
            lax.psum_scatter(terms[5], ("ulysses", "blk"), scatter_dimension=0, tiled=True),
        )
        grad_totals = tuple((a + b for a, b in zip(grad_totals, reduced)))
    output = jnp.concatenate(outputs_list, axis=0)
    inputs_grad = jnp.concatenate(input_grads, axis=0)
    conditioning_grad = jnp.concatenate(cond_grads, axis=0)
    return (
        output,
        inputs_grad,
        conditioning_grad,
        ada_grad,
        grad_totals[0],
        grad_totals[1],
        grad_totals[2],
        grad_totals[3],
        grad_totals[4],
        grad_totals[5],
    )


def dot_nt(left, right):
    return lax.dot_general(left, right, (((1,), (1,)), ((), ())), preferred_element_type=f32)


def dot_tn(left, right):
    return lax.dot_general(left, right, (((0,), (0,)), ((), ())), preferred_element_type=f32)


def row_norm(values):
    centered = values - jnp.mean(values, axis=1, keepdims=True)
    inv_std = lax.rsqrt(jnp.mean(centered * centered, axis=1, keepdims=True) + eps_norm)
    return centered * inv_std, inv_std


def row_back(grads, normed, inv_std):
    return inv_std * (
        grads
        - jnp.mean(grads, axis=1, keepdims=True)
        - normed * jnp.mean(grads * normed, axis=1, keepdims=True)
    )


def turn(values, cos_ref, sin_ref, sign):
    lane = lax.broadcasted_iota(jnp.int32, values.shape, 1) % HEAD_DIM
    swapped = jnp.where(
        lane < HEAD_DIM // 2, pltpu.roll(values, 128 - HEAD_DIM // 2, 1), pltpu.roll(values, HEAD_DIM // 2, 1)
    )
    return values * cos_ref[...] + sign * (swapped * sin_ref[...])


def mod_row(table_ref, s, i):
    width = table_ref.shape[1] // 7
    return table_ref[s : s + 1, i * width : (i + 1) * width]


EXTRA = 48


def split_low(values):
    high = values.astype(bf16).astype(f32)
    return high, values - high


def extra_rows(mods, gains, store):
    mods = jnp.concatenate(split_low(mods), axis=0)
    for i in range(3):
        store(i * mods.shape[0], mods[:, EXTRA * i : EXTRA * (i + 1)])
    store(3 * mods.shape[0], jnp.concatenate(split_low(gains), axis=0))


def join_rows(rows, i, seqs):
    return rows[2 * seqs * i : 2 * seqs * i + seqs] + rows[2 * seqs * i + seqs : 2 * seqs * (i + 1)]


def pack_kernel(
    x_ref, g_ref, qkv_ref, ada_ref, cond_ref, one_ref, two_ref, up_ref, xc_ref, piece_ref, ext_ref,
):
    n_u, block, cols = piece_ref.shape
    xc_ref[0] = x_ref[...]
    xc_ref[1] = g_ref[...]
    width = qkv_ref.shape[1] // 3
    ff = up_ref.shape[1] // n_u
    heads = width // n_u // HEAD_DIM
    ext_ref[...] = jnp.zeros_like(ext_ref)
    mods = dot_nt(cond_ref[...], ada_ref[...])
    gains = jnp.concatenate([one_ref[...], two_ref[...]], axis=0).astype(f32)

    def store(row, value):
        ext_ref[row : row + value.shape[0], : value.shape[1]] = value

    extra_rows(mods, gains, store)
    extra = ext_ref[...].astype(bf16)
    for i in range(n_u):
        pieces = []
        for h in range(heads):
            at = (i * heads + h) * HEAD_DIM
            pieces += [qkv_ref[:, at : at + HEAD_DIM], qkv_ref[:, width + at : width + at + HEAD_DIM]]
        at = 2 * width + i * heads * HEAD_DIM
        pieces += [qkv_ref[:, at : at + heads * HEAD_DIM], extra]
        piece_ref[i, :, : cols - ff] = jnp.concatenate(pieces, axis=1)
        piece_ref[i, :, cols - ff :] = up_ref[:, i * ff : (i + 1) * ff]


def first_kernel(
    at_ref, xg_ref, cos_ref, sin_ref, a0, a1, a2, a3, a4, a5, a6, a7,
    chunk_ref, first_ref, table_ref, w_ref, wide_ref,
):
    u, b = at_ref[0], at_ref[1]
    n_u, _, seqs, rows, width = xg_ref.shape
    span = n_u * rows
    cols = w_ref.shape[1]
    heads = cols // 192
    block = width // 32
    for i, part_ref in enumerate((a0, a1, a2, a3, a4, a5, a6, a7)):
        there = b ^ i
        for j in range(n_u):
            start = pl.multiple_of((j * 8 + there) * block, 8)
            wide_ref[pl.ds(start, block), :] = part_ref[j * block : (j + 1) * block, :].astype(f32)
    w_ref[...] = wide_ref[:, :cols].astype(bf16)
    pieces, gains = [], []
    for d in range(32):
        part = wide_ref[d * block : (d + 1) * block, cols:]
        pieces += [join_rows(part, i, seqs)[:, :EXTRA] for i in range(3)]
        gains.append(join_rows(part, 3, seqs)[:, :block])
    table_ref[...] = jnp.concatenate(pieces + gains, axis=1)
    gain = mod_row(table_ref, 0, 6)
    zero = jnp.zeros(chunk_ref.shape[1:], bf16)
    chunk_ref[0] = zero
    chunk_ref[chunk_ref.shape[0] - 1] = zero
    for s in range(seqs):
        factor = gain * (1.0 + mod_row(table_ref, s, 1))
        for m in range(n_u):
            normed, _ = row_norm(xg_ref[u ^ m, 0, s].astype(f32))
            first = normed * factor + mod_row(table_ref, s, 0)
            first_ref[s * span + m * rows : s * span + (m + 1) * rows, :] = first.astype(bf16)
        projected = DOT(first_ref[s * span : (s + 1) * span, :], w_ref[...])
        for h in range(heads):
            pair = 1 + s * heads + h
            both = turn(projected[:, 128 * h : 128 * (h + 1)], cos_ref, sin_ref, 1.0)
            chunk_ref[pair, :span, :] = both.astype(bf16)
            v = projected[:, 128 * heads + 64 * h : 128 * heads + 64 * (h + 1)].astype(bf16)
            chunk_ref[pair, span:, :] = jnp.concatenate([v[: span // 2], v[span // 2 :]], axis=1)


def unpack_tokens(t_ref, s, h, heads):
    half = t_ref[1 + s * heads + h]
    return jnp.concatenate([half[:, :HEAD_DIM], half[:, HEAD_DIM:]], axis=0)


def store_parts(send_ref, keep_ref, part, s, rows):
    for m in range(4):
        block = part[m * rows : (m + 1) * rows]
        if m % 2:
            send_ref[m // 2, s] = block.astype(bf16)
        else:
            keep_ref[m // 2, s] = block.astype(bf16)


def out_kernel(
    at_ref, t_ref, a0, a1, a2, a3, a4, a5, a6, a7, att_ref, send_ref, keep_ref, w_ref, wide_ref,
):
    _, seqs, rows, _ = send_ref.shape
    block = w_ref.shape[0] // 8
    low = a0.shape[0] - block
    for i, part_ref in enumerate((a0, a1, a2, a3, a4, a5, a6, a7)):
        start = pl.multiple_of((at_ref[1] ^ i) * block, 8)
        wide_ref[pl.ds(start, block), :] = part_ref[low:, :].astype(f32)
    w_ref[...] = wide_ref[...].astype(bf16)
    heads = w_ref.shape[0] // HEAD_DIM
    span = 4 * rows
    for s in range(seqs):
        att = jnp.concatenate([unpack_tokens(t_ref, s, h, heads) for h in range(heads)], axis=1)
        att_ref[s * span : (s + 1) * span, :] = att
        store_parts(send_ref, keep_ref, DOT(att, w_ref[...]), s, rows)


def block_of(own_ref, got_ref, m, s):
    return (got_ref if m % 2 else own_ref)[m // 2, s].astype(f32)


def middle_of(xg_ref, own_ref, got_ref, table_ref, u, m, s):
    return xg_ref[u ^ m, 0, s].astype(f32) + mod_row(table_ref, s, 2) * block_of(own_ref, got_ref, m, s)


def ff_kernel(
    at_ref, xg_ref, own_ref, got_ref, table_ref, a0, a1, a2, a3, a4, a5, a6, a7, b0, b1, b2, b3, b4, b5, b6, b7,
    lsend_ref, lkeep_ref, dsend_ref, dkeep_ref, sums_ref, ukeep_ref, usend_ref, wkeep_ref, wsend_ref,
    second_ref, hidden_ref, low_ref, raised_ref, normed_ref, wide_ref, up_ref, down_ref,
):
    u = at_ref[0]
    n_u, _, seqs, rows, width = xg_ref.shape
    span = n_u * rows
    gain = mod_row(table_ref, 1, 6)
    scale = math.sqrt(2.0 / math.pi)
    block = width // 32
    low = n_u * block
    u, b = at_ref[0], at_ref[1]
    ups, downs = (a0, a1, a2, a3, a4, a5, a6, a7), (b0, b1, b2, b3, b4, b5, b6, b7)
    for i, (part_ref, low_part_ref) in enumerate(zip(ups, downs)):
        there = b ^ i
        down_ref[pl.ds(pl.multiple_of(there * low, 32), low), :] = low_part_ref[:low, :]
        for j in range(n_u):
            start = pl.multiple_of((j * 8 + there) * block, 8)
            wide_ref[pl.ds(start, block), :] = part_ref[j * block : (j + 1) * block, :].astype(f32)
    up_ref[...] = wide_ref[...].astype(bf16)
    for s in range(seqs):
        at = slice(s * span, (s + 1) * span)
        factor = gain * (1.0 + mod_row(table_ref, s, 4))
        gate = mod_row(table_ref, s, 5)
        for m in range(n_u):
            here = slice(s * span + m * rows, s * span + (m + 1) * rows)
            normed, _ = row_norm(middle_of(xg_ref, own_ref, got_ref, table_ref, u, m, s))
            normed_ref[m * rows : (m + 1) * rows, :] = normed
            second_ref[here, :] = (normed * factor + mod_row(table_ref, s, 3)).astype(bf16)
            low_ref[here, :] = (gate * xg_ref[u ^ m, 1, s].astype(f32)).astype(bf16)
        raised = DOT(second_ref[at, :], up_ref[...])
        d_hidden = dot_nt(low_ref[at, :], down_ref[...])
        square = raised * raised
        t = jnp.tanh(scale * raised * (1.0 + 0.044715 * square))
        hidden_ref[at, :] = (0.5 * raised * (1.0 + t)).astype(bf16)
        slope = 0.5 * (1.0 + t) + 0.5 * raised * (1.0 - t * t) * (scale * (1.0 + 3.0 * 0.044715 * square))
        raised_ref[at, :] = (d_hidden * slope).astype(bf16)
        d_second = dot_nt(raised_ref[at, :], up_ref[...])
        store_parts(dsend_ref, dkeep_ref, d_second, s, rows)
        lowered = DOT(hidden_ref[at, :], down_ref[...])
        store_parts(lsend_ref, lkeep_ref, lowered, s, rows)
        sums_ref[s, 0:1, :] = jnp.sum(d_second, axis=0, keepdims=True)
        sums_ref[s, 1:2, :] = jnp.sum(d_second * normed_ref[...], axis=0, keepdims=True)
        gated = jnp.zeros((1, width), f32)
        for m in range(n_u):
            grad = xg_ref[u ^ m, 1, s].astype(f32)
            gated = gated + jnp.sum(grad * lowered[m * rows : (m + 1) * rows], axis=0, keepdims=True)
        sums_ref[s, 2:3, :] = gated
    n_z, side = ukeep_ref.shape[0], b % 2
    wide_ref[...] = dot_tn(hidden_ref[...], low_ref[...])
    for y, out_ref in enumerate((wkeep_ref, wsend_ref)):
        for z in range(n_z):
            start = pl.multiple_of((2 * z + (side ^ y)) * low, 32)
            out_ref[z] = wide_ref[pl.ds(start, low), :].astype(bf16)
    wide_ref[...] = dot_tn(second_ref[...], raised_ref[...])
    for y, out_ref in enumerate((ukeep_ref, usend_ref)):
        for z in range(n_z):
            for i in range(n_u):
                start = pl.multiple_of(((u ^ i) * 2 * n_z + 2 * z + (side ^ y)) * block, 8)
                out_ref[z, i] = wide_ref[pl.ds(start, block), :].astype(bf16)


def middle_back_kernel(
    at_ref, xg_ref, own_ref, got_ref, down_ref, dgot_ref, table_ref, w_ref, att_ref,
    chunk_ref, dmid_ref, gate_ref, okeep_ref, osend_ref, branch_ref, outs_ref,
):
    u = at_ref[0]
    n_u, _, seqs, rows, width = xg_ref.shape
    span = n_u * rows
    heads = w_ref.shape[0] // HEAD_DIM
    gain = mod_row(table_ref, 1, 6)
    zero = jnp.zeros(chunk_ref.shape[1:], bf16)
    chunk_ref[0] = zero
    chunk_ref[chunk_ref.shape[0] - 1] = zero
    for s in range(seqs):
        at = slice(s * span, (s + 1) * span)
        factor = gain * (1.0 + mod_row(table_ref, s, 4))
        gate = mod_row(table_ref, s, 2)
        for m in range(n_u):
            normed, inv_std = row_norm(middle_of(xg_ref, own_ref, got_ref, table_ref, u, m, s))
            grads = block_of(down_ref, dgot_ref, m, s) * factor
            d_middle = xg_ref[u ^ m, 1, s].astype(f32) + row_back(grads, normed, inv_std)
            branch_ref[s * span + m * rows : s * span + (m + 1) * rows, :] = (gate * d_middle).astype(bf16)
            if m == 0:
                dmid_ref[s] = d_middle
                gate_ref[s] = jnp.sum(d_middle * own_ref[0, s].astype(f32), axis=0, keepdims=True)
        d_att = dot_nt(branch_ref[at, :], w_ref[...]).astype(bf16)
        for h in range(heads):
            d = d_att[:, HEAD_DIM * h : HEAD_DIM * (h + 1)]
            chunk_ref[1 + s * heads + h] = jnp.concatenate([d[: span // 2], d[span // 2 :]], axis=1)
    n_z, block, _ = okeep_ref.shape
    outs_ref[...] = dot_tn(att_ref[...], branch_ref[...])
    for y, out_ref in enumerate((okeep_ref, osend_ref)):
        for z in range(n_z):
            start = pl.multiple_of((2 * z + ((at_ref[1] % 2) ^ y)) * block, 8)
            out_ref[z] = outs_ref[pl.ds(start, block), :].astype(bf16)


def first_back_kernel(
    at_ref, t_ref, xg_ref, table_ref, cos_ref, sin_ref, w_ref, first_ref, gate_ref, two_ref,
    send_ref, keep_ref, blocks_ref, proj_ref, normed_ref, sums_ref, ext_ref, both_ref,
):
    u = at_ref[0]
    n_u, _, seqs, rows, width = xg_ref.shape
    span = n_u * rows
    cols = w_ref.shape[1]
    heads = cols // 192
    gain_grads = [jnp.zeros((1, width), f32)] * 2
    total, block, _ = blocks_ref.shape
    for s in range(seqs):
        at = slice(s * span, (s + 1) * span)
        for h in range(heads):
            pair = t_ref[1 + s * heads + h]
            both = turn(pair[:span].astype(f32), cos_ref, sin_ref, -1.0)
            proj_ref[at, 128 * h : 128 * (h + 1)] = both.astype(bf16)
            v = pair[span:]
            proj_ref[at, 128 * heads + 64 * h : 128 * heads + 64 * (h + 1)] = jnp.concatenate(
                [v[:, :HEAD_DIM], v[:, HEAD_DIM:]], axis=0
            )
        d_first = dot_nt(proj_ref[at, :], w_ref[...])
        store_parts(send_ref, keep_ref, d_first, s, rows)
        for m in range(n_u):
            normed, _ = row_norm(xg_ref[u ^ m, 0, s].astype(f32))
            normed_ref[m * rows : (m + 1) * rows, :] = normed
        dots = [jnp.sum(d_first * normed_ref[...], axis=0, keepdims=True), two_ref[s, 1:2, :]]
        for i in range(2):
            gain_grads[i] = gain_grads[i] + dots[i] * (1.0 + mod_row(table_ref, s, 1 + 3 * i))
        rows_out = [
            jnp.sum(d_first, axis=0, keepdims=True),
            dots[0] * mod_row(table_ref, 0, 6),
            gate_ref[s],
            two_ref[s, 0:1, :],
            dots[1] * mod_row(table_ref, 1, 6),
            two_ref[s, 2:3, :],
        ]
        for i, row in enumerate(rows_out):
            sums_ref[s : s + 1, i * width : (i + 1) * width] = row
    for i in range(2):
        sums_ref[i : i + 1, 6 * width :] = gain_grads[i]
    ext_ref[...] = jnp.zeros_like(ext_ref)
    high = sums_ref[...].astype(bf16).astype(f32)
    both_ref[...] = jnp.concatenate([high, sums_ref[...] - high], axis=0)
    lines = 2 * seqs
    for d in range(total):
        for i in range(3):
            at = 3 * EXTRA * d + EXTRA * i
            ext_ref[d * block + lines * i : d * block + lines * (i + 1), :EXTRA] = both_ref[:, at : at + EXTRA]
        at = 6 * width + block * d
        ext_ref[d * block + 3 * lines : d * block + 4 * lines, :block] = both_ref[:, at : at + block]
    grads = dot_tn(first_ref[...], proj_ref[...])
    for i in range(total):
        at = slice(i * block, (i + 1) * block)
        blocks_ref[i, :, :cols] = grads[at].astype(bf16)
        blocks_ref[i, :, cols:] = ext_ref[at].astype(bf16)


def row_grad_kernel(at_ref, raw_ref, p0, p1, p2, p3, ada_ref, cond_ref, qkv_ref, up_ref, part_ref, adag_ref, gain_ref, mod_ref):
    u = at_ref[0]
    total, block, cols = raw_ref.shape
    cols = cols - HEAD_DIM
    n_u = 4
    n_b = total // n_u
    heads = cols // 192
    width = qkv_ref.shape[1] // 3
    seqs = mod_ref.shape[0]
    extra = jnp.zeros((block, HEAD_DIM), f32)
    for i in range(n_u):
        part = raw_ref[i * n_b].astype(f32)
        for j in range(1, n_b):
            part = part + raw_ref[i * n_b + j].astype(f32)
        extra = extra + part[:, cols:]
        for h in range(heads):
            to = (i * heads + h) * HEAD_DIM
            qkv_ref[:, to : to + HEAD_DIM] = part[:, 128 * h : 128 * h + HEAD_DIM]
            qkv_ref[:, width + to : width + to + HEAD_DIM] = part[:, 128 * h + HEAD_DIM : 128 * (h + 1)]
        at = i * heads * HEAD_DIM
        qkv_ref[:, 2 * width + at : 2 * width + at + heads * HEAD_DIM] = part[:, 128 * heads : cols]
    mod_ref[...] = jnp.concatenate([join_rows(extra, i, seqs)[:, :EXTRA] for i in range(3)], axis=1)
    gain_ref[...] = join_rows(extra, 3, seqs)[:, :block]
    mods = mod_ref[...].astype(bf16)
    grads = DOT(mods, ada_ref[...])
    for i in range(total):
        part_ref[i] = grads
    adag_ref[...] = dot_tn(mods, cond_ref[...])
    cols = up_ref.shape[1] // n_u
    for i, piece_ref in enumerate((p0, p1, p2, p3)):
        up_ref[:, pl.ds(pl.multiple_of((u ^ i) * cols, 128), cols)] = piece_ref[...]


def input_grad_kernel(x_ref, near_ref, got_ref, dmid_ref, table_ref, out_ref):
    seqs = x_ref.shape[0]
    for s in range(seqs):
        factor = mod_row(table_ref, 0, 6) * (1.0 + mod_row(table_ref, s, 1))
        normed, inv_std = row_norm(x_ref[s].astype(f32))
        grads = (near_ref[s].astype(f32) + got_ref[s].astype(f32)) * factor
        out_ref[s] = dmid_ref[s] + row_back(grads, normed, inv_std)


def call(kernel, name, outs, scratch, flops, *args, limit=16, staged=()):
    count = len(args)
    specs = [
        pl.BlockSpec(
            memory_space=pltpu.SMEM if a.dtype == jnp.int32 else pltpu.HBM if i in staged else pltpu.VMEM
        )
        for i, a in enumerate(args)
    ]
    size = sum(math.prod(a.shape) * a.dtype.itemsize for a in args)
    size += sum(math.prod(shape) * jnp.dtype(dtype).itemsize for shape, dtype in outs)
    shapes = [pltpu.VMEM(*s) for s in scratch]
    body = kernel
    if staged:
        shapes = [pltpu.VMEM(args[i].shape, args[i].dtype) for i in staged] + [
            pltpu.SemaphoreType.DMA((len(staged),))
        ] + shapes

        def body(*refs):
            ins, rest = list(refs[:count]), refs[count:]
            out_refs, held = rest[: len(outs)], rest[len(outs) :]
            sems = held[len(staged)]
            copies = []
            for j, i in enumerate(staged):
                copies.append(pltpu.make_async_copy(ins[i], held[j], sems.at[j]))
                ins[i] = held[j]
            for copy in copies:
                copy.start()
            for copy in copies:
                copy.wait()
            kernel(*ins, *out_refs, *held[len(staged) + 1 :])

    return pl.pallas_call(
        body,
        out_shape=tuple(jax.ShapeDtypeStruct(shape, dtype) for shape, dtype in outs),
        in_specs=specs,
        out_specs=tuple(pl.BlockSpec(memory_space=pltpu.VMEM) for _ in outs),
        scratch_shapes=shapes,
        cost_estimate=pl.CostEstimate(flops=int(flops) // 1000, bytes_accessed=int(size) // 1000, transcendentals=0),
        compiler_params=pltpu.CompilerParams(vmem_limit_bytes=limit << 20),
        name=name,
    )(*args)


def fits_tp(mesh):
    ulysses, blk = mesh.shape["ulysses"], mesh.shape["blk"]
    return ulysses == 4 and blk == 8 and HEADS % ulysses == 0


def swap_u(values, mask):
    return lax.ppermute(values, "ulysses", [(i, i ^ mask) for i in range(4)])


def swap_b(values, mask):
    return lax.ppermute(values, "blk", [(i, i ^ mask) for i in range(8)])


def scatter_z(blocks):
    groups = [[2 * z + y for z in range(4)] for y in range(2)]
    return lax.psum_scatter(blocks, "blk", scatter_dimension=0, axis_index_groups=groups, tiled=True)[0]


def exchange(blocks, axis):
    return lax.all_to_all(blocks, axis, split_axis=0, concat_axis=0, tiled=True)


def half_sum(send, keep):
    return (keep.astype(f32) + swap_u(send, 1).astype(f32)).astype(bf16)


def pair_sum(left, right):
    return (left.astype(f32) + right.astype(f32)).astype(bf16)


def along_z(values):
    return [values] + [swap_b(values, 2 * m) for m in (1, 2, 3)]


def along_y(parts):
    out = []
    for part in parts:
        out += [part, swap_b(part, 1)]
    return out


def sum_z(half):
    total = half[0]
    for m in (1, 2, 3):
        total = total + swap_b(half[m].astype(bf16), 2 * m).astype(f32)
    return total


def tp_shards(inputs, conditioning, w_ada, w_qkv, w_out, w_up, w_down, gain_one, gain_two, cotangent):
    n_u, n_b = 4, 8
    n_all = n_u * n_b
    everywhere = ("ulysses", "blk")
    seqs, rows, width = inputs.shape
    u = lax.axis_index("ulysses")
    b = lax.axis_index("blk")
    at = jnp.stack([u, b]).astype(jnp.int32)
    heads = HEADS // n_u
    head_width = heads * HEAD_DIM
    cols = 3 * head_width
    w_rows, down_rows = w_qkv.shape[0], w_down.shape[0]
    ff_local = w_up.shape[1] // n_u
    span = n_u * rows
    tokens = seqs * span

    both, pieces = call(
        pack_kernel, "pack",
        [((2,) + inputs.shape, bf16), ((n_u, w_rows, cols + HEAD_DIM + ff_local), bf16)],
        [((w_rows, HEAD_DIM), f32)], 0,
        inputs, cotangent, w_qkv, w_ada.T, conditioning, gain_one[None], gain_two[None], w_up,
        limit=60,
    )
    blocks = u ^ jnp.arange(n_u, dtype=jnp.int32)
    positions = ((blocks * n_b + b) * rows)[:, None] + jnp.arange(rows, dtype=jnp.int32)[None, :]
    cos_table, sin_table = rotary_tables(positions.reshape(-1).astype(f32))
    cos_table, sin_table = cos_table[:, 0], sin_table[:, 0]
    cos_table = jnp.concatenate([cos_table] * 4, axis=1)
    sin_table = jnp.concatenate([-sin_table, sin_table] * 2, axis=1)

    pieces, cos_table, sin_table, at = lax.optimization_barrier(
        (exchange(pieces, "ulysses"), cos_table, sin_table, at)
    )
    pieces = pieces.reshape(n_u * w_rows, cols + HEAD_DIM + ff_local)
    xg = lax.all_gather(both, "ulysses", axis=0, tiled=False)
    up_near = pieces[:, cols + HEAD_DIM :]
    down_z = along_z(jnp.concatenate([w_down, w_out], axis=0))
    pieces, down_z[1], down_z[2] = lax.optimization_barrier((pieces, down_z[1], down_z[2]))
    near = pieces[:, : cols + HEAD_DIM]
    rows_zy = along_y(along_z(near))

    chunks, first_in, table, w_qkv_u = call(
        first_kernel, "first",
        [((n_b, 3 * span // 2, 128), bf16), ((tokens, width), bf16), ((seqs, 7 * width), f32),
         ((width, cols), bf16)],
        [((width, cols + HEAD_DIM), f32)],
        2 * tokens * width * cols,
        at, xg, cos_table, sin_table, *rows_zy,
        limit=48,
    )
    chunks, down_z = lax.optimization_barrier((chunks, down_z))
    owned = exchange(chunks, "blk")
    down_zy = along_y(down_z)
    up_near, down_zy[1], down_zy[3] = lax.optimization_barrier((up_near, down_zy[1], down_zy[3]))
    up_z = along_z(up_near)
    attn_low, attn_full, log_total = attn_fwd(owned)
    part_shape = (2, seqs, rows, width)
    attn_low, up_z, down_zy = lax.optimization_barrier((attn_low, up_z, down_zy))
    attn_tokens = exchange(attn_low, "blk")
    up_zy = along_y(up_z[:1])
    attn_tokens, up_zy = lax.optimization_barrier((attn_tokens, up_zy))
    attended, send, keep, w_out_u = call(
        out_kernel, "out",
        [((tokens, head_width), bf16), (part_shape, bf16), (part_shape, bf16), ((head_width, width), bf16)],
        [((head_width, width), f32)],
        2 * tokens * width * head_width,
        at, attn_tokens, *down_zy,
    )

    half = half_sum(send, keep)
    across = swap_u(half, 2)
    up_zy = up_zy + along_y(up_z[1:])
    across, up_zy = lax.optimization_barrier((across, up_zy))
    own = pair_sum(half, across[::-1])
    got = swap_u(own, 1)
    lsend, lkeep, dsend, dkeep, sums_two, up_keep, up_send, down_keep, down_send = call(
        ff_kernel, "ff",
        [(part_shape, bf16), (part_shape, bf16), (part_shape, bf16), (part_shape, bf16), ((seqs, 3, width), f32)]
        + [((n_b // 2, n_u, w_rows, width), bf16)] * 2 + [((n_b // 2, down_rows, width), bf16)] * 2,
        [((tokens, width), bf16), ((tokens, ff_local), bf16), ((tokens, width), bf16), ((tokens, ff_local), bf16),
         ((span, width), f32), ((width, ff_local), f32), ((width, ff_local), bf16), ((ff_local, width), bf16)],
        12 * tokens * width * ff_local,
        at, xg, own, got, table, *up_zy, *down_zy,
        limit=60,
    )
    down_other, up_other = swap_b(down_send, 1), swap_b(up_send, 1)
    half = half_sum(dsend, dkeep)
    across = swap_u(half, 2)
    across, down_other = lax.optimization_barrier((across, down_other))
    down_grad = scatter_z(pair_sum(down_keep, down_other))
    d_own = pair_sum(half, across[::-1])
    d_got = swap_u(d_own, 1)
    d_chunks, d_middle, sum_gate, out_keep, out_send = call(
        middle_back_kernel, "middle_back",
        [((n_b, span // 2, 128), bf16), ((seqs, rows, width), f32), ((seqs, 1, width), f32)]
        + [((n_b // 2, w_rows, width), bf16)] * 2,
        [((tokens, width), bf16), ((head_width, width), f32)],
        4 * tokens * width * head_width,
        at, xg, own, got, d_own, d_got, table, w_out_u, attended,
        limit=60,
    )
    d_attn = exchange(d_chunks, "blk")
    out_other = swap_b(out_send, 1)
    up_low = pair_sum(up_keep, up_other)
    d_attn, out_other, down_grad = lax.optimization_barrier((d_attn, out_other, down_grad))
    up_low = jnp.concatenate([up_low, pair_sum(out_keep, out_other)[:, None]], axis=1)
    up_sum = scatter_z(up_low)
    d_owned = attn_bwd(owned, d_attn, attn_full, log_total)
    d_owned, lsend, lkeep = lax.optimization_barrier((d_owned, lsend, lkeep))
    lhalf = half_sum(lsend, lkeep)
    lowered = lhalf[0].astype(f32) + swap_u(lhalf[1], 2).astype(f32)
    gates = table.reshape(2, 7, 1, width)
    output = inputs.astype(f32) + gates[:, 2] * own[0].astype(f32) + gates[:, 5] * lowered
    up_sum = up_sum.astype(f32)
    up_parts = [up_sum[0]] + [swap_u(up_sum[m], m) for m in (1, 2, 3)]
    d_tokens = exchange(d_owned, "blk")
    d_tokens, up_parts, down_grad, output = lax.optimization_barrier((d_tokens, up_parts, down_grad, output))

    send, keep, qkv_blocks = call(
        first_back_kernel, "first_back",
        [(part_shape, bf16), (part_shape, bf16), ((n_all, w_rows, cols + HEAD_DIM), bf16)],
        [((tokens, cols), bf16), ((span, width), f32), ((seqs, 7 * width), f32), ((width, HEAD_DIM), f32),
         ((2 * seqs, 7 * width), f32)],
        4 * tokens * width * cols,
        at, d_tokens, xg, table, cos_table, sin_table, w_qkv_u, first_in, sum_gate, sums_two,
        limit=60,
    )
    half = half_sum(send, keep)
    far = swap_u(half[1], 2)
    inputs_grad, = call(
        input_grad_kernel, "input_grad",
        [((seqs, rows, width), f32)], [], 0,
        inputs, half[0], far, d_middle, table,
    )
    qkv_grad, up_grad, cond_part, ada_grad, gain_grads, _ = call(
        row_grad_kernel, "row_grad",
        [(w_qkv.shape, f32), (w_up.shape, f32), ((n_all,) + conditioning.shape, f32), (w_ada.shape[::-1], f32),
         ((2, w_rows), f32), ((seqs, w_ada.shape[1]), f32)],
        [], 0,
        at, exchange(qkv_blocks, everywhere), *up_parts, w_ada.T, conditioning,
        limit=6,
    )
    conditioning_grad = jnp.sum(exchange(cond_part, everywhere), axis=0)
    return (
        output,
        inputs_grad,
        conditioning_grad,
        ada_grad.T,
        qkv_grad,
        up_sum[n_u],
        up_grad,
        down_grad.astype(f32),
        gain_grads[0],
        gain_grads[1],
    )


def solution(mesh):
    body = tp_shards if fits_tp(mesh) else shards
    in_specs = (
        P(None, ("ulysses", "blk"), None),
        P(),
        P(None, ("ulysses", "blk")),
        P(("ulysses", "blk"), None),
        P(("ulysses", "blk"), None),
        P(("ulysses", "blk"), None),
        P(("ulysses", "blk"), None),
        P(("ulysses", "blk")),
        P(("ulysses", "blk")),
        P(None, ("ulysses", "blk"), None),
    )
    out_specs = (
        P(None, ("ulysses", "blk"), None),
        P(None, ("ulysses", "blk"), None),
        P(),
        P(None, ("ulysses", "blk")),
        P(("ulysses", "blk"), None),
        P(("ulysses", "blk"), None),
        P(("ulysses", "blk"), None),
        P(("ulysses", "blk"), None),
        P(("ulysses", "blk")),
        P(("ulysses", "blk")),
    )
    return jax.shard_map(body, mesh=mesh, in_specs=in_specs, out_specs=out_specs, check_vma=False)
```
